32 devices in a mesh: dp: 8 (over y, x, core), seq: 4 (over z).
Axes of the slice: x: 2, y: 2, z: 4, core: 2. Of those that a mesh axis runs over, the one named last changes fastest.
Arguments:
- hidden_in: bfloat16 [8, 1024, 768], P('dp', 'seq'), may hold values from -8 to 8, as said below
- encoder_in: bfloat16 [8, 1024, 768], P('dp', 'seq'), may hold values from -6 to 6
- prefix_len: int32 [8], P('dp'), may hold values from 102 to 512, as said below
- exit_flags: int32 [8, 1024], P('dp', 'seq'), may hold values 0 or 1
- target_ids: int32 [8, 1024], P('dp', 'seq'), may hold values from 0 to 32127
- out_cotangent: float32 [8, 1024, 768], P('dp', 'seq'), may hold values from -6 to 6
- self_gain: bfloat16 [768], P('dp'), may hold values from 0.5 to 1.5
- self_query: bfloat16 [768, 768], P('dp', 'seq'), may hold values from -0.4375 to 0.4375
- self_key: bfloat16 [768, 768], P('dp', 'seq'), may hold values from -0.21875 to 0.21875
- self_value: bfloat16 [768, 768], P('dp', 'seq'), may hold values from -0.21875 to 0.21875
- self_output: bfloat16 [768, 768], P('dp', 'seq'), may hold values from -0.875 to 0.875
- cross_gain: bfloat16 [768], P('dp'), may hold values from 0.5 to 1.5
- cross_query: bfloat16 [768, 768], P('dp', 'seq'), may hold values from -0.4375 to 0.4375
- cross_key: bfloat16 [768, 768], P('dp', 'seq'), may hold values from -0.21875 to 0.21875
- cross_value: bfloat16 [768, 768], P('dp', 'seq'), may hold values from -0.21875 to 0.21875
- cross_output: bfloat16 [768, 768], P('dp', 'seq'), may hold values from -0.875 to 0.875
- feed_gain: bfloat16 [768], P('dp'), may hold values from 0.5 to 1.5
- feed_gate: bfloat16 [768, 2048], P('dp', 'seq'), may hold values from -0.21875 to 0.21875
- feed_up: bfloat16 [768, 2048], P('dp', 'seq'), may hold values from -0.21875 to 0.21875
- feed_down: bfloat16 [2048, 768], P('dp', 'seq'), may hold values from -0.25 to 0.25
- exit_gain: bfloat16 [768], P('dp'), may hold values from 0.5 to 1.5
- embedding: bfloat16 [32128, 768], P('dp', 'seq'), may hold values from -0.21875 to 0.21875
Outputs:
- block_output: bfloat16 [8, 1024, 768], P('dp', 'seq')
- token_losses: float32 [8, 1024], P('dp', 'seq')
- hidden_grad: float32 [8, 1024, 768], P('dp', 'seq')
- encoder_grad: float32 [8, 1024, 768], P('dp', 'seq')
- self_gain_grad: float32 [768], P('dp')
- self_query_grad: float32 [768, 768], P('dp', 'seq')
- self_key_grad: float32 [768, 768], P('dp', 'seq')
- self_value_grad: float32 [768, 768], P('dp', 'seq')
- self_output_grad: float32 [768, 768], P('dp', 'seq')
- cross_gain_grad: float32 [768], P('dp')
- cross_query_grad: float32 [768, 768], P('dp', 'seq')
- cross_key_grad: float32 [768, 768], P('dp', 'seq')
- cross_value_grad: float32 [768, 768], P('dp', 'seq')
- cross_output_grad: float32 [768, 768], P('dp', 'seq')
- feed_gain_grad: float32 [768], P('dp')
- feed_gate_grad: float32 [768, 2048], P('dp', 'seq')
- feed_up_grad: float32 [768, 2048], P('dp', 'seq')
- feed_down_grad: float32 [2048, 768], P('dp', 'seq')
- exit_gain_grad: float32 [768], P('dp')
- embedding_grad: float32 [32128, 768], P('dp', 'seq')
The draws below stay inside these ranges and needn't reach their ends.
Inputs may be any that keep to these rules, and one draw needn't show every extreme that they name: `prefix_len`: each sequence's prefix length; both the shortest and the longest allowed value occur in every draw. `hidden_in`: the layer's input.
All inputs are finite; a program needn't handle non-finite values. No bound on the sum of `exit_flags` on one device may be relied on, other than what follows from the above.
Results may differ from the reference program's by a relative error of at most 0.033.
Values may be sent and summed in bfloat16 or wider, within the bound.
No kernel may reach another device: no remote copies, remote signals or barrier semaphores. Data moves between devices by JAX's collectives and lax.ppermute only.
A program may use at most 320 MiB of HBM per device.

```python
import jax
import jax.numpy as jnp
from jax import lax

D = 768
FF = 2048
HEADS = 12
HD = 64
V = 32128
LEN = 1024
ENC = 1024
SEQS = 8


def draw_prefix_len(key, part):
    shortest = LEN // 10
    longest = LEN // 2
    drawn = jax.random.randint(jax.random.fold_in(key, 11), (SEQS,), shortest, longest + 1)
    drawn = drawn.at[0].set(longest).at[1].set(shortest)
    return jax.random.permutation(jax.random.fold_in(key, 12), drawn).astype(jnp.int32)


def draw_hidden_in(key, part):
    offset = jax.random.normal(jax.random.fold_in(key, 21), (D,), jnp.float32)
    noise = jax.random.normal(jax.random.fold_in(key, 22), (SEQS, LEN, D), jnp.float32)
    values = jnp.clip(noise + offset[None, None, :], -8.0, 8.0)
    return values.astype(jnp.bfloat16)


def plant(entries, stream_key, low, top_value):
    longest = entries.shape.index(max(entries.shape))
    spots = []
    for shift in (0, 1):
        where = [jax.random.randint(jax.random.fold_in(stream_key, axis), (), 0, length) for axis, length in enumerate(entries.shape)]
        where[longest] = (where[longest] + shift) % entries.shape[longest]
        spots.append(tuple(where))
    return entries.at[spots[0]].set(low).at[spots[1]].set(top_value)


def levels(own_key, dims, pieces, least, top_value):
    gain = 1.0
    for dim, shards_of in pieces:
        heights = jax.random.uniform(jax.random.fold_in(jax.random.fold_in(own_key, 6), dim), (shards_of,), jnp.float32, least / len(pieces), top_value / len(pieces))
        gain = gain * jnp.repeat(jnp.exp(heights), dims[dim] // shards_of).reshape((-1,) + (1,) * (len(dims) - 1 - dim))
    return gain


def bell_draw(stream_key, shape, scale, most, pieces=(), dtype=jnp.bfloat16):
    result = scale * jax.random.normal(stream_key, shape, jnp.float32)
    if pieces:
        result = result * levels(stream_key, shape, pieces, -0.22, 0.18)
    return jnp.clip(result, -most, most).astype(dtype)


def setup_inputs(seed: int = 0) -> dict:
    key_list = jax.random.split(jax.random.key(seed), 23)
    hidden_in = draw_hidden_in(jax.random.fold_in(key_list[22], 71), 0)
    encoder_in = bell_draw(key_list[1], (SEQS, ENC, D), 1.0, 6.0, ((0, 8), (1, 4)))
    prefix_len = draw_prefix_len(jax.random.fold_in(key_list[22], 71), 0)
    exit_flags = plant((jax.random.randint(key_list[3], (SEQS, LEN), 0, 2) < 1).astype(jnp.int32), jax.random.fold_in(key_list[3], 1), 0, 1)
    target_ids = plant(jax.random.randint(key_list[4], (SEQS, LEN), 0, V), jax.random.fold_in(key_list[4], 1), 0, V - 1).astype(jnp.int32)
    out_cotangent = bell_draw(key_list[5], (SEQS, LEN, D), 1.0, 6.0, ((0, 8), (1, 4)), jnp.float32)
    self_gain = jnp.clip(1.0 + 0.1 * jax.random.normal(key_list[6], (D,), jnp.float32), 0.5, 1.5).astype(jnp.bfloat16)
    self_query = bell_draw(key_list[7], (D, HEADS * HD), (D // 4) ** -0.5, 0.4375, ((0, 8), (1, 4)))
    self_key = bell_draw(key_list[8], (D, HEADS * HD), D ** -0.5, 0.21875, ((0, 8), (1, 4)))
    self_value = bell_draw(key_list[9], (D, HEADS * HD), D ** -0.5, 0.21875, ((0, 8), (1, 4)))
    self_output = bell_draw(key_list[10], (HEADS * HD, D), (D // 16) ** -0.5, 0.875, ((0, 8), (1, 4)))
    cross_gain = jnp.clip(1.0 + 0.1 * jax.random.normal(key_list[11], (D,), jnp.float32), 0.5, 1.5).astype(jnp.bfloat16)
    cross_query = bell_draw(key_list[12], (D, HEADS * HD), (D // 4) ** -0.5, 0.4375, ((0, 8), (1, 4)))
    cross_key = bell_draw(key_list[13], (D, HEADS * HD), D ** -0.5, 0.21875, ((0, 8), (1, 4)))
    cross_value = bell_draw(key_list[14], (D, HEADS * HD), D ** -0.5, 0.21875, ((0, 8), (1, 4)))
    cross_output = bell_draw(key_list[15], (HEADS * HD, D), (D // 16) ** -0.5, 0.875, ((0, 8), (1, 4)))
    feed_gain = jnp.clip(1.0 + 0.1 * jax.random.normal(key_list[16], (D,), jnp.float32), 0.5, 1.5).astype(jnp.bfloat16)
    feed_gate = bell_draw(key_list[17], (D, FF), D ** -0.5, 0.21875, ((0, 8), (1, 4)))
    feed_up = bell_draw(key_list[18], (D, FF), D ** -0.5, 0.21875, ((0, 8), (1, 4)))
    feed_down = bell_draw(key_list[19], (FF, D), (FF // 4) ** -0.5, 0.25, ((0, 8), (1, 4)))
    exit_gain = jnp.clip(1.0 + 0.1 * jax.random.normal(key_list[20], (D,), jnp.float32), 0.5, 1.5).astype(jnp.bfloat16)
    embedding = bell_draw(key_list[21], (V, D), D ** -0.5, 0.21875, ((0, 8), (1, 4)))
    return {"hidden_in": hidden_in, "encoder_in": encoder_in, "prefix_len": prefix_len, "exit_flags": exit_flags, "target_ids": target_ids, "out_cotangent": out_cotangent, "self_gain": self_gain, "self_query": self_query, "self_key": self_key, "self_value": self_value, "self_output": self_output, "cross_gain": cross_gain, "cross_query": cross_query, "cross_key": cross_key, "cross_value": cross_value, "cross_output": cross_output, "feed_gain": feed_gain, "feed_gate": feed_gate, "feed_up": feed_up, "feed_down": feed_down, "exit_gain": exit_gain, "embedding": embedding}


@jax.custom_vjp
def low(v):
    return lax.optimization_barrier(v.astype(jnp.bfloat16)).astype(jnp.float32)

@jax.custom_vjp
def low_back(v):
    return v

def low_keep(v):
    return (low(v), None)

def low_pass(kept, grad):
    return (grad,)

def back_keep(v):
    return (v, None)

def back_low(kept, grad):
    return (low(grad),)
low.defvjp(low_keep, low_pass)
low_back.defvjp(back_keep, back_low)
exact_mode = lax.Precision.HIGHEST
norm_eps = 1e-06
masked_score = -1000000000.0

def low_both(inputs):
    return low_back(low(inputs))

def matmul(first_op, second_op):
    return jnp.dot(first_op, second_op, precision=exact_mode)

def norm_rows(inputs, scaling):
    return inputs * lax.rsqrt(lax.optimization_barrier(jnp.mean(inputs * inputs, axis=-1, keepdims=True)) + norm_eps) * scaling

def attention(queries, key_rows, values, allowed):
    query_heads = queries.reshape(queries.shape[0], HEADS, HD)
    key_heads = key_rows.reshape(key_rows.shape[0], HEADS, HD)
    value_heads = values.reshape(values.shape[0], HEADS, HD)
    raw_scores = low_back(jnp.einsum('qhe,khe->hqk', query_heads, key_heads, precision=exact_mode))
    scores = raw_scores * HD ** (-0.5)
    if allowed is not None:
        scores = jnp.where(allowed[None], scores, masked_score)
    row_max = lax.optimization_barrier(jnp.max(scores, axis=-1, keepdims=True))
    exponent = jnp.exp(scores - row_max)
    shares = exponent / lax.optimization_barrier(jnp.sum(exponent, axis=-1, keepdims=True))
    mixture = jnp.einsum('hqk,khe->qhe', low(shares), value_heads, precision=exact_mode)
    return mixture.reshape(queries.shape[0], HEADS * HD)

def one_sequence(weights, residual, states, prefix_one, flag_row, target_row, cotangent):
    self_gain, self_query, self_key, self_value, self_output, cross_gain, cross_query, cross_key, cross_value, cross_output, feed_gain, feed_gate, feed_up, feed_down, exit_gain, embedding = weights
    position = jnp.arange(residual.shape[0])
    allowed = (position[None, :] <= position[:, None]) | (position[None, :] < prefix_one)
    normed = low(norm_rows(residual, self_gain))
    mixture = low_both(attention(low_both(matmul(normed, self_query)), low_both(matmul(normed, self_key)), low_both(matmul(normed, self_value)), allowed))
    after_self = residual + low_back(matmul(mixture, self_output))
    normed = low(norm_rows(after_self, cross_gain))
    mixture = low_both(attention(low_both(matmul(normed, cross_query)), low_both(matmul(states, cross_key)), low_both(matmul(states, cross_value)), None))
    after_cross = after_self + low_back(matmul(mixture, cross_output))
    normed = low(norm_rows(after_cross, feed_gain))
    gate_pre = low_back(matmul(normed, feed_gate))
    up_pre = low_back(matmul(normed, feed_up))
    hidden_mid = low(jax.nn.gelu(gate_pre, approximate=True) * up_pre)
    after_feed = after_cross + low_back(matmul(hidden_mid, feed_down))
    final = low(norm_rows(after_feed, exit_gain))
    logits = low_back(jnp.dot(final, embedding.T, precision=exact_mode))
    row_max = lax.optimization_barrier(jnp.max(logits, axis=1, keepdims=True))
    log_total = row_max + jnp.log(lax.optimization_barrier(jnp.sum(jnp.exp(logits - row_max), axis=1, keepdims=True)))
    target_hits = jnp.arange(logits.shape[1])[None, :] == target_row[:, None]
    picked = lax.optimization_barrier(jnp.sum(jnp.where(target_hits, logits, 0.0), axis=1, keepdims=True))
    token_losses = flag_row.astype(jnp.float32)[:, None] * (log_total - picked)
    objective = jnp.sum(token_losses) + jnp.sum(after_feed * cotangent)
    return (objective, (after_feed, token_losses[:, 0]))

def reference(hidden_in, encoder_in, prefix_len, exit_flags, target_ids, out_cotangent, self_gain, self_query, self_key, self_value, self_output, cross_gain, cross_query, cross_key, cross_value, cross_output, feed_gain, feed_gate, feed_up, feed_down, exit_gain, embedding):
    weights = tuple((matrix.astype(jnp.float32) for matrix in (self_gain, self_query, self_key, self_value, self_output, cross_gain, cross_query, cross_key, cross_value, cross_output, feed_gain, feed_gate, feed_up, feed_down, exit_gain, embedding)))
    residual_all = hidden_in.astype(jnp.float32)
    states_all = encoder_in.astype(jnp.float32)

    def objective_of(weights, residual_all, states_all):

        def step_one(running, element):
            residual, states, prefix_one, flag_row, target_row, cotangent = element
            partial_objective, extras = jax.checkpoint(one_sequence)(weights, residual, states, prefix_one, flag_row, target_row, cotangent)
            return (running + partial_objective, extras)
        return lax.scan(step_one, jnp.zeros((), jnp.float32), (residual_all, states_all, prefix_len, exit_flags, target_ids, out_cotangent))
    objective, pullback, outputs = jax.vjp(objective_of, weights, residual_all, states_all, has_aux=True)
    weight_grads, hidden_grad, encoder_grad = pullback(jnp.ones((), jnp.float32))
    after_feeds, token_losses = outputs
    return (after_feeds.astype(jnp.bfloat16), token_losses, hidden_grad, encoder_grad, weight_grads[0], weight_grads[1], weight_grads[2], weight_grads[3], weight_grads[4], weight_grads[5], weight_grads[6], weight_grads[7], weight_grads[8], weight_grads[9], weight_grads[10], weight_grads[11], weight_grads[12], weight_grads[13], weight_grads[14], weight_grads[15])
```

```python
import functools

import jax
import jax.numpy as jnp
from jax import lax
from jax.experimental import pallas as pl
from jax.experimental.pallas import tpu as pltpu
from jax.sharding import PartitionSpec as P

HD = 64
QUERY_ROWS = 256
GAIN_LANES = 128

norm_eps = 1e-06
masked_score = -1000000000.0
both = ("seq", "dp")


def contract(first_op, second_op, first_dim, second_dim):
    return lax.dot_general(
        first_op,
        second_op,
        (((first_dim,), (second_dim,)), ((), ())),
        preferred_element_type=jnp.float32,
    )


def mix(spec, first_op, second_op):
    return jnp.einsum(spec, first_op, second_op, preferred_element_type=jnp.float32)


def norm_rows(inputs, scaling):
    return (
        inputs * lax.rsqrt(jnp.mean(inputs * inputs, axis=-1, keepdims=True) + norm_eps) * scaling
    )


def norm_back(inputs, scaling, upstream):
    unused, pullback = jax.vjp(norm_rows, inputs, scaling)
    return pullback(upstream)


def gated_unit(gate_in, upward):
    return jax.nn.gelu(gate_in, approximate=True) * upward


def swap(pieces):
    return lax.all_to_all(pieces, "seq", 0, 0, tiled=True)


def head_lanes(width, head):
    lanes = lax.broadcasted_iota(jnp.int32, (1, width), 1)
    return (lanes >= head * HD) & (lanes < (head + 1) * HD)


def attend_kernel(prefix_ref, *refs, places, width, causal):
    out_ref = refs[-1]
    step = pl.program_id(0)
    (q_at, q_lane), (k_at, k_lane), (v_at, v_lane) = places
    rows = out_ref.shape[0]
    queries = refs[q_at][pl.ds(pl.multiple_of(step * rows, rows), rows), q_lane : q_lane + width]
    key_rows = refs[k_at][:, k_lane : k_lane + width]
    values = refs[v_at][:, v_lane : v_lane + width]
    count = key_rows.shape[0]
    queries = queries * jnp.asarray(HD**-0.5, queries.dtype)
    if causal:
        query_pos = step * rows + lax.broadcasted_iota(jnp.int32, (rows, count), 0)
        key_pos = lax.broadcasted_iota(jnp.int32, (rows, count), 1)
        allowed = (key_pos <= query_pos) | (key_pos < prefix_ref[0])
    total = jnp.zeros((rows, width), jnp.float32)
    for head in range(width // HD):
        mine = head_lanes(width, head)
        scores = contract(jnp.where(mine, queries, jnp.zeros_like(queries)), key_rows, 1, 1)
        if causal:
            scores = jnp.where(allowed, scores, masked_score)
        exponent = jnp.exp(scores - jnp.max(scores, axis=1, keepdims=True))
        shares = exponent * (1.0 / jnp.sum(exponent, axis=1, keepdims=True))
        total = jnp.where(mine, contract(shares.astype(values.dtype), values, 1, 0), total)
    out_ref[...] = total.astype(out_ref.dtype)


def attend_back_kernel(prefix_ref, *refs, places, spots, width, causal):
    count_in = 1 + max(at for at, lane in places)
    upstream_ref = refs[count_in]
    outs = refs[count_in + 1 : -2]
    key_sum, value_sum = refs[-2:]
    step = pl.program_id(0)
    (q_at, q_lane), (k_at, k_lane), (v_at, v_lane) = places
    (dq_at, dq_lane), (dk_at, dk_lane), (dv_at, dv_lane) = spots
    rows = upstream_ref.shape[0]
    block = pl.ds(pl.multiple_of(step * rows, rows), rows)
    queries = refs[q_at][block, q_lane : q_lane + width]
    key_rows = refs[k_at][:, k_lane : k_lane + width]
    values = refs[v_at][:, v_lane : v_lane + width]
    upstream = upstream_ref[...]
    count = key_rows.shape[0]
    queries = queries * jnp.asarray(HD**-0.5, queries.dtype)
    if causal:
        key_pos = lax.broadcasted_iota(jnp.int32, (count, rows), 0)
        query_pos = step * rows + lax.broadcasted_iota(jnp.int32, (count, rows), 1)
        allowed = (key_pos <= query_pos) | (key_pos < prefix_ref[0])
    query_grads = jnp.zeros((rows, width), jnp.float32)
    key_grads = jnp.zeros((count, width), jnp.float32)
    value_grads = jnp.zeros((count, width), jnp.float32)
    for head in range(width // HD):
        mine = head_lanes(width, head)
        scores = contract(key_rows, jnp.where(mine, queries, jnp.zeros_like(queries)), 1, 1)
        if causal:
            scores = jnp.where(allowed, scores, masked_score)
        exponent = jnp.exp(scores - jnp.max(scores, axis=0, keepdims=True))
        shares = exponent * (1.0 / jnp.sum(exponent, axis=0, keepdims=True))
        share_grads = contract(values, jnp.where(mine, upstream, jnp.zeros_like(upstream)), 1, 1)
        centre = jnp.sum(shares * share_grads, axis=0, keepdims=True)
        score_grads = (shares * (share_grads - centre)).astype(queries.dtype)
        query_grads = jnp.where(mine, contract(score_grads, key_rows, 0, 0), query_grads)
        key_grads = jnp.where(mine, contract(score_grads, queries, 1, 0), key_grads)
        value_grads = jnp.where(
            mine, contract(shares.astype(upstream.dtype), upstream, 1, 0), value_grads
        )
    outs[dq_at][block, dq_lane : dq_lane + width] = (query_grads * HD**-0.5).astype(
        outs[dq_at].dtype
    )

    @pl.when(step == 0)
    def _():
        key_sum[...] = key_grads
        value_sum[...] = value_grads

    @pl.when(step > 0)
    def _():
        key_sum[...] += key_grads
        value_sum[...] += value_grads

    @pl.when(step == pl.num_programs(0) - 1)
    def _():
        outs[dk_at][:, dk_lane : dk_lane + width] = key_sum[...].astype(outs[dk_at].dtype)
        outs[dv_at][:, dv_lane : dv_lane + width] = value_sum[...].astype(outs[dv_at].dtype)


def whole(array):
    return pl.BlockSpec(array.shape, lambda step: (0,) * len(array.shape))


def attend(prefix, arrays, places, width, causal):
    count = arrays[0].shape[0]
    rows = min(QUERY_ROWS, count)
    return pl.pallas_call(
        functools.partial(attend_kernel, places=places, width=width, causal=causal),
        grid=(count // rows,),
        in_specs=[pl.BlockSpec(memory_space=pltpu.SMEM)] + [whole(array) for array in arrays],
        out_specs=pl.BlockSpec((rows, width), lambda step: (step, 0)),
        out_shape=jax.ShapeDtypeStruct((count, width), jnp.bfloat16),
    )(prefix, *arrays)


def attend_back(prefix, arrays, upstream, places, spots, out_widths, width, causal):
    count = arrays[0].shape[0]
    rows = min(QUERY_ROWS, count)
    shapes = [jax.ShapeDtypeStruct((count, lanes), jnp.bfloat16) for lanes in out_widths]
    return pl.pallas_call(
        functools.partial(
            attend_back_kernel, places=places, spots=spots, width=width, causal=causal
        ),
        grid=(count // rows,),
        in_specs=[pl.BlockSpec(memory_space=pltpu.SMEM)]
        + [whole(array) for array in arrays]
        + [pl.BlockSpec((rows, width), lambda step: (step, 0))],
        out_specs=[whole(shape) for shape in shapes],
        out_shape=shapes,
        scratch_shapes=[pltpu.VMEM((count, width), jnp.float32)] * 2,
    )(prefix, *arrays, upstream)


def per_device(
    hidden_in,
    encoder_in,
    prefix_len,
    exit_flags,
    target_ids,
    out_cotangent,
    self_gain,
    self_query,
    self_key,
    self_value,
    self_output,
    cross_gain,
    cross_query,
    cross_key,
    cross_value,
    cross_output,
    feed_gain,
    feed_gate,
    feed_up,
    feed_down,
    exit_gain,
    embedding,
):
    seq_count, local_len, width = hidden_in.shape
    n_seq = lax.axis_size("seq")
    n_dp = lax.axis_size("dp")
    own = self_query.shape[1]
    own_feed = feed_gate.shape[1]
    own_rows = self_query.shape[0]
    vocab_rows = embedding.shape[0]
    low = jnp.bfloat16

    gains = jnp.stack([self_gain, cross_gain, feed_gain, exit_gain], axis=1)
    gains = jnp.pad(gains, ((0, 0), (0, GAIN_LANES - gains.shape[1])))
    self_pack = jnp.concatenate([self_query, self_key, self_value, self_output, gains], axis=1)
    self_full = lax.all_gather(self_pack, both, axis=0, tiled=True).reshape(n_seq, width, -1)
    cross_pack = jnp.concatenate([cross_query, cross_key, cross_value, cross_output], axis=1)
    cross_full = lax.all_gather(cross_pack, both, axis=0, tiled=True).reshape(n_seq, width, -1)
    feed_pack = jnp.concatenate([feed_gate, feed_up], axis=1)
    feed_full = lax.all_gather(feed_pack, both, axis=0, tiled=True).reshape(n_seq, width, -1)
    down_full = lax.all_gather(feed_down.T, both, axis=0, tiled=True).reshape(
        n_seq, n_dp, own, feed_down.shape[0]
    )
    table = lax.all_gather(embedding.T, "seq", axis=0, tiled=True)
    marks = lax.all_gather(jnp.concatenate([exit_flags, target_ids], axis=0), "dp", axis=0)

    self_qkv, self_out = self_full[:, :, : 3 * own], self_full[:, :, 3 * own : 4 * own]
    cross_q, cross_kv = cross_full[:, :, :own], cross_full[:, :, own : 3 * own]
    cross_out = cross_full[:, :, 3 * own :]
    gain_rows = self_full[0, :, 4 * own : 4 * own + 4].astype(jnp.float32).T
    gain_one, gain_two, gain_three, gain_exit = gain_rows

    residual_in = hidden_in.astype(jnp.float32).reshape(-1, width)
    token_count = residual_in.shape[0]
    normed_one = norm_rows(residual_in, gain_one).astype(low)
    qkv_one = swap(mix("td,zdn->ztn", normed_one, self_qkv).astype(low)).reshape(-1, 3 * own)
    self_places = ((0, 0), (0, own), (0, 2 * own))
    mixture_one = attend(prefix_len, [qkv_one], self_places, own, True)
    mixture_one = swap(mixture_one.reshape(n_seq, token_count, own))
    mixture_one = mixture_one.transpose(1, 0, 2).reshape(token_count, width)
    after_self = residual_in + mix("td,zdn->tzn", mixture_one, self_out).reshape(
        token_count, width
    )
    normed_two = norm_rows(after_self, gain_two).astype(low)
    states = encoder_in.reshape(-1, width)
    kv_two = swap(mix("td,zdn->ztn", states, cross_kv).astype(low)).reshape(-1, 2 * own)
    q_two = swap(mix("td,zdn->ztn", normed_two, cross_q).astype(low)).reshape(-1, own)
    cross_places = ((0, 0), (1, 0), (1, own))
    mixture_two = attend(prefix_len, [q_two, kv_two], cross_places, own, False)
    mixture_two = swap(mixture_two.reshape(n_seq, token_count, own))
    mixture_two = mixture_two.transpose(1, 0, 2).reshape(token_count, width)
    after_cross = after_self + mix("td,zdn->tzn", mixture_two, cross_out).reshape(
        token_count, width
    )
    normed_three = norm_rows(after_cross, gain_three).astype(low)
    gate_up = mix("td,zdn->ztn", normed_three, feed_full)
    gate_pre, up_pre = gate_up[:, :, :own_feed], gate_up[:, :, own_feed:]
    hidden_mid = gated_unit(gate_pre, up_pre).astype(low)
    hidden_rows = hidden_mid.transpose(1, 0, 2).reshape(token_count, n_dp, -1)
    after_feed = after_cross + mix("tkr,zknr->tzn", hidden_rows, down_full).reshape(
        token_count, width
    )
    block_output = after_feed.astype(low).reshape(hidden_in.shape)
    normed_exit = norm_rows(after_feed, gain_exit).astype(low)

    tokens = lax.all_gather(normed_exit, "dp", axis=0, tiled=True)
    flag_rows = marks[:, 0].reshape(-1, 1).astype(jnp.float32)
    target_rows = marks[:, 1].reshape(-1, 1) - lax.axis_index("dp") * vocab_rows
    logits = contract(tokens, table, 1, 0)
    row_max = jnp.max(logits, axis=1, keepdims=True)
    row_sum = jnp.sum(jnp.exp(logits - row_max), axis=1, keepdims=True)
    hits = jnp.arange(vocab_rows)[None, :] == target_rows
    picked = jnp.sum(jnp.where(hits, logits, 0.0), axis=1, keepdims=True)
    parts = lax.all_gather(jnp.stack([row_max[:, 0], row_sum[:, 0], picked[:, 0]]), "dp", axis=0)
    top = jnp.max(parts[:, 0], axis=0)
    log_total = top + jnp.log(jnp.sum(parts[:, 1] * jnp.exp(parts[:, 0] - top), axis=0))
    all_losses = flag_rows[:, 0] * (log_total - jnp.sum(parts[:, 2], axis=0))
    token_losses = lax.dynamic_slice(
        all_losses, (lax.axis_index("dp") * token_count,), (token_count,)
    ).reshape(exit_flags.shape)
    logit_grads = (
        flag_rows * (jnp.exp(logits - log_total[:, None]) - hits.astype(jnp.float32))
    ).astype(low)
    exit_in_grad = lax.psum_scatter(
        contract(logit_grads, table, 1, 1).astype(low), "dp", scatter_dimension=0, tiled=True
    ).astype(jnp.float32)
    embedding_grad = lax.psum_scatter(
        contract(tokens, logit_grads, 0, 0).astype(low), "seq", scatter_dimension=0, tiled=True
    ).astype(jnp.float32).T

    def scatter(full):
        return lax.psum_scatter(
            full.reshape(-1, full.shape[-1]).astype(low), both, scatter_dimension=0, tiled=True
        ).astype(jnp.float32)

    feed_grad, full_exit_gain = norm_back(after_feed, gain_exit, exit_in_grad)
    feed_grad = feed_grad + out_cotangent.reshape(token_count, width)
    branch_three = feed_grad.astype(low)
    branch_cols = branch_three.reshape(token_count, n_seq, own)
    down_grad = scatter(mix("tzn,tkr->zknr", branch_cols, hidden_rows)).T
    hidden_mid_grad = (
        mix("tzn,zknr->tkr", branch_cols, down_full)
        .reshape(token_count, n_seq, own_feed)
        .transpose(1, 0, 2)
    )
    unused, gated_pull = jax.vjp(gated_unit, gate_pre, up_pre)
    gate_grad, up_grad = gated_pull(hidden_mid_grad)
    gate_up_grad = jnp.concatenate([gate_grad.astype(low), up_grad.astype(low)], axis=2)
    feed_sums = scatter(mix("td,ztn->zdn", normed_three, gate_up_grad))
    normed_three_grad = mix("ztn,zdn->td", gate_up_grad, feed_full)
    cross_grad, full_feed_gain = norm_back(after_cross, gain_three, normed_three_grad)
    cross_grad = cross_grad + feed_grad
    branch_two = cross_grad.astype(low)
    branch_cols = branch_two.reshape(token_count, n_seq, own)
    mixture_two_grad = mix("twm,wdm->td", branch_cols, cross_out).astype(low)
    mixture_two_grad = swap(mixture_two_grad.reshape(token_count, n_seq, own).transpose(1, 0, 2))
    q_grad, kv_grad = attend_back(
        prefix_len,
        [q_two, kv_two],
        mixture_two_grad.reshape(-1, own),
        cross_places,
        cross_places,
        (own, 2 * own),
        own,
        False,
    )
    q_grad = swap(q_grad.reshape(n_seq, token_count, own))
    kv_grad = swap(kv_grad.reshape(n_seq, token_count, 2 * own))
    encoder_grad = mix("ztn,zdn->td", kv_grad, cross_kv).reshape(encoder_in.shape)
    cross_sums = scatter(
        jnp.concatenate(
            [
                mix("td,ztn->zdn", normed_two, q_grad).astype(low),
                mix("td,ztn->zdn", states, kv_grad).astype(low),
                mix("td,tzn->zdn", mixture_two, branch_cols).astype(low),
            ],
            axis=2,
        )
    )
    self_grad, full_cross_gain = norm_back(
        after_self, gain_two, mix("ztn,zdn->td", q_grad, cross_q)
    )
    self_grad = self_grad + cross_grad
    branch_one = self_grad.astype(low)
    branch_cols = branch_one.reshape(token_count, n_seq, own)
    mixture_one_grad = mix("twm,wdm->td", branch_cols, self_out).astype(low)
    mixture_one_grad = swap(mixture_one_grad.reshape(token_count, n_seq, own).transpose(1, 0, 2))
    (qkv_grad,) = attend_back(
        prefix_len,
        [qkv_one],
        mixture_one_grad.reshape(-1, own),
        self_places,
        self_places,
        (3 * own,),
        own,
        True,
    )
    qkv_grad = swap(qkv_grad.reshape(n_seq, token_count, 3 * own))
    normed_one_grad = mix("ztn,zdn->td", qkv_grad, self_qkv)
    input_grad, full_self_gain = norm_back(residual_in, gain_one, normed_one_grad)
    hidden_grad = (input_grad + self_grad).reshape(hidden_in.shape)
    gain_terms = jnp.stack(
        [full_self_gain, full_cross_gain, full_feed_gain, full_exit_gain], axis=1
    ).astype(low)
    gain_terms = jnp.pad(gain_terms, ((0, 0), (0, GAIN_LANES - gain_terms.shape[1])))
    self_sums = scatter(
        jnp.concatenate(
            [
                mix("td,ztn->zdn", normed_one, qkv_grad).astype(low),
                mix("td,tzn->zdn", mixture_one, branch_cols).astype(low),
                jnp.broadcast_to(gain_terms[None], (n_seq, width, GAIN_LANES)),
            ],
            axis=2,
        )
    )

    def piece(sums, at):
        return sums[:, at * own : (at + 1) * own]

    gain_sums = self_sums[:, 4 * own : 4 * own + 4].T
    return (
        block_output,
        token_losses,
        hidden_grad,
        encoder_grad,
        gain_sums[0],
        piece(self_sums, 0),
        piece(self_sums, 1),
        piece(self_sums, 2),
        piece(self_sums, 3),
        gain_sums[1],
        piece(cross_sums, 0),
        piece(cross_sums, 1),
        piece(cross_sums, 2),
        piece(cross_sums, 3),
        gain_sums[2],
        feed_sums[:, :own_feed],
        feed_sums[:, own_feed:],
        down_grad,
        gain_sums[3],
        embedding_grad,
    )


def solution(mesh):
    tokens = P("dp", "seq")
    rows = P("dp")
    matrix = P("dp", "seq")
    block = P("dp", "seq", None)
    attention = (rows,) + (matrix,) * 4
    return jax.shard_map(
        per_device,
        mesh=mesh,
        in_specs=(block, block, rows, tokens, tokens, block)
        + attention * 2
        + (rows, matrix, matrix, matrix, rows, matrix),
        out_specs=(block, tokens, block, block)
        + attention * 2
        + (rows, matrix, matrix, matrix, rows, matrix),
        check_vma=False,
    )
```

```python
import functools

import jax
import jax.numpy as jnp
from jax import lax
from jax.experimental import pallas as pl
from jax.experimental.pallas import tpu as pltpu
from jax.sharding import PartitionSpec as P

HD = 64
QUERY_ROWS = 256
GAIN_LANES = 128

norm_eps = 1e-06
masked_score = -1000000000.0


def contract(first_op, second_op, first_dim, second_dim):
    return lax.dot_general(
        first_op,
        second_op,
        (((first_dim,), (second_dim,)), ((), ())),
        preferred_element_type=jnp.float32,
    )


def norm_rows(inputs, scaling):
    return (
        inputs * lax.rsqrt(jnp.mean(inputs * inputs, axis=-1, keepdims=True) + norm_eps) * scaling
    )


def norm_back(inputs, scaling, upstream):
    unused, pullback = jax.vjp(norm_rows, inputs, scaling)
    return pullback(upstream)


def gated_unit(gate_in, upward):
    return jax.nn.gelu(gate_in, approximate=True) * upward


def swap(pieces):
    return lax.all_to_all(pieces, "seq", 0, 0, tiled=True)


def spread(shard):
    return swap(jnp.broadcast_to(shard[None], (lax.axis_size("seq"),) + shard.shape))


def stacked(matrix, count):
    rows, columns = matrix.shape
    return matrix.astype(jnp.bfloat16).reshape(rows, count, columns // count).transpose(1, 0, 2)


def side_by_side(pieces):
    count, rows, columns = pieces.shape
    return pieces.transpose(1, 0, 2).reshape(rows, count * columns)


def cut(array, sizes, axis):
    edges = [sum(sizes[:at]) for at in range(1, len(sizes))]
    return jnp.split(array, edges, axis=axis)


def head_lanes(width, head):
    lanes = lax.broadcasted_iota(jnp.int32, (1, width), 1)
    return (lanes >= head * HD) & (lanes < (head + 1) * HD)


def attend_kernel(prefix_ref, *refs, places, width, causal):
    out_ref = refs[-1]
    step = pl.program_id(0)
    (q_at, q_lane), (k_at, k_lane), (v_at, v_lane) = places
    rows = out_ref.shape[0]
    queries = refs[q_at][pl.ds(pl.multiple_of(step * rows, rows), rows), q_lane : q_lane + width]
    key_rows = refs[k_at][:, k_lane : k_lane + width]
    values = refs[v_at][:, v_lane : v_lane + width]
    count = key_rows.shape[0]
    queries = queries * jnp.asarray(HD**-0.5, queries.dtype)
    if causal:
        query_pos = step * rows + lax.broadcasted_iota(jnp.int32, (rows, count), 0)
        key_pos = lax.broadcasted_iota(jnp.int32, (rows, count), 1)
        allowed = (key_pos <= query_pos) | (key_pos < prefix_ref[0])
    total = jnp.zeros((rows, width), jnp.float32)
    for head in range(width // HD):
        mine = head_lanes(width, head)
        scores = contract(jnp.where(mine, queries, jnp.zeros_like(queries)), key_rows, 1, 1)
        if causal:
            scores = jnp.where(allowed, scores, masked_score)
        exponent = jnp.exp(scores - jnp.max(scores, axis=1, keepdims=True))
        shares = exponent * (1.0 / jnp.sum(exponent, axis=1, keepdims=True))
        total = jnp.where(mine, contract(shares.astype(values.dtype), values, 1, 0), total)
    out_ref[...] = total.astype(out_ref.dtype)


def attend_back_kernel(prefix_ref, *refs, places, spots, width, causal):
    count_in = 1 + max(at for at, lane in places)
    upstream_ref = refs[count_in]
    outs = refs[count_in + 1 : -2]
    key_sum, value_sum = refs[-2:]
    step = pl.program_id(0)
    (q_at, q_lane), (k_at, k_lane), (v_at, v_lane) = places
    (dq_at, dq_lane), (dk_at, dk_lane), (dv_at, dv_lane) = spots
    rows = upstream_ref.shape[0]
    block = pl.ds(pl.multiple_of(step * rows, rows), rows)
    queries = refs[q_at][block, q_lane : q_lane + width]
    key_rows = refs[k_at][:, k_lane : k_lane + width]
    values = refs[v_at][:, v_lane : v_lane + width]
    upstream = upstream_ref[...]
    count = key_rows.shape[0]
    queries = queries * jnp.asarray(HD**-0.5, queries.dtype)
    if causal:
        key_pos = lax.broadcasted_iota(jnp.int32, (count, rows), 0)
        query_pos = step * rows + lax.broadcasted_iota(jnp.int32, (count, rows), 1)
        allowed = (key_pos <= query_pos) | (key_pos < prefix_ref[0])
    query_grads = jnp.zeros((rows, width), jnp.float32)
    key_grads = jnp.zeros((count, width), jnp.float32)
    value_grads = jnp.zeros((count, width), jnp.float32)
    for head in range(width // HD):
        mine = head_lanes(width, head)
        scores = contract(key_rows, jnp.where(mine, queries, jnp.zeros_like(queries)), 1, 1)
        if causal:
            scores = jnp.where(allowed, scores, masked_score)
        exponent = jnp.exp(scores - jnp.max(scores, axis=0, keepdims=True))
        shares = exponent * (1.0 / jnp.sum(exponent, axis=0, keepdims=True))
        share_grads = contract(values, jnp.where(mine, upstream, jnp.zeros_like(upstream)), 1, 1)
        centre = jnp.sum(shares * share_grads, axis=0, keepdims=True)
        score_grads = (shares * (share_grads - centre)).astype(queries.dtype)
        query_grads = jnp.where(mine, contract(score_grads, key_rows, 0, 0), query_grads)
        key_grads = jnp.where(mine, contract(score_grads, queries, 1, 0), key_grads)
        value_grads = jnp.where(
            mine, contract(shares.astype(upstream.dtype), upstream, 1, 0), value_grads
        )
    outs[dq_at][block, dq_lane : dq_lane + width] = (query_grads * HD**-0.5).astype(
        outs[dq_at].dtype
    )

    @pl.when(step == 0)
    def _():
        key_sum[...] = key_grads
        value_sum[...] = value_grads

    @pl.when(step > 0)
    def _():
        key_sum[...] += key_grads
        value_sum[...] += value_grads

    @pl.when(step == pl.num_programs(0) - 1)
    def _():
        outs[dk_at][:, dk_lane : dk_lane + width] = key_sum[...].astype(outs[dk_at].dtype)
        outs[dv_at][:, dv_lane : dv_lane + width] = value_sum[...].astype(outs[dv_at].dtype)


def whole(array):
    return pl.BlockSpec(array.shape, lambda step: (0,) * len(array.shape))


def attend(prefix, arrays, places, width, causal):
    count = arrays[0].shape[0]
    rows = min(QUERY_ROWS, count)
    return pl.pallas_call(
        functools.partial(attend_kernel, places=places, width=width, causal=causal),
        grid=(count // rows,),
        in_specs=[pl.BlockSpec(memory_space=pltpu.SMEM)] + [whole(array) for array in arrays],
        out_specs=pl.BlockSpec((rows, width), lambda step: (step, 0)),
        out_shape=jax.ShapeDtypeStruct((count, width), jnp.bfloat16),
    )(prefix, *arrays)


def attend_back(prefix, arrays, upstream, places, spots, out_widths, width, causal):
    count = arrays[0].shape[0]
    rows = min(QUERY_ROWS, count)
    shapes = [jax.ShapeDtypeStruct((count, lanes), jnp.bfloat16) for lanes in out_widths]
    return pl.pallas_call(
        functools.partial(
            attend_back_kernel, places=places, spots=spots, width=width, causal=causal
        ),
        grid=(count // rows,),
        in_specs=[pl.BlockSpec(memory_space=pltpu.SMEM)]
        + [whole(array) for array in arrays]
        + [pl.BlockSpec((rows, width), lambda step: (step, 0))],
        out_specs=[whole(shape) for shape in shapes],
        out_shape=shapes,
        scratch_shapes=[pltpu.VMEM((count, width), jnp.float32)] * 2,
    )(prefix, *arrays, upstream)


def per_device(
    hidden_in,
    encoder_in,
    prefix_len,
    exit_flags,
    target_ids,
    out_cotangent,
    self_gain,
    self_query,
    self_key,
    self_value,
    self_output,
    cross_gain,
    cross_query,
    cross_key,
    cross_value,
    cross_output,
    feed_gain,
    feed_gate,
    feed_up,
    feed_down,
    exit_gain,
    embedding,
):
    seq_count, local_len, width = hidden_in.shape
    n_seq = lax.axis_size("seq")
    n_dp = lax.axis_size("dp")
    own = self_query.shape[1]
    own_feed = feed_gate.shape[1]
    own_rows = self_query.shape[0]
    vocab_rows = embedding.shape[0]
    low = jnp.bfloat16

    gains = jnp.stack([self_gain, cross_gain, feed_gain, exit_gain], axis=1)
    gains = jnp.pad(gains, ((0, 0), (0, GAIN_LANES - gains.shape[1])))
    down_folds = -(-feed_down.shape[0] // own_rows)
    down_pad = down_folds * own_rows - feed_down.shape[0]
    self_parts = spread(
        jnp.concatenate([self_query, self_key, self_value, self_output], axis=1)
    )
    self_full = lax.all_gather(
        jnp.concatenate(
            [
                side_by_side(self_parts[:, :, : 3 * own]),
                side_by_side(self_parts[:, :, 3 * own :]),
                gains,
            ],
            axis=1,
        ),
        "dp",
        axis=0,
        tiled=True,
    )
    rest_sizes = (own, 2 * own, own, own_feed, own_feed) + (own,) * down_folds
    rest_parts = spread(
        jnp.concatenate(
            [cross_query, cross_key, cross_value, cross_output, feed_gate, feed_up]
            + list(
                jnp.pad(feed_down, ((0, down_pad), (0, 0))).reshape(down_folds, own_rows, own)
            ),
            axis=1,
        )
    )
    rest_full = lax.all_gather(
        jnp.concatenate(
            [side_by_side(part) for part in cut(rest_parts, rest_sizes, 2)], axis=1
        ),
        "dp",
        axis=0,
        tiled=True,
    )
    table = lax.all_gather(embedding.T, "seq", axis=0, tiled=True)
    marks = lax.all_gather(jnp.concatenate([exit_flags, target_ids], axis=0), "dp", axis=0)

    full_sizes = tuple(n_seq * size for size in rest_sizes)
    self_qkv, self_out = self_full[:, : 3 * width], self_full[:, 3 * width : 4 * width]
    cross_q, cross_kv, cross_out, gate_full, up_full, *down_parts = cut(rest_full, full_sizes, 1)
    down_full = jnp.stack(
        [part.reshape(n_dp, own_rows, width) for part in down_parts], axis=1
    ).reshape(n_dp, -1, width)[:, : feed_down.shape[0]]
    down_full = down_full.reshape(-1, width)
    gain_rows = self_full[:, 4 * width : 4 * width + 4].astype(jnp.float32).T
    gain_one, gain_two, gain_three, gain_exit = gain_rows

    residual_in = hidden_in.astype(jnp.float32).reshape(-1, width)
    token_count = residual_in.shape[0]
    normed_one = norm_rows(residual_in, gain_one).astype(low)
    qkv_one = swap(stacked(contract(normed_one, self_qkv, 1, 0), n_seq)).reshape(-1, 3 * own)
    self_places = ((0, 0), (0, own), (0, 2 * own))
    mixture_one = attend(prefix_len, [qkv_one], self_places, own, True)
    mixture_one = side_by_side(swap(mixture_one.reshape(n_seq, token_count, own)))
    after_self = residual_in + contract(mixture_one, self_out, 1, 0)
    normed_two = norm_rows(after_self, gain_two).astype(low)
    states = encoder_in.reshape(-1, width)
    kv_two = swap(stacked(contract(states, cross_kv, 1, 0), n_seq)).reshape(-1, 2 * own)
    q_two = swap(stacked(contract(normed_two, cross_q, 1, 0), n_seq)).reshape(-1, own)
    cross_places = ((0, 0), (1, 0), (1, own))
    mixture_two = attend(prefix_len, [q_two, kv_two], cross_places, own, False)
    mixture_two = side_by_side(swap(mixture_two.reshape(n_seq, token_count, own)))
    after_cross = after_self + contract(mixture_two, cross_out, 1, 0)
    normed_three = norm_rows(after_cross, gain_three).astype(low)
    gate_pre = contract(normed_three, gate_full, 1, 0)
    up_pre = contract(normed_three, up_full, 1, 0)
    hidden_mid = gated_unit(gate_pre, up_pre).astype(low)
    after_feed = after_cross + contract(hidden_mid, down_full, 1, 0)
    block_output = after_feed.astype(low).reshape(hidden_in.shape)
    normed_exit = norm_rows(after_feed, gain_exit).astype(low)

    tokens = lax.all_gather(normed_exit, "dp", axis=0, tiled=True)
    flag_rows = marks[:, 0].reshape(-1, 1).astype(jnp.float32)
    target_rows = marks[:, 1].reshape(-1, 1) - lax.axis_index("dp") * vocab_rows
    logits = contract(tokens, table, 1, 0)
    row_max = jnp.max(logits, axis=1, keepdims=True)
    row_sum = jnp.sum(jnp.exp(logits - row_max), axis=1, keepdims=True)
    hits = jnp.arange(vocab_rows)[None, :] == target_rows
    picked = jnp.sum(jnp.where(hits, logits, 0.0), axis=1, keepdims=True)
    parts = lax.all_gather(jnp.stack([row_max[:, 0], row_sum[:, 0], picked[:, 0]]), "dp", axis=0)
    top = jnp.max(parts[:, 0], axis=0)
    log_total = top + jnp.log(jnp.sum(parts[:, 1] * jnp.exp(parts[:, 0] - top), axis=0))
    all_losses = flag_rows[:, 0] * (log_total - jnp.sum(parts[:, 2], axis=0))
    token_losses = lax.dynamic_slice(
        all_losses, (lax.axis_index("dp") * token_count,), (token_count,)
    ).reshape(exit_flags.shape)
    logit_grads = (
        flag_rows * (jnp.exp(logits - log_total[:, None]) - hits.astype(jnp.float32))
    ).astype(low)
    exit_in_grad = lax.psum_scatter(
        contract(logit_grads, table, 1, 1).astype(low), "dp", scatter_dimension=0, tiled=True
    )
    table_terms = contract(tokens, logit_grads, 0, 0).astype(low)
    exit_in_grad, table_terms = lax.optimization_barrier((exit_in_grad, table_terms))
    exit_in_grad = exit_in_grad.astype(jnp.float32)
    embedding_grad = lax.psum_scatter(table_terms, "seq", scatter_dimension=0, tiled=True)
    embedding_grad = embedding_grad.astype(jnp.float32).T

    feed_grad, full_exit_gain = norm_back(after_feed, gain_exit, exit_in_grad)
    feed_grad = feed_grad + out_cotangent.reshape(token_count, width)
    branch_three = feed_grad.astype(low)
    hidden_mid_grad = contract(branch_three, down_full, 1, 1)
    unused, gated_pull = jax.vjp(gated_unit, gate_pre, up_pre)
    gate_grad, up_grad = gated_pull(hidden_mid_grad)
    gate_grad, up_grad = gate_grad.astype(low), up_grad.astype(low)
    normed_three_grad = contract(gate_grad, gate_full, 1, 1) + contract(up_grad, up_full, 1, 1)
    cross_grad, full_feed_gain = norm_back(after_cross, gain_three, normed_three_grad)
    cross_grad = cross_grad + feed_grad
    branch_two = cross_grad.astype(low)
    mixture_two_grad = swap(stacked(contract(branch_two, cross_out, 1, 1), n_seq))
    q_grad, kv_grad = attend_back(
        prefix_len,
        [q_two, kv_two],
        mixture_two_grad.reshape(-1, own),
        cross_places,
        cross_places,
        (own, 2 * own),
        own,
        False,
    )
    q_grad = side_by_side(swap(q_grad.reshape(n_seq, token_count, own)))
    kv_grad = side_by_side(swap(kv_grad.reshape(n_seq, token_count, 2 * own)))
    encoder_grad = contract(kv_grad, cross_kv, 1, 1).reshape(encoder_in.shape)
    down_terms = contract(hidden_mid, branch_three, 0, 0).astype(low)
    down_terms = jnp.pad(
        down_terms.reshape(n_dp, -1, width), ((0, 0), (0, down_pad), (0, 0))
    ).reshape(n_dp, down_folds, own_rows, width)
    rest_terms = lax.psum_scatter(
        jnp.concatenate(
            [
                contract(normed_two, q_grad, 0, 0).astype(low),
                contract(states, kv_grad, 0, 0).astype(low),
                contract(mixture_two, branch_two, 0, 0).astype(low),
                contract(normed_three, gate_grad, 0, 0).astype(low),
                contract(normed_three, up_grad, 0, 0).astype(low),
            ]
            + [down_terms[:, fold].reshape(width, width) for fold in range(down_folds)],
            axis=1,
        ),
        "dp",
        scatter_dimension=0,
        tiled=True,
    )
    rest_sums = swap(
        jnp.concatenate(
            [stacked(part, n_seq) for part in cut(rest_terms, full_sizes, 1)], axis=2
        )
    )
    rest_sums = jnp.sum(rest_sums.astype(jnp.float32), axis=0)
    cross_q_sum, cross_kv_sum, cross_out_sum, gate_sum, up_sum, *down_sums = cut(
        rest_sums, rest_sizes, 1
    )
    down_grad = jnp.concatenate(down_sums, axis=0)[: feed_down.shape[0]]
    self_grad, full_cross_gain = norm_back(after_self, gain_two, contract(q_grad, cross_q, 1, 1))
    self_grad = self_grad + cross_grad
    branch_one = self_grad.astype(low)
    mixture_one_grad = swap(stacked(contract(branch_one, self_out, 1, 1), n_seq))
    (qkv_grad,) = attend_back(
        prefix_len,
        [qkv_one],
        mixture_one_grad.reshape(-1, own),
        self_places,
        self_places,
        (3 * own,),
        own,
        True,
    )
    qkv_grad = side_by_side(swap(qkv_grad.reshape(n_seq, token_count, 3 * own)))
    normed_one_grad = contract(qkv_grad, self_qkv, 1, 1)
    input_grad, full_self_gain = norm_back(residual_in, gain_one, normed_one_grad)
    hidden_grad = (input_grad + self_grad).reshape(hidden_in.shape)
    gain_terms = jnp.stack(
        [full_self_gain, full_cross_gain, full_feed_gain, full_exit_gain], axis=1
    ).astype(low)
    gain_terms = jnp.pad(gain_terms, ((0, 0), (0, GAIN_LANES - gain_terms.shape[1])))
    self_terms = lax.psum_scatter(
        jnp.concatenate(
            [
                contract(normed_one, qkv_grad, 0, 0).astype(low),
                contract(mixture_one, branch_one, 0, 0).astype(low),
                gain_terms,
            ],
            axis=1,
        ),
        "dp",
        scatter_dimension=0,
        tiled=True,
    )
    self_sums = swap(
        jnp.concatenate(
            [
                stacked(self_terms[:, : 3 * width], n_seq),
                stacked(self_terms[:, 3 * width : 4 * width], n_seq),
                jnp.broadcast_to(self_terms[None, :, 4 * width :], (n_seq, own_rows, GAIN_LANES)),
            ],
            axis=2,
        )
    )
    self_sums = jnp.sum(self_sums.astype(jnp.float32), axis=0)

    def piece(sums, at):
        return sums[:, at * own : (at + 1) * own]

    gain_sums = self_sums[:, 4 * own : 4 * own + 4].T
    return (
        block_output,
        token_losses,
        hidden_grad,
        encoder_grad,
        gain_sums[0],
        piece(self_sums, 0),
        piece(self_sums, 1),
        piece(self_sums, 2),
        piece(self_sums, 3),
        gain_sums[1],
        cross_q_sum,
        piece(cross_kv_sum, 0),
        piece(cross_kv_sum, 1),
        cross_out_sum,
        gain_sums[2],
        gate_sum,
        up_sum,
        down_grad,
        gain_sums[3],
        embedding_grad,
    )


def solution(mesh):
    tokens = P("dp", "seq")
    rows = P("dp")
    matrix = P("dp", "seq")
    block = P("dp", "seq", None)
    attention = (rows,) + (matrix,) * 4
    return jax.shard_map(
        per_device,
        mesh=mesh,
        in_specs=(block, block, rows, tokens, tokens, block)
        + attention * 2
        + (rows, matrix, matrix, matrix, rows, matrix),
        out_specs=(block, tokens, block, block)
        + attention * 2
        + (rows, matrix, matrix, matrix, rows, matrix),
        check_vma=False,
    )
```

```python
import functools

import jax
import jax.numpy as jnp
from jax import lax
from jax.experimental import pallas as pl
from jax.experimental.layout import Layout, with_layout_constraint
from jax.experimental.pallas import tpu as pltpu
from jax.sharding import PartitionSpec as P

HD = 64
GAIN_LANES = 128
TOKEN_ROWS = 256
LANES = 128

norm_eps = 1e-06
masked_score = -1000000000.0


def contract(first_op, second_op, first_dim, second_dim):
    return lax.dot_general(
        first_op,
        second_op,
        (((first_dim,), (second_dim,)), ((), ())),
        preferred_element_type=jnp.float32,
    )


def rows_first(array):
    return with_layout_constraint(array, Layout(major_to_minor=tuple(range(array.ndim))))


def norm_columns(inputs, scaling):
    return (
        inputs
        * lax.rsqrt(jnp.mean(inputs * inputs, axis=0, keepdims=True) + norm_eps)
        * scaling[:, None]
    )


def norm_back(inputs, scaling, upstream):
    unused, pullback = jax.vjp(norm_columns, inputs, scaling)
    return pullback(upstream)


def gated_unit(gate_in, upward):
    return jax.nn.gelu(gate_in, approximate=True) * upward


def swap(pieces):
    return lax.all_to_all(pieces, "seq", 0, 0, tiled=True)


def move_kernel(*refs, moves, count):
    for source, taken, target, put in moves:
        refs[count + target][put] = refs[source][taken]


def move(arrays, shapes, moves):
    return pl.pallas_call(
        functools.partial(move_kernel, moves=moves, count=len(arrays)),
        out_shape=[jax.ShapeDtypeStruct(shape, jnp.bfloat16) for shape in shapes],
    )(*arrays)


def sum_kernel(terms_ref, *refs, pieces):
    for ref, low, high in zip(refs, pieces[:-1], pieces[1:]):
        total = terms_ref[0, :, low:high].astype(jnp.float32)
        for block in range(1, terms_ref.shape[0]):
            total += terms_ref[block, :, low:high].astype(jnp.float32)
        ref[...] = total


def edges(sizes):
    return [sum(sizes[:at]) for at in range(len(sizes) + 1)]


every = slice(None)


def fetch(shards, extra):
    n_seq = lax.axis_size("seq")
    rows = shards[0].shape[0]
    sizes = [shard.shape[1] for shard in shards]
    starts = edges(sizes)
    moves = [
        (at, (every, every), 0, (block, every, slice(starts[at], starts[at + 1])))
        for at in range(len(shards))
        for block in range(n_seq)
    ]
    (copies,) = move(shards, [(n_seq, rows, starts[-1])], moves)
    parts = swap(copies)
    moves = [
        (
            0,
            (block, every, slice(starts[at], starts[at + 1])),
            0,
            (every, slice(low, low + sizes[at])),
        )
        for at in range(len(shards))
        for block in range(n_seq)
        for low in [n_seq * starts[at] + block * sizes[at]]
    ]
    width = n_seq * starts[-1]
    if extra is not None:
        moves.append((1, (every, every), 0, (every, slice(width, width + extra.shape[1]))))
        width += extra.shape[1]
    (full,) = move([parts] if extra is None else [parts, extra], [(rows, width)], moves)
    return lax.all_gather(full, "dp", axis=0, tiled=True)


def deliver(terms, sizes, extra, out_sizes):
    n_seq = lax.axis_size("seq")
    rows = terms.shape[0]
    starts = edges(sizes)
    moves = [
        (
            0,
            (every, slice(low, low + sizes[at])),
            0,
            (block, every, slice(starts[at], starts[at + 1])),
        )
        for at in range(len(sizes))
        for block in range(n_seq)
        for low in [n_seq * starts[at] + block * sizes[at]]
    ]
    width = starts[-1]
    if extra:
        low = n_seq * width
        moves += [
            (0, (every, slice(low, low + extra)), 0, (block, every, slice(width, width + extra)))
            for block in range(n_seq)
        ]
    (parts,) = move([terms], [(n_seq, rows, width + extra)], moves)
    return pl.pallas_call(
        functools.partial(sum_kernel, pieces=edges(out_sizes)),
        out_shape=[jax.ShapeDtypeStruct((rows, size), jnp.float32) for size in out_sizes],
    )(swap(parts))


def cut(array, sizes):
    return jnp.split(array, edges(sizes)[1:-1], axis=1)


def head_rows(row, head):
    return slice(row + head * HD, row + (head + 1) * HD)


def score_columns(key_ref, key_row, queries, head, allowed):
    scores = jnp.concatenate(
        [
            contract(key_ref[block, head_rows(key_row, head), :], queries, 0, 0)
            for block in range(key_ref.shape[0])
        ],
        axis=0,
    )
    if allowed is not None:
        scores = jnp.where(allowed, scores, masked_score)
    exponent = jnp.exp(scores - jnp.max(scores, axis=0, keepdims=True))
    return exponent * (1.0 / jnp.sum(exponent, axis=0, keepdims=True))


def allowed_columns(prefix_ref, step, blocks, rows):
    key_pos = lax.broadcasted_iota(jnp.int32, (blocks * rows, rows), 0)
    query_pos = step * rows + lax.broadcasted_iota(jnp.int32, (blocks * rows, rows), 1)
    return (key_pos <= query_pos) | (key_pos < prefix_ref[0])


def attend_kernel(prefix_ref, *refs, places, causal):
    out_ref = refs[-1]
    step = pl.program_id(0)
    (q_at, q_row), (k_at, k_row), (v_at, v_row) = places
    blocks, unused, rows = refs[k_at].shape
    allowed = allowed_columns(prefix_ref, step, blocks, rows) if causal else None
    for head in range(out_ref.shape[1] // HD):
        queries = refs[q_at][step, head_rows(q_row, head), :]
        queries = queries * jnp.asarray(HD**-0.5, queries.dtype)
        shares = score_columns(refs[k_at], k_row, queries, head, allowed).astype(queries.dtype)
        total = jnp.zeros(queries.shape, jnp.float32)
        for block in range(blocks):
            values = refs[v_at][block, head_rows(v_row, head), :]
            total += contract(values, shares[block * rows : (block + 1) * rows], 1, 0)
        out_ref[0, head_rows(0, head), :] = total.astype(out_ref.dtype)


def attend_back_kernel(prefix_ref, *refs, places, count, causal):
    upstream_ref = refs[count]
    outs = refs[count + 1 : -2]
    key_sum, value_sum = refs[-2:]
    step = pl.program_id(0)
    (q_at, q_row), (k_at, k_row), (v_at, v_row) = places
    blocks, unused, rows = refs[k_at].shape
    allowed = allowed_columns(prefix_ref, step, blocks, rows) if causal else None

    @pl.when(step == 0)
    def _():
        key_sum[...] = jnp.zeros_like(key_sum)
        value_sum[...] = jnp.zeros_like(value_sum)

    for head in range(upstream_ref.shape[1] // HD):
        mine = head_rows(0, head)
        queries = refs[q_at][step, head_rows(q_row, head), :]
        queries = queries * jnp.asarray(HD**-0.5, queries.dtype)
        upstream = upstream_ref[0, mine, :]
        shares = score_columns(refs[k_at], k_row, queries, head, allowed)
        share_grads = jnp.concatenate(
            [
                contract(refs[v_at][block, head_rows(v_row, head), :], upstream, 0, 0)
                for block in range(blocks)
            ],
            axis=0,
        )
        centre = jnp.sum(shares * share_grads, axis=0, keepdims=True)
        score_grads = (shares * (share_grads - centre)).astype(queries.dtype)
        shares = shares.astype(queries.dtype)
        total = jnp.zeros(queries.shape, jnp.float32)
        for block in range(blocks):
            part = slice(block * rows, (block + 1) * rows)
            key_rows = refs[k_at][block, head_rows(k_row, head), :]
            total += contract(key_rows, score_grads[part], 1, 0)
            key_sum[block, mine, :] += contract(queries, score_grads[part], 1, 1)
            value_sum[block, mine, :] += contract(upstream, shares[part], 1, 1)
        outs[q_at][step, head_rows(q_row, head), :] = (total * HD**-0.5).astype(outs[q_at].dtype)

    @pl.when(step == pl.num_programs(0) - 1)
    def _():
        width = key_sum.shape[1]
        outs[k_at][:, k_row : k_row + width, :] = key_sum[...].astype(outs[k_at].dtype)
        outs[v_at][:, v_row : v_row + width, :] = value_sum[...].astype(outs[v_at].dtype)


def exit_kernel(token_ref, table_ref, shifted_ref, product_ref, part_ref, logit_ref, *, rows):
    lanes = table_ref.shape[1]
    chunk = next(size for size in (1024, 512, 256, 128) if lanes % size == 0)
    tokens = token_ref[...]
    row_max = jnp.full((tokens.shape[0], 1), -jnp.inf, jnp.float32)
    for low in range(0, lanes, chunk):
        logits = contract(tokens, table_ref[:, low : low + chunk], 1, 0)
        if low + chunk > rows:
            lane = low + lax.broadcasted_iota(jnp.int32, (1, chunk), 1)
            logits = jnp.where(lane < rows, logits, -jnp.inf)
        logit_ref[:, low : low + chunk] = logits
        row_max = jnp.maximum(row_max, jnp.max(logits, axis=1, keepdims=True))
    row_sum = jnp.zeros_like(row_max)
    product = jnp.zeros(product_ref.shape, jnp.float32)
    for low in range(0, lanes, chunk):
        shifted = jnp.exp(logit_ref[:, low : low + chunk] - row_max)
        row_sum += jnp.sum(shifted, axis=1, keepdims=True)
        shifted = shifted.astype(shifted_ref.dtype)
        shifted_ref[:, low : low + chunk] = shifted
        product += contract(shifted, table_ref[:, low : low + chunk], 1, 1)
    product_ref[...] = product
    lane = lax.broadcasted_iota(jnp.int32, part_ref.shape, 1)
    part_ref[...] = jnp.where(lane == 0, row_max, row_sum)


def exit_rows(tokens, table, rows):
    count, width = tokens.shape
    lanes = table.shape[1]
    step_rows = min(TOKEN_ROWS, count)
    return pl.pallas_call(
        functools.partial(exit_kernel, rows=rows),
        grid=(count // step_rows,),
        in_specs=[pl.BlockSpec((step_rows, width), lambda step: (step, 0)), whole(table)],
        out_specs=[
            pl.BlockSpec((step_rows, lanes), lambda step: (step, 0)),
            pl.BlockSpec((step_rows, width), lambda step: (step, 0)),
            pl.BlockSpec((step_rows, LANES), lambda step: (step, 0)),
        ],
        out_shape=[
            jax.ShapeDtypeStruct((count, lanes), jnp.bfloat16),
            jax.ShapeDtypeStruct((count, width), jnp.float32),
            jax.ShapeDtypeStruct((count, LANES), jnp.float32),
        ],
        scratch_shapes=[pltpu.VMEM((step_rows, lanes), jnp.float32)],
    )(tokens, table)


def whole(array):
    return pl.BlockSpec(array.shape, lambda step: (0,) * len(array.shape))


def attend(prefix, arrays, places, width, causal):
    blocks, unused, rows = arrays[0].shape
    return pl.pallas_call(
        functools.partial(attend_kernel, places=places, causal=causal),
        grid=(blocks,),
        in_specs=[pl.BlockSpec(memory_space=pltpu.SMEM)] + [whole(array) for array in arrays],
        out_specs=pl.BlockSpec((1, width, rows), lambda step: (step, 0, 0)),
        out_shape=jax.ShapeDtypeStruct((blocks, width, rows), jnp.bfloat16),
    )(prefix, *arrays)


def attend_back(prefix, arrays, upstream, places, causal):
    blocks, width, rows = upstream.shape
    return pl.pallas_call(
        functools.partial(attend_back_kernel, places=places, count=len(arrays), causal=causal),
        grid=(blocks,),
        in_specs=[pl.BlockSpec(memory_space=pltpu.SMEM)]
        + [whole(array) for array in arrays]
        + [pl.BlockSpec((1, width, rows), lambda step: (step, 0, 0))],
        out_specs=[whole(array) for array in arrays],
        out_shape=[jax.ShapeDtypeStruct(array.shape, array.dtype) for array in arrays],
        scratch_shapes=[pltpu.VMEM((blocks, width, rows), jnp.float32)] * 2,
    )(prefix, *arrays, upstream)


def per_device(
    hidden_in,
    encoder_in,
    prefix_len,
    exit_flags,
    target_ids,
    out_cotangent,
    self_gain,
    self_query,
    self_key,
    self_value,
    self_output,
    cross_gain,
    cross_query,
    cross_key,
    cross_value,
    cross_output,
    feed_gain,
    feed_gate,
    feed_up,
    feed_down,
    exit_gain,
    embedding,
):
    width = hidden_in.shape[2]
    n_seq = lax.axis_size("seq")
    n_dp = lax.axis_size("dp")
    own_rows, own = self_query.shape
    own_feed = feed_gate.shape[1]
    fold_rows = feed_down.shape[0]
    folds = -(-fold_rows // own_rows)
    vocab_rows = embedding.shape[0]
    vocab_lanes = -(-vocab_rows // LANES) * LANES
    low = jnp.bfloat16

    gains = jnp.stack([self_gain, cross_gain, feed_gain, exit_gain], axis=1)
    gains = jnp.pad(gains, ((0, 0), (0, GAIN_LANES - gains.shape[1])))
    near = fetch(
        [
            jnp.concatenate([self_query, self_key, self_value], axis=1),
            self_output,
            cross_query,
            jnp.concatenate([cross_key, cross_value], axis=1),
            cross_output,
        ],
        gains,
    )
    near_sizes = (3 * own, own, own, 2 * own, own)
    self_qkv, self_out, cross_q, cross_kv, cross_out, gain_columns = cut(
        near, tuple(n_seq * size for size in near_sizes) + (GAIN_LANES,)
    )
    folded = jnp.pad(feed_down, ((0, folds * own_rows - fold_rows), (0, 0)))
    feed = fetch(
        [feed_gate, feed_up]
        + [folded[fold * own_rows : (fold + 1) * own_rows] for fold in range(folds)],
        None,
    )
    feed_sizes = (own_feed, own_feed) + (own,) * folds
    gate_full, up_full, *downs = cut(feed, tuple(n_seq * size for size in feed_sizes))
    table = lax.all_gather(
        jnp.pad(embedding.T, ((0, 0), (0, vocab_lanes - vocab_rows))), "seq", axis=0, tiled=True
    )
    marks = lax.all_gather(jnp.concatenate([exit_flags, target_ids], axis=0), "dp", axis=0)
    gain_one, gain_two, gain_three, gain_exit = gain_columns[:, :4].astype(jnp.float32).T

    def blocks(rows):
        return rows.astype(low).reshape(n_seq, -1, rows.shape[1])

    def fold_up(rows):
        rows = rows.reshape(n_dp, fold_rows, -1)
        rows = jnp.pad(rows, ((0, 0), (0, folds * own_rows - fold_rows), (0, 0)))
        return [
            rows[:, fold * own_rows : (fold + 1) * own_rows].reshape(width, -1)
            for fold in range(folds)
        ]

    def unfold(parts):
        parts = [part.reshape(n_dp, own_rows, -1) for part in parts]
        rows = jnp.concatenate(parts, axis=1)[:, :fold_rows]
        return rows.reshape(n_dp * fold_rows, -1)

    residual_in = hidden_in.reshape(-1, width).T.astype(jnp.float32)
    token_count = residual_in.shape[1]
    states = encoder_in.reshape(-1, width).T
    cotangent = out_cotangent.reshape(-1, width).T
    residual_in, states, cotangent, marks = lax.optimization_barrier(
        (residual_in, states, cotangent, marks)
    )
    residual_in, states = rows_first(residual_in), rows_first(states)
    cotangent = rows_first(cotangent)
    normed_one = norm_columns(residual_in, gain_one).astype(low)
    qkv_one = swap(blocks(contract(self_qkv, normed_one, 0, 0)))
    kv_two = swap(blocks(contract(cross_kv, states, 0, 0)))
    self_places = ((0, 0), (0, own), (0, 2 * own))
    mixture_one = swap(attend(prefix_len, [qkv_one], self_places, own, True))
    mixture_one = mixture_one.reshape(width, token_count)
    after_self = residual_in + contract(self_out, mixture_one, 0, 0)
    normed_two = norm_columns(after_self, gain_two).astype(low)
    q_two = swap(blocks(contract(cross_q, normed_two, 0, 0)))
    cross_places = ((0, 0), (1, 0), (1, own))
    mixture_two = swap(attend(prefix_len, [q_two, kv_two], cross_places, own, False))
    mixture_two = mixture_two.reshape(width, token_count)
    after_cross = after_self + contract(cross_out, mixture_two, 0, 0)
    normed_three = norm_columns(after_cross, gain_three).astype(low)
    gate_pre = contract(gate_full, normed_three, 0, 0)
    up_pre = contract(up_full, normed_three, 0, 0)
    hidden_mid = gated_unit(gate_pre, up_pre).astype(low)
    hidden_folds = fold_up(hidden_mid)
    after_feed = after_cross
    for down, hidden in zip(downs, hidden_folds):
        after_feed = after_feed + contract(down, hidden, 0, 0)
    block_output = after_feed.T.astype(low).reshape(hidden_in.shape)
    normed_exit = rows_first(norm_columns(after_feed, gain_exit).astype(low).T)
    normed_exit, table = lax.optimization_barrier((normed_exit, table))

    tokens = lax.all_gather(normed_exit, "dp", axis=0, tiled=True)
    flag_rows = marks[:, 0].reshape(-1, 1).astype(jnp.float32)
    target_rows = marks[:, 1].reshape(-1, 1) - lax.axis_index("dp") * vocab_rows
    hits = jnp.arange(vocab_lanes)[None, :] == target_rows
    hits = hits & (target_rows < vocab_rows)
    target_terms = contract(hits.astype(low), table, 1, 1).astype(low)
    tokens, target_terms = lax.optimization_barrier((tokens, target_terms))
    shifted, products, parts = exit_rows(tokens, table, vocab_rows)
    picked = jnp.sum(tokens.astype(jnp.float32) * target_terms.astype(jnp.float32), axis=1)
    row_max = parts[:, 0]
    parts = lax.all_gather(jnp.stack([row_max, parts[:, 1], picked]), "dp", axis=0)
    top = jnp.max(parts[:, 0], axis=0)
    log_total = top + jnp.log(jnp.sum(parts[:, 1] * jnp.exp(parts[:, 0] - top), axis=0))
    all_losses = flag_rows[:, 0] * (log_total - jnp.sum(parts[:, 2], axis=0))
    token_losses = lax.dynamic_slice(
        all_losses, (lax.axis_index("dp") * token_count,), (token_count,)
    ).reshape(exit_flags.shape)
    factor = flag_rows * jnp.exp(row_max - log_total)[:, None]
    exit_in_grad = lax.psum_scatter(
        rows_first((factor * products - flag_rows * target_terms.astype(jnp.float32)).astype(low)),
        "dp",
        scatter_dimension=0,
        tiled=True,
    )
    logit_grads = jnp.where(hits, factor * shifted - flag_rows, factor * shifted).astype(low)
    table_terms = contract(tokens, logit_grads, 0, 0).astype(low)
    exit_in_grad, table_terms = lax.optimization_barrier((rows_first(exit_in_grad), table_terms))
    exit_in_grad = rows_first(exit_in_grad.T).astype(jnp.float32)
    table_sums = lax.psum_scatter(table_terms, "seq", scatter_dimension=0, tiled=True)

    feed_grad, full_exit_gain = norm_back(after_feed, gain_exit, exit_in_grad)
    feed_grad = feed_grad + cotangent
    branch_three = feed_grad.astype(low)
    hidden_mid_grad = unfold([contract(down, branch_three, 1, 0) for down in downs])
    unused, gated_pull = jax.vjp(gated_unit, gate_pre, up_pre)
    gate_grad, up_grad = gated_pull(hidden_mid_grad)
    gate_grad, up_grad = gate_grad.astype(low), up_grad.astype(low)
    normed_three_grad = contract(gate_full, gate_grad, 1, 0) + contract(up_full, up_grad, 1, 0)
    cross_grad, full_feed_gain = norm_back(after_cross, gain_three, normed_three_grad)
    cross_grad = cross_grad + feed_grad
    branch_two = cross_grad.astype(low)
    mixture_two_grad = swap(blocks(contract(cross_out, branch_two, 1, 0)))
    q_grad, kv_grad = attend_back(
        prefix_len, [q_two, kv_two], mixture_two_grad, cross_places, False
    )
    q_grad = swap(q_grad).reshape(-1, token_count)
    kv_grad = swap(kv_grad).reshape(-1, token_count)
    encoder_grad = contract(kv_grad, cross_kv, 0, 1).reshape(encoder_in.shape)
    rest_terms = jnp.concatenate(
        [
            contract(normed_two, q_grad, 1, 1).astype(low),
            contract(states, kv_grad, 1, 1).astype(low),
            contract(mixture_two, branch_two, 1, 1).astype(low),
            contract(normed_three, gate_grad, 1, 1).astype(low),
            contract(normed_three, up_grad, 1, 1).astype(low),
        ]
        + [contract(hidden, branch_three, 1, 1).astype(low) for hidden in hidden_folds],
        axis=1,
    )
    self_grad, full_cross_gain = norm_back(after_self, gain_two, contract(cross_q, q_grad, 1, 0))
    self_grad = self_grad + cross_grad
    branch_one = self_grad.astype(low)
    mixture_one_grad = blocks(contract(self_out, branch_one, 1, 0))
    mixture_one_grad, rest_terms = lax.optimization_barrier((mixture_one_grad, rest_terms))
    rest_terms, table_sums = lax.optimization_barrier((rest_terms, table_sums))
    embedding_grad = table_sums[:, :vocab_rows].astype(jnp.float32).T
    rest_terms = lax.psum_scatter(rest_terms, "dp", scatter_dimension=0, tiled=True)
    (qkv_grad,) = attend_back(prefix_len, [qkv_one], swap(mixture_one_grad), self_places, True)
    qkv_grad = swap(qkv_grad).reshape(-1, token_count)
    normed_one_grad = contract(self_qkv, qkv_grad, 1, 0)
    input_grad, full_self_gain = norm_back(residual_in, gain_one, normed_one_grad)
    hidden_grad = (input_grad + self_grad).T.reshape(hidden_in.shape)
    gain_terms = jnp.stack(
        [full_self_gain, full_cross_gain, full_feed_gain, full_exit_gain], axis=1
    ).astype(low)
    gain_terms = jnp.pad(gain_terms, ((0, 0), (0, GAIN_LANES - gain_terms.shape[1])))
    self_terms = jnp.concatenate(
        [
            contract(normed_one, qkv_grad, 1, 1).astype(low),
            contract(mixture_one, branch_one, 1, 1).astype(low),
            gain_terms,
        ],
        axis=1,
    )
    self_terms, rest_terms = lax.optimization_barrier((self_terms, rest_terms))
    self_terms = lax.psum_scatter(self_terms, "dp", scatter_dimension=0, tiled=True)
    (
        cross_query_grad,
        cross_key_grad,
        cross_value_grad,
        cross_output_grad,
        feed_gate_grad,
        feed_up_grad,
        *down_sums,
    ) = deliver(rest_terms, near_sizes[2:] + feed_sizes, 0, (own,) * 4 + feed_sizes)
    down_grad = jnp.concatenate(down_sums, axis=0)[:fold_rows]
    self_query_grad, self_key_grad, self_value_grad, self_output_grad, gain_sums = deliver(
        self_terms, near_sizes[:2], GAIN_LANES, (own,) * 4 + (GAIN_LANES,)
    )
    gain_sums = gain_sums[:, :4].T
    return (
        block_output,
        token_losses,
        hidden_grad,
        encoder_grad,
        gain_sums[0],
        self_query_grad,
        self_key_grad,
        self_value_grad,
        self_output_grad,
        gain_sums[1],
        cross_query_grad,
        cross_key_grad,
        cross_value_grad,
        cross_output_grad,
        gain_sums[2],
        feed_gate_grad,
        feed_up_grad,
        down_grad,
        gain_sums[3],
        embedding_grad,
    )


def solution(mesh):
    tokens = P("dp", "seq")
    rows = P("dp")
    matrix = P("dp", "seq")
    block = P("dp", "seq", None)
    attention = (rows,) + (matrix,) * 4
    return jax.shard_map(
        per_device,
        mesh=mesh,
        in_specs=(block, block, rows, tokens, tokens, block)
        + attention * 2
        + (rows, matrix, matrix, matrix, rows, matrix),
        out_specs=(block, tokens, block, block)
        + attention * 2
        + (rows, matrix, matrix, matrix, rows, matrix),
        check_vma=False,
    )
```

```python
import functools

import jax
import jax.numpy as jnp
from jax import lax
from jax.experimental import pallas as pl
from jax.experimental.layout import Layout, with_layout_constraint
from jax.experimental.pallas import tpu as pltpu
from jax.sharding import Mesh
from jax.sharding import PartitionSpec as P

HD = 64
GAIN_LANES = 128
TOKEN_ROWS = 256
LANES = 128

norm_eps = 1e-06
masked_score = -1000000000.0
dp = ("group", "part")


def contract(first_op, second_op, first_dim, second_dim):
    return lax.dot_general(
        first_op,
        second_op,
        (((first_dim,), (second_dim,)), ((), ())),
        preferred_element_type=jnp.float32,
    )


def rows_first(array):
    return with_layout_constraint(array, Layout(major_to_minor=tuple(range(array.ndim))))


def norm_columns(inputs, scaling):
    return (
        inputs
        * lax.rsqrt(jnp.mean(inputs * inputs, axis=0, keepdims=True) + norm_eps)
        * scaling[:, None]
    )


def norm_back(inputs, scaling, upstream):
    unused, pullback = jax.vjp(norm_columns, inputs, scaling)
    return pullback(upstream)


def gated_unit(gate_in, upward):
    return jax.nn.gelu(gate_in, approximate=True) * upward


def swap(pieces, axis):
    return lax.all_to_all(pieces, axis, 0, 0, tiled=True)


def relocate(block):
    size = lax.axis_size("seq")
    pairs = [
        ((group * size + part) * size + at, (group * size + at) * size + part)
        for group in range(lax.axis_size("group"))
        for part in range(size)
        for at in range(size)
    ]
    return lax.ppermute(block, ("group", "part", "seq"), pairs)


def shift(block, by):
    size = lax.axis_size("seq")
    return lax.ppermute(block, "seq", [(at, (at + by) % size) for at in range(size)])


def spot(by):
    size = lax.axis_size("seq")
    at = lax.axis_index("seq") + by % size
    return jnp.where(at >= size, at - size, at)


def move_kernel(*refs, moves, count):
    for source, taken, target, put in moves:
        refs[count + target][put] = refs[source][taken]


def move(arrays, shapes, moves):
    return pl.pallas_call(
        functools.partial(move_kernel, moves=moves, count=len(arrays)),
        out_shape=[jax.ShapeDtypeStruct(shape, jnp.bfloat16) for shape in shapes],
    )(*arrays)


def sum_kernel(terms_ref, *refs, pieces):
    for ref, low, high in zip(refs, pieces[:-1], pieces[1:]):
        total = terms_ref[0, :, low:high].astype(jnp.float32)
        for block in range(1, terms_ref.shape[0]):
            total += terms_ref[block, :, low:high].astype(jnp.float32)
        ref[...] = total


def edges(sizes):
    return [sum(sizes[:at]) for at in range(len(sizes) + 1)]


every = slice(None)


def fetch(shards, extra):
    n_seq = lax.axis_size("seq")
    rows = shards[0].shape[0]
    sizes = [shard.shape[1] for shard in shards]
    starts = edges(sizes)
    moves = [
        (at, (every, every), 0, (block, every, slice(starts[at], starts[at + 1])))
        for at in range(len(shards))
        for block in range(n_seq)
    ]
    (copies,) = move(shards, [(n_seq, rows, starts[-1])], moves)
    parts = swap(copies, "seq")
    moves = [
        (
            0,
            (block, every, slice(starts[at], starts[at + 1])),
            0,
            (every, slice(low, low + sizes[at])),
        )
        for at in range(len(shards))
        for block in range(n_seq)
        for low in [n_seq * starts[at] + block * sizes[at]]
    ]
    width = n_seq * starts[-1]
    if extra is not None:
        moves.append((1, (every, every), 0, (every, slice(width, width + extra.shape[1]))))
        width += extra.shape[1]
    (full,) = move([parts] if extra is None else [parts, extra], [(rows, width)], moves)
    return lax.all_gather(full, dp, axis=0, tiled=True)


def deliver(terms, sizes, extra, out_sizes):
    n_seq = lax.axis_size("seq")
    rows = terms.shape[0]
    starts = edges(sizes)
    moves = [
        (
            0,
            (every, slice(low, low + sizes[at])),
            0,
            (block, every, slice(starts[at], starts[at + 1])),
        )
        for at in range(len(sizes))
        for block in range(n_seq)
        for low in [n_seq * starts[at] + block * sizes[at]]
    ]
    width = starts[-1]
    if extra:
        low = n_seq * width
        moves += [
            (0, (every, slice(low, low + extra)), 0, (block, every, slice(width, width + extra)))
            for block in range(n_seq)
        ]
    (parts,) = move([terms], [(n_seq, rows, width + extra)], moves)
    return pl.pallas_call(
        functools.partial(sum_kernel, pieces=edges(out_sizes)),
        out_shape=[jax.ShapeDtypeStruct((rows, size), jnp.float32) for size in out_sizes],
    )(swap(parts, "seq"))


def cut(array, sizes):
    return jnp.split(array, edges(sizes)[1:-1], axis=1)


def head_rows(row, head):
    return slice(row + head * HD, row + (head + 1) * HD)


def score_columns(key_ref, key_row, queries, head, allowed):
    scores = jnp.concatenate(
        [
            contract(key_ref[block, head_rows(key_row, head), :], queries, 0, 0)
            for block in range(key_ref.shape[0])
        ],
        axis=0,
    )
    if allowed is not None:
        scores = jnp.where(allowed, scores, masked_score)
    exponent = jnp.exp(scores - jnp.max(scores, axis=0, keepdims=True))
    return exponent * (1.0 / jnp.sum(exponent, axis=0, keepdims=True))


def allowed_columns(prefix_ref, step, blocks, rows):
    key_pos = lax.broadcasted_iota(jnp.int32, (blocks * rows, rows), 0)
    query_pos = step * rows + lax.broadcasted_iota(jnp.int32, (blocks * rows, rows), 1)
    return (key_pos <= query_pos) | (key_pos < prefix_ref[0])


def attend_kernel(prefix_ref, *refs, places, causal):
    out_ref = refs[-1]
    step = pl.program_id(0)
    (q_at, q_row), (k_at, k_row), (v_at, v_row) = places
    blocks, unused, rows = refs[k_at].shape
    allowed = allowed_columns(prefix_ref, step, blocks, rows) if causal else None
    for head in range(out_ref.shape[1] // HD):
        queries = refs[q_at][step, head_rows(q_row, head), :]
        queries = queries * jnp.asarray(HD**-0.5, queries.dtype)
        shares = score_columns(refs[k_at], k_row, queries, head, allowed).astype(queries.dtype)
        total = jnp.zeros(queries.shape, jnp.float32)
        for block in range(blocks):
            values = refs[v_at][block, head_rows(v_row, head), :]
            total += contract(values, shares[block * rows : (block + 1) * rows], 1, 0)
        out_ref[0, head_rows(0, head), :] = total.astype(out_ref.dtype)


def attend_back_kernel(prefix_ref, *refs, places, spots, count, causal):
    upstream_ref = refs[count]
    out_ref, key_sum, value_sum = refs[count + 1 :]
    step = pl.program_id(0)
    (q_at, q_row), (k_at, k_row), (v_at, v_row) = places
    blocks, unused, rows = refs[k_at].shape
    allowed = allowed_columns(prefix_ref, step, blocks, rows) if causal else None

    @pl.when(step == 0)
    def _():
        key_sum[...] = jnp.zeros_like(key_sum)
        value_sum[...] = jnp.zeros_like(value_sum)

    for head in range(upstream_ref.shape[1] // HD):
        mine = head_rows(0, head)
        queries = refs[q_at][step, head_rows(q_row, head), :]
        queries = queries * jnp.asarray(HD**-0.5, queries.dtype)
        upstream = upstream_ref[0, mine, :]
        shares = score_columns(refs[k_at], k_row, queries, head, allowed)
        share_grads = jnp.concatenate(
            [
                contract(refs[v_at][block, head_rows(v_row, head), :], upstream, 0, 0)
                for block in range(blocks)
            ],
            axis=0,
        )
        centre = jnp.sum(shares * share_grads, axis=0, keepdims=True)
        score_grads = (shares * (share_grads - centre)).astype(queries.dtype)
        shares = shares.astype(queries.dtype)
        total = jnp.zeros(queries.shape, jnp.float32)
        for block in range(blocks):
            part = slice(block * rows, (block + 1) * rows)
            key_rows = refs[k_at][block, head_rows(k_row, head), :]
            total += contract(key_rows, score_grads[part], 1, 0)
            key_sum[block, mine, :] += contract(queries, score_grads[part], 1, 1)
            value_sum[block, mine, :] += contract(upstream, shares[part], 1, 1)
        out_ref[step, head_rows(spots[0], head), :] = (total * HD**-0.5).astype(out_ref.dtype)

    @pl.when(step == pl.num_programs(0) - 1)
    def _():
        width = key_sum.shape[1]
        out_ref[:, spots[1] : spots[1] + width, :] = key_sum[...].astype(out_ref.dtype)
        out_ref[:, spots[2] : spots[2] + width, :] = value_sum[...].astype(out_ref.dtype)


def exit_kernel(token_ref, table_ref, shifted_ref, product_ref, part_ref, logit_ref, *, rows):
    lanes = table_ref.shape[1]
    chunk = next(size for size in (1024, 512, 256, 128) if lanes % size == 0)
    tokens = token_ref[...]
    row_max = jnp.full((tokens.shape[0], 1), -jnp.inf, jnp.float32)
    for low in range(0, lanes, chunk):
        logits = contract(tokens, table_ref[:, low : low + chunk], 1, 0)
        if low + chunk > rows:
            lane = low + lax.broadcasted_iota(jnp.int32, (1, chunk), 1)
            logits = jnp.where(lane < rows, logits, -jnp.inf)
        logit_ref[:, low : low + chunk] = logits
        row_max = jnp.maximum(row_max, jnp.max(logits, axis=1, keepdims=True))
    row_sum = jnp.zeros_like(row_max)
    product = jnp.zeros(product_ref.shape, jnp.float32)
    for low in range(0, lanes, chunk):
        shifted = jnp.exp(logit_ref[:, low : low + chunk] - row_max)
        row_sum += jnp.sum(shifted, axis=1, keepdims=True)
        shifted = shifted.astype(shifted_ref.dtype)
        shifted_ref[:, low : low + chunk] = shifted
        product += contract(shifted, table_ref[:, low : low + chunk], 1, 1)
    product_ref[...] = product
    lane = lax.broadcasted_iota(jnp.int32, part_ref.shape, 1)
    part_ref[...] = jnp.where(lane == 0, row_max, row_sum)


def exit_rows(tokens, table, rows):
    count, width = tokens.shape
    lanes = table.shape[1]
    step_rows = min(TOKEN_ROWS, count)
    return pl.pallas_call(
        functools.partial(exit_kernel, rows=rows),
        grid=(count // step_rows,),
        in_specs=[pl.BlockSpec((step_rows, width), lambda step: (step, 0)), whole(table)],
        out_specs=[
            pl.BlockSpec((step_rows, lanes), lambda step: (step, 0)),
            pl.BlockSpec((step_rows, width), lambda step: (step, 0)),
            pl.BlockSpec((step_rows, LANES), lambda step: (step, 0)),
        ],
        out_shape=[
            jax.ShapeDtypeStruct((count, lanes), jnp.bfloat16),
            jax.ShapeDtypeStruct((count, width), jnp.float32),
            jax.ShapeDtypeStruct((count, LANES), jnp.float32),
        ],
        scratch_shapes=[pltpu.VMEM((step_rows, lanes), jnp.float32)],
    )(tokens, table)


def whole(array):
    return pl.BlockSpec(array.shape, lambda step: (0,) * len(array.shape))


def attend(prefix, arrays, places, width, causal):
    blocks, unused, rows = arrays[0].shape
    return pl.pallas_call(
        functools.partial(attend_kernel, places=places, causal=causal),
        grid=(blocks,),
        in_specs=[pl.BlockSpec(memory_space=pltpu.SMEM)] + [whole(array) for array in arrays],
        out_specs=pl.BlockSpec((1, width, rows), lambda step: (step, 0, 0)),
        out_shape=jax.ShapeDtypeStruct((blocks, width, rows), jnp.bfloat16),
    )(prefix, *arrays)


def attend_back(prefix, arrays, upstream, places, causal):
    blocks, width, rows = upstream.shape
    shape = jax.ShapeDtypeStruct((blocks, 3 * width, rows), jnp.bfloat16)
    return pl.pallas_call(
        functools.partial(
            attend_back_kernel,
            places=places,
            spots=(0, width, 2 * width),
            count=len(arrays),
            causal=causal,
        ),
        grid=(blocks,),
        in_specs=[pl.BlockSpec(memory_space=pltpu.SMEM)]
        + [whole(array) for array in arrays]
        + [pl.BlockSpec((1, width, rows), lambda step: (step, 0, 0))],
        out_specs=whole(shape),
        out_shape=shape,
        scratch_shapes=[pltpu.VMEM((blocks, width, rows), jnp.float32)] * 2,
    )(prefix, *arrays, upstream)


def per_device(
    hidden_in,
    encoder_in,
    prefix_len,
    exit_flags,
    target_ids,
    out_cotangent,
    self_gain,
    self_query,
    self_key,
    self_value,
    self_output,
    cross_gain,
    cross_query,
    cross_key,
    cross_value,
    cross_output,
    feed_gain,
    feed_gate,
    feed_up,
    feed_down,
    exit_gain,
    embedding,
):
    width = hidden_in.shape[2]
    n_seq = lax.axis_size("seq")
    n_dp = lax.axis_size(dp)
    own_rows, own = self_query.shape
    own_feed = feed_gate.shape[1]
    fold_rows = feed_down.shape[0]
    folds = -(-fold_rows // own_rows)
    vocab_rows = embedding.shape[0]
    vocab_lanes = -(-vocab_rows // LANES) * LANES
    low = jnp.bfloat16

    gains = jnp.stack([self_gain, cross_gain, feed_gain, exit_gain], axis=1)
    gains = jnp.pad(gains, ((0, 0), (0, GAIN_LANES - gains.shape[1])))
    near = fetch(
        [
            jnp.concatenate([self_query, self_key, self_value], axis=1),
            self_output,
            cross_query,
            jnp.concatenate([cross_key, cross_value], axis=1),
            cross_output,
        ],
        gains,
    )
    near_sizes = (3 * own, own, own, 2 * own, own)
    self_qkv, self_out, cross_q, cross_kv, cross_out, gain_columns = cut(
        near, tuple(n_seq * size for size in near_sizes) + (GAIN_LANES,)
    )
    folded = jnp.pad(feed_down, ((0, folds * own_rows - fold_rows), (0, 0)))
    feed = fetch(
        [feed_gate, feed_up]
        + [folded[fold * own_rows : (fold + 1) * own_rows] for fold in range(folds)],
        None,
    )
    feed_sizes = (own_feed, own_feed) + (own,) * folds
    gate_full, up_full, *downs = cut(feed, tuple(n_seq * size for size in feed_sizes))
    shard = jnp.pad(embedding.T, ((0, 0), (0, vocab_lanes - vocab_rows)))
    shards = [shard] + [shift(shard, by) for by in range(1, n_seq)]
    table = jnp.zeros((width, vocab_lanes), low)
    for by in range(n_seq):
        table = lax.dynamic_update_slice(table, shards[by], (spot(-by) * own, 0))

    marks = jnp.concatenate(
        [exit_flags, target_ids, jnp.broadcast_to(prefix_len[:, None], exit_flags.shape)], axis=0
    )
    marks = relocate(marks)
    prefix_len = marks[2, :1]
    marks = lax.all_gather(marks[:2], dp, axis=0)
    hidden = relocate(hidden_in.reshape(-1, width))
    states = relocate(encoder_in.reshape(-1, width))
    cotangent = relocate(out_cotangent.reshape(-1, width))
    gain_one, gain_two, gain_three, gain_exit = gain_columns[:, :4].astype(jnp.float32).T

    def blocks(rows):
        return rows.astype(low).reshape(n_seq, -1, rows.shape[1])

    def fold_up(rows):
        rows = rows.reshape(n_dp, fold_rows, -1)
        rows = jnp.pad(rows, ((0, 0), (0, folds * own_rows - fold_rows), (0, 0)))
        return [
            rows[:, fold * own_rows : (fold + 1) * own_rows].reshape(width, -1)
            for fold in range(folds)
        ]

    def unfold(parts):
        parts = [part.reshape(n_dp, own_rows, -1) for part in parts]
        rows = jnp.concatenate(parts, axis=1)[:, :fold_rows]
        return rows.reshape(n_dp * fold_rows, -1)

    residual_in = hidden.T.astype(jnp.float32)
    token_count = residual_in.shape[1]
    residual_in, states, marks = lax.optimization_barrier((residual_in, states.T, marks))
    residual_in, states = rows_first(residual_in), rows_first(states)
    cotangent = rows_first(cotangent.T)
    normed_one = norm_columns(residual_in, gain_one).astype(low)
    attended = swap(
        jnp.concatenate(
            [
                blocks(contract(self_qkv, normed_one, 0, 0)),
                blocks(contract(cross_kv, states, 0, 0)),
            ],
            axis=1,
        ),
        "part",
    )
    self_places = ((0, 0), (0, own), (0, 2 * own))
    mixture_one = swap(attend(prefix_len, [attended], self_places, own, True), "part")
    mixture_one = mixture_one.reshape(width, token_count)
    after_self = residual_in + contract(self_out, mixture_one, 0, 0)
    normed_two = norm_columns(after_self, gain_two).astype(low)
    q_two = swap(blocks(contract(cross_q, normed_two, 0, 0)), "part")
    cross_places = ((0, 0), (1, 3 * own), (1, 4 * own))
    mixture_two = swap(attend(prefix_len, [q_two, attended], cross_places, own, False), "part")
    mixture_two = mixture_two.reshape(width, token_count)
    after_cross = after_self + contract(cross_out, mixture_two, 0, 0)
    normed_three = norm_columns(after_cross, gain_three).astype(low)
    gate_pre = contract(gate_full, normed_three, 0, 0)
    up_pre = contract(up_full, normed_three, 0, 0)
    hidden_mid = gated_unit(gate_pre, up_pre).astype(low)
    hidden_folds = fold_up(hidden_mid)
    after_feed = after_cross
    for down, hidden in zip(downs, hidden_folds):
        after_feed = after_feed + contract(down, hidden, 0, 0)
    block_output = relocate(after_feed.T.astype(low)).reshape(hidden_in.shape)
    normed_exit = rows_first(norm_columns(after_feed, gain_exit).astype(low).T)
    normed_exit, table = lax.optimization_barrier((normed_exit, table))

    tokens = lax.all_gather(normed_exit, dp, axis=0, tiled=True)
    flag_rows = marks[:, 0].reshape(-1, 1).astype(jnp.float32)
    target_rows = marks[:, 1].reshape(-1, 1) - lax.axis_index(dp) * vocab_rows
    hits = jnp.arange(vocab_lanes)[None, :] == target_rows
    hits = hits & (target_rows < vocab_rows)
    target_terms = contract(hits.astype(low), table, 1, 1).astype(low)
    tokens, target_terms = lax.optimization_barrier((tokens, target_terms))
    shifted, products, parts = exit_rows(tokens, table, vocab_rows)
    picked = jnp.sum(tokens.astype(jnp.float32) * target_terms.astype(jnp.float32), axis=1)
    row_max = parts[:, 0]
    parts = lax.all_gather(jnp.stack([row_max, parts[:, 1], picked]), dp, axis=0)
    top = jnp.max(parts[:, 0], axis=0)
    log_total = top + jnp.log(jnp.sum(parts[:, 1] * jnp.exp(parts[:, 0] - top), axis=0))
    all_losses = flag_rows[:, 0] * (log_total - jnp.sum(parts[:, 2], axis=0))
    token_losses = lax.dynamic_slice(
        all_losses, (lax.axis_index(dp) * token_count,), (token_count,)
    )
    token_losses = relocate(token_losses.reshape(exit_flags.shape))
    factor = flag_rows * jnp.exp(row_max - log_total)[:, None]
    exit_in_grad = lax.psum_scatter(
        rows_first((factor * products - flag_rows * target_terms.astype(jnp.float32)).astype(low)),
        dp,
        scatter_dimension=0,
        tiled=True,
    )
    logit_grads = jnp.where(hits, factor * shifted - flag_rows, factor * shifted).astype(low)
    table_terms = contract(tokens, logit_grads, 0, 0).astype(low)
    exit_in_grad, table_terms, block_output, token_losses = lax.optimization_barrier(
        (rows_first(exit_in_grad), table_terms, block_output, token_losses)
    )
    exit_in_grad = rows_first(exit_in_grad.T).astype(jnp.float32)

    def table_block(by):
        return lax.dynamic_slice(table_terms, (spot(by) * own, 0), (own, vocab_lanes))

    table_parts = [shift(table_block(by), by) for by in range(1, n_seq)]
    table_sums = table_block(0).astype(jnp.float32)

    feed_grad, full_exit_gain = norm_back(after_feed, gain_exit, exit_in_grad)
    feed_grad = feed_grad + cotangent
    branch_three = feed_grad.astype(low)
    hidden_mid_grad = unfold([contract(down, branch_three, 1, 0) for down in downs])
    unused, gated_pull = jax.vjp(gated_unit, gate_pre, up_pre)
    gate_grad, up_grad = gated_pull(hidden_mid_grad)
    gate_grad, up_grad = gate_grad.astype(low), up_grad.astype(low)
    normed_three_grad = contract(gate_full, gate_grad, 1, 0) + contract(up_full, up_grad, 1, 0)
    cross_grad, full_feed_gain = norm_back(after_cross, gain_three, normed_three_grad)
    cross_grad = cross_grad + feed_grad
    branch_two = cross_grad.astype(low)
    mixture_two_grad = blocks(contract(cross_out, branch_two, 1, 0))
    feed_terms = jnp.concatenate(
        [
            contract(normed_three, gate_grad, 1, 1).astype(low),
            contract(normed_three, up_grad, 1, 1).astype(low),
        ]
        + [contract(hidden, branch_three, 1, 1).astype(low) for hidden in hidden_folds],
        axis=1,
    )
    mixture_two_grad, feed_terms = lax.optimization_barrier((mixture_two_grad, feed_terms))
    feed_terms = lax.psum_scatter(feed_terms, dp, scatter_dimension=0, tiled=True)
    cross_grads = attend_back(
        prefix_len, [q_two, attended], swap(mixture_two_grad, "part"), cross_places, False
    )
    cross_grads, table_parts[0] = lax.optimization_barrier((cross_grads, table_parts[0]))
    cross_grads = swap(cross_grads, "part")
    q_grad = cross_grads[:, :own].reshape(-1, token_count)
    kv_grad = cross_grads[:, own:].reshape(-1, token_count)
    encoder_grad = relocate(contract(kv_grad, cross_kv, 0, 1)).reshape(encoder_in.shape)
    cross_terms = jnp.concatenate(
        [
            contract(normed_two, q_grad, 1, 1).astype(low),
            contract(states, kv_grad, 1, 1).astype(low),
            contract(mixture_two, branch_two, 1, 1).astype(low),
        ],
        axis=1,
    )
    self_grad, full_cross_gain = norm_back(after_self, gain_two, contract(cross_q, q_grad, 1, 0))
    self_grad = self_grad + cross_grad
    branch_one = self_grad.astype(low)
    mixture_one_grad = blocks(contract(self_out, branch_one, 1, 0))
    mixture_one_grad, cross_terms, table_parts[1] = lax.optimization_barrier(
        (mixture_one_grad, cross_terms, table_parts[1])
    )
    qkv_grad = attend_back(
        prefix_len, [attended], swap(mixture_one_grad, "part"), self_places, True
    )
    qkv_grad, table_parts[2:], encoder_grad, feed_terms, cross_terms = lax.optimization_barrier(
        (qkv_grad, table_parts[2:], encoder_grad, feed_terms, cross_terms)
    )
    cross_terms = lax.psum_scatter(cross_terms, dp, scatter_dimension=0, tiled=True)
    qkv_grad = swap(qkv_grad, "part").reshape(-1, token_count)
    normed_one_grad = contract(self_qkv, qkv_grad, 1, 0)
    input_grad, full_self_gain = norm_back(residual_in, gain_one, normed_one_grad)
    hidden_grad = relocate((input_grad + self_grad).T).reshape(hidden_in.shape)
    gain_terms = jnp.stack(
        [full_self_gain, full_cross_gain, full_feed_gain, full_exit_gain], axis=1
    ).astype(low)
    gain_terms = jnp.pad(gain_terms, ((0, 0), (0, GAIN_LANES - gain_terms.shape[1])))
    self_terms = jnp.concatenate(
        [
            contract(normed_one, qkv_grad, 1, 1).astype(low),
            contract(mixture_one, branch_one, 1, 1).astype(low),
            gain_terms,
        ],
        axis=1,
    )
    self_terms, cross_terms = lax.optimization_barrier((self_terms, cross_terms))
    self_terms = lax.psum_scatter(self_terms, dp, scatter_dimension=0, tiled=True)
    for part in table_parts:
        table_sums = table_sums + part.astype(jnp.float32)
    embedding_grad = table_sums[:, :vocab_rows].T
    cross_query_grad, cross_key_grad, cross_value_grad, cross_output_grad = deliver(
        cross_terms, near_sizes[2:], 0, (own,) * 4
    )
    feed_gate_grad, feed_up_grad, *down_sums = deliver(feed_terms, feed_sizes, 0, feed_sizes)
    down_grad = jnp.concatenate(down_sums, axis=0)[:fold_rows]
    self_query_grad, self_key_grad, self_value_grad, self_output_grad, gain_sums = deliver(
        self_terms, near_sizes[:2], GAIN_LANES, (own,) * 4 + (GAIN_LANES,)
    )
    gain_sums = gain_sums[:, :4].T
    return (
        block_output,
        token_losses,
        hidden_grad,
        encoder_grad,
        gain_sums[0],
        self_query_grad,
        self_key_grad,
        self_value_grad,
        self_output_grad,
        gain_sums[1],
        cross_query_grad,
        cross_key_grad,
        cross_value_grad,
        cross_output_grad,
        gain_sums[2],
        feed_gate_grad,
        feed_up_grad,
        down_grad,
        gain_sums[3],
        embedding_grad,
    )


def solution(mesh):
    size = mesh.shape["seq"]
    planes = Mesh(mesh.devices.reshape(-1, size, size), dp + ("seq",))
    tokens = P(dp, "seq")
    rows = P(dp)
    matrix = P(dp, "seq")
    block = P(dp, "seq", None)
    attention = (rows,) + (matrix,) * 4
    return jax.shard_map(
        per_device,
        mesh=planes,
        in_specs=(block, block, rows, tokens, tokens, block)
        + attention * 2
        + (rows, matrix, matrix, matrix, rows, matrix),
        out_specs=(block, tokens, block, block)
        + attention * 2
        + (rows, matrix, matrix, matrix, rows, matrix),
        check_vma=False,
    )
```

```python
import functools

import jax
import jax.numpy as jnp
from jax import lax
from jax.experimental import pallas as pl
from jax.experimental.layout import Layout, with_layout_constraint
from jax.experimental.pallas import tpu as pltpu
from jax.sharding import Mesh
from jax.sharding import PartitionSpec as P

HD = 64
GAIN_LANES = 128
TOKEN_ROWS = 256
LANES = 128

norm_eps = 1e-06
masked_score = -1000000000.0
dp = ("group", "part")


def contract(first_op, second_op, first_dim, second_dim):
    return lax.dot_general(
        first_op,
        second_op,
        (((first_dim,), (second_dim,)), ((), ())),
        preferred_element_type=jnp.float32,
    )


def rows_first(array):
    return with_layout_constraint(array, Layout(major_to_minor=tuple(range(array.ndim))))


def norm_columns(inputs, scaling):
    return (
        inputs
        * lax.rsqrt(jnp.mean(inputs * inputs, axis=0, keepdims=True) + norm_eps)
        * scaling[:, None]
    )


def norm_back(inputs, scaling, upstream):
    unused, pullback = jax.vjp(norm_columns, inputs, scaling)
    return pullback(upstream)


def gated_unit(gate_in, upward):
    return jax.nn.gelu(gate_in, approximate=True) * upward


def swap(pieces, axis):
    return lax.all_to_all(pieces, axis, 0, 0, tiled=True)


def relocate(block):
    size = lax.axis_size("seq")
    pairs = [
        ((group * size + part) * size + at, (group * size + at) * size + part)
        for group in range(lax.axis_size("group"))
        for part in range(size)
        for at in range(size)
    ]
    return lax.ppermute(block, ("group", "part", "seq"), pairs)


def shift(block, by):
    size = lax.axis_size("seq")
    return lax.ppermute(block, "seq", [(at, (at + by) % size) for at in range(size)])


def spot(by):
    size = lax.axis_size("seq")
    at = lax.axis_index("seq") + by % size
    return jnp.where(at >= size, at - size, at)


def move_kernel(*refs, moves, count):
    for source, taken, target, put in moves:
        refs[count + target][put] = refs[source][taken]


def move(arrays, shapes, moves):
    return pl.pallas_call(
        functools.partial(move_kernel, moves=moves, count=len(arrays)),
        out_shape=[jax.ShapeDtypeStruct(shape, jnp.bfloat16) for shape in shapes],
    )(*arrays)


def sum_kernel(terms_ref, *refs, pieces):
    for ref, low, high in zip(refs, pieces[:-1], pieces[1:]):
        total = terms_ref[0, :, low:high].astype(jnp.float32)
        for block in range(1, terms_ref.shape[0]):
            total += terms_ref[block, :, low:high].astype(jnp.float32)
        ref[...] = total


def edges(sizes):
    return [sum(sizes[:at]) for at in range(len(sizes) + 1)]


every = slice(None)


def exchange(shards, after):
    n_seq = lax.axis_size("seq")
    rows = shards[0].shape[0]
    sizes = [shard.shape[1] for shard in shards]
    starts = edges(sizes)
    moves = [
        (at, (every, every), 0, (block, every, slice(starts[at], starts[at + 1])))
        for at in range(len(shards))
        for block in range(n_seq)
    ]
    (copies,) = move(shards, [(n_seq, rows, starts[-1])], moves)
    copies, after = lax.optimization_barrier((copies, after))
    return swap(copies, "seq"), after


def fetch(parts, sizes, extra):
    n_seq, rows, unused = parts.shape
    starts = edges(sizes)
    moves = [
        (
            0,
            (block, every, slice(starts[at], starts[at + 1])),
            0,
            (every, slice(low, low + sizes[at])),
        )
        for at in range(len(sizes))
        for block in range(n_seq)
        for low in [n_seq * starts[at] + block * sizes[at]]
    ]
    width = n_seq * starts[-1]
    if extra is not None:
        moves.append((1, (every, every), 0, (every, slice(width, width + extra.shape[1]))))
        width += extra.shape[1]
    (full,) = move([parts] if extra is None else [parts, extra], [(rows, width)], moves)
    return lax.all_gather(full, dp, axis=0, tiled=True)


def deliver(terms, sizes, extra, out_sizes):
    n_seq = lax.axis_size("seq")
    rows = terms.shape[0]
    starts = edges(sizes)
    moves = [
        (
            0,
            (every, slice(low, low + sizes[at])),
            0,
            (block, every, slice(starts[at], starts[at + 1])),
        )
        for at in range(len(sizes))
        for block in range(n_seq)
        for low in [n_seq * starts[at] + block * sizes[at]]
    ]
    width = starts[-1]
    if extra:
        low = n_seq * width
        moves += [
            (0, (every, slice(low, low + extra)), 0, (block, every, slice(width, width + extra)))
            for block in range(n_seq)
        ]
    (parts,) = move([terms], [(n_seq, rows, width + extra)], moves)
    return pl.pallas_call(
        functools.partial(sum_kernel, pieces=edges(out_sizes)),
        out_shape=[jax.ShapeDtypeStruct((rows, size), jnp.float32) for size in out_sizes],
    )(swap(parts, "seq"))


def cut(array, sizes):
    return jnp.split(array, edges(sizes)[1:-1], axis=1)


def head_rows(row, head):
    return slice(row + head * HD, row + (head + 1) * HD)


def score_columns(key_ref, key_row, queries, head, allowed):
    scores = jnp.concatenate(
        [
            contract(key_ref[block, head_rows(key_row, head), :], queries, 0, 0)
            for block in range(key_ref.shape[0])
        ],
        axis=0,
    )
    if allowed is not None:
        scores = jnp.where(allowed, scores, masked_score)
    exponent = jnp.exp(scores - jnp.max(scores, axis=0, keepdims=True))
    return exponent * (1.0 / jnp.sum(exponent, axis=0, keepdims=True))


def allowed_columns(prefix_ref, step, blocks, rows):
    key_pos = lax.broadcasted_iota(jnp.int32, (blocks * rows, rows), 0)
    query_pos = step * rows + lax.broadcasted_iota(jnp.int32, (blocks * rows, rows), 1)
    return (key_pos <= query_pos) | (key_pos < prefix_ref[0])


def attend_kernel(prefix_ref, *refs, places, causal):
    out_ref = refs[-1]
    step = pl.program_id(0)
    (q_at, q_row), (k_at, k_row), (v_at, v_row) = places
    blocks, unused, rows = refs[k_at].shape
    allowed = allowed_columns(prefix_ref, step, blocks, rows) if causal else None
    for head in range(out_ref.shape[1] // HD):
        queries = refs[q_at][step, head_rows(q_row, head), :]
        queries = queries * jnp.asarray(HD**-0.5, queries.dtype)
        shares = score_columns(refs[k_at], k_row, queries, head, allowed).astype(queries.dtype)
        total = jnp.zeros(queries.shape, jnp.float32)
        for block in range(blocks):
            values = refs[v_at][block, head_rows(v_row, head), :]
            total += contract(values, shares[block * rows : (block + 1) * rows], 1, 0)
        out_ref[0, head_rows(0, head), :] = total.astype(out_ref.dtype)


def attend_back_kernel(prefix_ref, *refs, places, spots, count, causal):
    upstream_ref = refs[count]
    out_ref, key_sum, value_sum = refs[count + 1 :]
    step = pl.program_id(0)
    (q_at, q_row), (k_at, k_row), (v_at, v_row) = places
    blocks, unused, rows = refs[k_at].shape
    allowed = allowed_columns(prefix_ref, step, blocks, rows) if causal else None

    @pl.when(step == 0)
    def _():
        key_sum[...] = jnp.zeros_like(key_sum)
        value_sum[...] = jnp.zeros_like(value_sum)

    for head in range(upstream_ref.shape[1] // HD):
        mine = head_rows(0, head)
        queries = refs[q_at][step, head_rows(q_row, head), :]
        queries = queries * jnp.asarray(HD**-0.5, queries.dtype)
        upstream = upstream_ref[0, mine, :]
        shares = score_columns(refs[k_at], k_row, queries, head, allowed)
        share_grads = jnp.concatenate(
            [
                contract(refs[v_at][block, head_rows(v_row, head), :], upstream, 0, 0)
                for block in range(blocks)
            ],
            axis=0,
        )
        centre = jnp.sum(shares * share_grads, axis=0, keepdims=True)
        score_grads = (shares * (share_grads - centre)).astype(queries.dtype)
        shares = shares.astype(queries.dtype)
        total = jnp.zeros(queries.shape, jnp.float32)
        for block in range(blocks):
            part = slice(block * rows, (block + 1) * rows)
            key_rows = refs[k_at][block, head_rows(k_row, head), :]
            total += contract(key_rows, score_grads[part], 1, 0)
            key_sum[block, mine, :] += contract(queries, score_grads[part], 1, 1)
            value_sum[block, mine, :] += contract(upstream, shares[part], 1, 1)
        out_ref[step, head_rows(spots[0], head), :] = (total * HD**-0.5).astype(out_ref.dtype)

    @pl.when(step == pl.num_programs(0) - 1)
    def _():
        width = key_sum.shape[1]
        out_ref[:, spots[1] : spots[1] + width, :] = key_sum[...].astype(out_ref.dtype)
        out_ref[:, spots[2] : spots[2] + width, :] = value_sum[...].astype(out_ref.dtype)


def exit_kernel(token_ref, table_ref, shifted_ref, product_ref, part_ref, logit_ref, *, rows):
    lanes = table_ref.shape[1]
    chunk = next(size for size in (1024, 512, 256, 128) if lanes % size == 0)
    tokens = token_ref[...]
    row_max = jnp.full((tokens.shape[0], 1), -jnp.inf, jnp.float32)
    for low in range(0, lanes, chunk):
        logits = contract(tokens, table_ref[:, low : low + chunk], 1, 0)
        if low + chunk > rows:
            lane = low + lax.broadcasted_iota(jnp.int32, (1, chunk), 1)
            logits = jnp.where(lane < rows, logits, -jnp.inf)
        logit_ref[:, low : low + chunk] = logits
        row_max = jnp.maximum(row_max, jnp.max(logits, axis=1, keepdims=True))
    row_sum = jnp.zeros_like(row_max)
    product = jnp.zeros(product_ref.shape, jnp.float32)
    for low in range(0, lanes, chunk):
        shifted = jnp.exp(logit_ref[:, low : low + chunk] - row_max)
        row_sum += jnp.sum(shifted, axis=1, keepdims=True)
        shifted = shifted.astype(shifted_ref.dtype)
        shifted_ref[:, low : low + chunk] = shifted
        product += contract(shifted, table_ref[:, low : low + chunk], 1, 1)
    product_ref[...] = product
    lane = lax.broadcasted_iota(jnp.int32, part_ref.shape, 1)
    part_ref[...] = jnp.where(lane == 0, row_max, row_sum)


def exit_rows(tokens, table, rows):
    count, width = tokens.shape
    lanes = table.shape[1]
    step_rows = min(TOKEN_ROWS, count)
    return pl.pallas_call(
        functools.partial(exit_kernel, rows=rows),
        grid=(count // step_rows,),
        in_specs=[pl.BlockSpec((step_rows, width), lambda step: (step, 0)), whole(table)],
        out_specs=[
            pl.BlockSpec((step_rows, lanes), lambda step: (step, 0)),
            pl.BlockSpec((step_rows, width), lambda step: (step, 0)),
            pl.BlockSpec((step_rows, LANES), lambda step: (step, 0)),
        ],
        out_shape=[
            jax.ShapeDtypeStruct((count, lanes), jnp.bfloat16),
            jax.ShapeDtypeStruct((count, width), jnp.float32),
            jax.ShapeDtypeStruct((count, LANES), jnp.float32),
        ],
        scratch_shapes=[pltpu.VMEM((step_rows, lanes), jnp.float32)],
    )(tokens, table)


def whole(array):
    return pl.BlockSpec(array.shape, lambda step: (0,) * len(array.shape))


def attend(prefix, arrays, places, width, causal):
    blocks, unused, rows = arrays[0].shape
    return pl.pallas_call(
        functools.partial(attend_kernel, places=places, causal=causal),
        grid=(blocks,),
        in_specs=[pl.BlockSpec(memory_space=pltpu.SMEM)] + [whole(array) for array in arrays],
        out_specs=pl.BlockSpec((1, width, rows), lambda step: (step, 0, 0)),
        out_shape=jax.ShapeDtypeStruct((blocks, width, rows), jnp.bfloat16),
    )(prefix, *arrays)


def attend_back(prefix, arrays, upstream, places, causal):
    blocks, width, rows = upstream.shape
    shape = jax.ShapeDtypeStruct((blocks, 3 * width, rows), jnp.bfloat16)
    return pl.pallas_call(
        functools.partial(
            attend_back_kernel,
            places=places,
            spots=(0, width, 2 * width),
            count=len(arrays),
            causal=causal,
        ),
        grid=(blocks,),
        in_specs=[pl.BlockSpec(memory_space=pltpu.SMEM)]
        + [whole(array) for array in arrays]
        + [pl.BlockSpec((1, width, rows), lambda step: (step, 0, 0))],
        out_specs=whole(shape),
        out_shape=shape,
        scratch_shapes=[pltpu.VMEM((blocks, width, rows), jnp.float32)] * 2,
    )(prefix, *arrays, upstream)


def per_device(
    hidden_in,
    encoder_in,
    prefix_len,
    exit_flags,
    target_ids,
    out_cotangent,
    self_gain,
    self_query,
    self_key,
    self_value,
    self_output,
    cross_gain,
    cross_query,
    cross_key,
    cross_value,
    cross_output,
    feed_gain,
    feed_gate,
    feed_up,
    feed_down,
    exit_gain,
    embedding,
):
    width = hidden_in.shape[2]
    n_seq = lax.axis_size("seq")
    n_dp = lax.axis_size(dp)
    own_rows, own = self_query.shape
    own_feed = feed_gate.shape[1]
    fold_rows = feed_down.shape[0]
    folds = -(-fold_rows // own_rows)
    vocab_rows = embedding.shape[0]
    vocab_lanes = -(-vocab_rows // LANES) * LANES
    low = jnp.bfloat16

    gains = jnp.stack([self_gain, cross_gain, feed_gain, exit_gain], axis=1)
    gains = jnp.pad(gains, ((0, 0), (0, GAIN_LANES - gains.shape[1])))
    near_parts, moved = exchange(
        [
            jnp.concatenate([self_query, self_key, self_value], axis=1),
            self_output,
            cross_query,
            jnp.concatenate([cross_key, cross_value], axis=1),
            cross_output,
        ],
        (),
    )
    near_sizes = (3 * own, own, own, 2 * own, own)

    marks = jnp.concatenate(
        [exit_flags, target_ids, jnp.broadcast_to(prefix_len[:, None], exit_flags.shape)], axis=0
    )
    near_parts, marks, hidden_in, encoder_in = lax.optimization_barrier(
        (near_parts, marks, hidden_in, encoder_in)
    )
    near = fetch(near_parts, near_sizes, gains)
    self_qkv, self_out, cross_q, cross_kv, cross_out, gain_columns = cut(
        near, tuple(n_seq * size for size in near_sizes) + (GAIN_LANES,)
    )
    moved = (
        relocate(marks),
        relocate(hidden_in.reshape(-1, width)),
        relocate(encoder_in.reshape(-1, width)),
    )
    folded = jnp.pad(feed_down, ((0, folds * own_rows - fold_rows), (0, 0)))
    feed_parts, (marks, hidden, states) = exchange(
        [feed_gate, feed_up]
        + [folded[fold * own_rows : (fold + 1) * own_rows] for fold in range(folds)],
        moved,
    )
    feed_sizes = (own_feed, own_feed) + (own,) * folds
    prefix_len = marks[2, :1]
    marks = lax.all_gather(marks[:2], dp, axis=0)
    shard = jnp.pad(embedding.T, ((0, 0), (0, vocab_lanes - vocab_rows)))
    feed_parts, shard, marks = lax.optimization_barrier((feed_parts, shard, marks))
    feed = fetch(feed_parts, feed_sizes, None)
    gate_full, up_full, *downs = cut(feed, tuple(n_seq * size for size in feed_sizes))
    shards = [shard]
    table = jnp.zeros((width, vocab_lanes), low)

    def next_shard(held):
        source, shards[-1] = lax.optimization_barrier((shard, shards[-1]))
        arrived, held = lax.optimization_barrier((shift(source, len(shards)), held))
        shards.append(arrived)
        return held

    cotangent = relocate(out_cotangent.reshape(-1, width))
    gain_one, gain_two, gain_three, gain_exit = gain_columns[:, :4].astype(jnp.float32).T

    def blocks(rows):
        return rows.astype(low).reshape(n_seq, -1, rows.shape[1])

    def fold_up(rows):
        rows = rows.reshape(n_dp, fold_rows, -1)
        rows = jnp.pad(rows, ((0, 0), (0, folds * own_rows - fold_rows), (0, 0)))
        return [
            rows[:, fold * own_rows : (fold + 1) * own_rows].reshape(width, -1)
            for fold in range(folds)
        ]

    def unfold(parts):
        parts = [part.reshape(n_dp, own_rows, -1) for part in parts]
        rows = jnp.concatenate(parts, axis=1)[:, :fold_rows]
        return rows.reshape(n_dp * fold_rows, -1)

    residual_in = hidden.T.astype(jnp.float32)
    token_count = residual_in.shape[1]
    residual_in, states, marks = lax.optimization_barrier((residual_in, states.T, marks))
    residual_in, states = rows_first(residual_in), rows_first(states)
    cotangent = rows_first(cotangent.T)
    normed_one = norm_columns(residual_in, gain_one).astype(low)
    attended = swap(
        jnp.concatenate(
            [
                blocks(contract(self_qkv, normed_one, 0, 0)),
                blocks(contract(cross_kv, states, 0, 0)),
            ],
            axis=1,
        ),
        "part",
    )
    self_places = ((0, 0), (0, own), (0, 2 * own))
    mixture_one = next_shard(attend(prefix_len, [attended], self_places, own, True))
    mixture_one = swap(mixture_one, "part")
    mixture_one = mixture_one.reshape(width, token_count)
    after_self = residual_in + contract(self_out, mixture_one, 0, 0)
    normed_two = norm_columns(after_self, gain_two).astype(low)
    q_two = swap(blocks(contract(cross_q, normed_two, 0, 0)), "part")
    cross_places = ((0, 0), (1, 3 * own), (1, 4 * own))
    mixture_two = next_shard(attend(prefix_len, [q_two, attended], cross_places, own, False))
    mixture_two = swap(mixture_two, "part")
    mixture_two = mixture_two.reshape(width, token_count)
    after_cross = after_self + contract(cross_out, mixture_two, 0, 0)
    normed_three = norm_columns(after_cross, gain_three).astype(low)
    gate_pre = contract(gate_full, normed_three, 0, 0)
    up_pre = contract(up_full, normed_three, 0, 0)
    hidden_mid = gated_unit(gate_pre, up_pre).astype(low)
    hidden_folds = fold_up(hidden_mid)
    after_feed = after_cross
    for down, hidden in zip(downs, hidden_folds):
        after_feed = after_feed + contract(down, hidden, 0, 0)
    block_output = relocate(after_feed.T.astype(low)).reshape(hidden_in.shape)
    normed_exit = rows_first(norm_columns(after_feed, gain_exit).astype(low).T)
    while len(shards) < n_seq:
        normed_exit = next_shard(normed_exit)
    for by in range(n_seq):
        table = lax.dynamic_update_slice(table, shards[by], (spot(-by) * own, 0))

    tokens = lax.all_gather(normed_exit, dp, axis=0, tiled=True)
    flag_rows = marks[:, 0].reshape(-1, 1).astype(jnp.float32)
    target_rows = marks[:, 1].reshape(-1, 1) - lax.axis_index(dp) * vocab_rows
    hits = jnp.arange(vocab_lanes)[None, :] == target_rows
    hits = hits & (target_rows < vocab_rows)
    target_terms = contract(hits.astype(low), table, 1, 1).astype(low)
    tokens, target_terms = lax.optimization_barrier((tokens, target_terms))
    shifted, products, parts = exit_rows(tokens, table, vocab_rows)
    picked = jnp.sum(tokens.astype(jnp.float32) * target_terms.astype(jnp.float32), axis=1)
    row_max = parts[:, 0]
    parts = lax.all_gather(jnp.stack([row_max, parts[:, 1], picked]), dp, axis=0)
    top = jnp.max(parts[:, 0], axis=0)
    log_total = top + jnp.log(jnp.sum(parts[:, 1] * jnp.exp(parts[:, 0] - top), axis=0))
    all_losses = flag_rows[:, 0] * (log_total - jnp.sum(parts[:, 2], axis=0))
    token_losses = lax.dynamic_slice(
        all_losses, (lax.axis_index(dp) * token_count,), (token_count,)
    )
    token_losses = relocate(token_losses.reshape(exit_flags.shape))
    factor = flag_rows * jnp.exp(row_max - log_total)[:, None]
    exit_in_grad = lax.psum_scatter(
        rows_first((factor * products - flag_rows * target_terms.astype(jnp.float32)).astype(low)),
        dp,
        scatter_dimension=0,
        tiled=True,
    )
    logit_grads = jnp.where(hits, factor * shifted - flag_rows, factor * shifted).astype(low)
    table_terms = contract(tokens, logit_grads, 0, 0).astype(low)
    exit_in_grad, unused, block_output, token_losses = lax.optimization_barrier(
        (rows_first(exit_in_grad), table_terms, block_output, token_losses)
    )
    exit_in_grad = rows_first(exit_in_grad.T).astype(jnp.float32)

    def table_block(by):
        return lax.dynamic_slice(table_terms, (spot(by) * own, 0), (own, vocab_lanes))

    table_parts = [table_block(0)]

    def next_part(held):
        by = len(table_parts)
        source, table_parts[-1] = lax.optimization_barrier((table_block(by), table_parts[-1]))
        arrived, held = lax.optimization_barrier((shift(source, by), held))
        table_parts.append(arrived)
        return held

    feed_grad, full_exit_gain = norm_back(after_feed, gain_exit, exit_in_grad)
    feed_grad = feed_grad + cotangent
    branch_three = feed_grad.astype(low)
    hidden_mid_grad = unfold([contract(down, branch_three, 1, 0) for down in downs])
    unused, gated_pull = jax.vjp(gated_unit, gate_pre, up_pre)
    gate_grad, up_grad = gated_pull(hidden_mid_grad)
    gate_grad, up_grad = gate_grad.astype(low), up_grad.astype(low)
    normed_three_grad = contract(gate_full, gate_grad, 1, 0) + contract(up_full, up_grad, 1, 0)
    cross_grad, full_feed_gain = norm_back(after_cross, gain_three, normed_three_grad)
    cross_grad = cross_grad + feed_grad
    branch_two = cross_grad.astype(low)
    mixture_two_grad = blocks(contract(cross_out, branch_two, 1, 0))
    feed_terms = jnp.concatenate(
        [
            contract(normed_three, gate_grad, 1, 1).astype(low),
            contract(normed_three, up_grad, 1, 1).astype(low),
        ]
        + [contract(hidden, branch_three, 1, 1).astype(low) for hidden in hidden_folds],
        axis=1,
    )
    mixture_two_grad, feed_terms = next_part((mixture_two_grad, feed_terms))
    feed_terms = lax.psum_scatter(feed_terms, dp, scatter_dimension=0, tiled=True)
    cross_grads = attend_back(
        prefix_len, [q_two, attended], swap(mixture_two_grad, "part"), cross_places, False
    )
    cross_grads = swap(next_part(cross_grads), "part")
    q_grad = cross_grads[:, :own].reshape(-1, token_count)
    kv_grad = cross_grads[:, own:].reshape(-1, token_count)
    encoder_grad = relocate(contract(kv_grad, cross_kv, 0, 1)).reshape(encoder_in.shape)
    cross_terms = jnp.concatenate(
        [
            contract(normed_two, q_grad, 1, 1).astype(low),
            contract(states, kv_grad, 1, 1).astype(low),
            contract(mixture_two, branch_two, 1, 1).astype(low),
        ],
        axis=1,
    )
    self_grad, full_cross_gain = norm_back(after_self, gain_two, contract(cross_q, q_grad, 1, 0))
    self_grad = self_grad + cross_grad
    branch_one = self_grad.astype(low)
    mixture_one_grad = blocks(contract(self_out, branch_one, 1, 0))
    mixture_one_grad, cross_terms = next_part((mixture_one_grad, cross_terms))
    qkv_grad = attend_back(
        prefix_len, [attended], swap(mixture_one_grad, "part"), self_places, True
    )
    qkv_grad, encoder_grad, feed_terms, cross_terms = lax.optimization_barrier(
        (qkv_grad, encoder_grad, feed_terms, cross_terms)
    )
    cross_terms = lax.psum_scatter(cross_terms, dp, scatter_dimension=0, tiled=True)
    qkv_grad = swap(qkv_grad, "part").reshape(-1, token_count)
    normed_one_grad = contract(self_qkv, qkv_grad, 1, 0)
    input_grad, full_self_gain = norm_back(residual_in, gain_one, normed_one_grad)
    hidden_grad = relocate((input_grad + self_grad).T).reshape(hidden_in.shape)
    gain_terms = jnp.stack(
        [full_self_gain, full_cross_gain, full_feed_gain, full_exit_gain], axis=1
    ).astype(low)
    gain_terms = jnp.pad(gain_terms, ((0, 0), (0, GAIN_LANES - gain_terms.shape[1])))
    self_terms = jnp.concatenate(
        [
            contract(normed_one, qkv_grad, 1, 1).astype(low),
            contract(mixture_one, branch_one, 1, 1).astype(low),
            gain_terms,
        ],
        axis=1,
    )
    self_terms, cross_terms = lax.optimization_barrier((self_terms, cross_terms))
    while len(table_parts) < n_seq:
        self_terms = next_part(self_terms)
    self_terms = lax.psum_scatter(self_terms, dp, scatter_dimension=0, tiled=True)
    table_sums = sum(part.astype(jnp.float32) for part in table_parts)
    embedding_grad = table_sums[:, :vocab_rows].T
    cross_query_grad, cross_key_grad, cross_value_grad, cross_output_grad = deliver(
        cross_terms, near_sizes[2:], 0, (own,) * 4
    )
    feed_gate_grad, feed_up_grad, *down_sums = deliver(feed_terms, feed_sizes, 0, feed_sizes)
    down_grad = jnp.concatenate(down_sums, axis=0)[:fold_rows]
    self_query_grad, self_key_grad, self_value_grad, self_output_grad, gain_sums = deliver(
        self_terms, near_sizes[:2], GAIN_LANES, (own,) * 4 + (GAIN_LANES,)
    )
    gain_sums = gain_sums[:, :4].T
    return (
        block_output,
        token_losses,
        hidden_grad,
        encoder_grad,
        gain_sums[0],
        self_query_grad,
        self_key_grad,
        self_value_grad,
        self_output_grad,
        gain_sums[1],
        cross_query_grad,
        cross_key_grad,
        cross_value_grad,
        cross_output_grad,
        gain_sums[2],
        feed_gate_grad,
        feed_up_grad,
        down_grad,
        gain_sums[3],
        embedding_grad,
    )


def solution(mesh):
    size = mesh.shape["seq"]
    planes = Mesh(mesh.devices.reshape(-1, size, size), dp + ("seq",))
    tokens = P(dp, "seq")
    rows = P(dp)
    matrix = P(dp, "seq")
    block = P(dp, "seq", None)
    attention = (rows,) + (matrix,) * 4
    return jax.shard_map(
        per_device,
        mesh=planes,
        in_specs=(block, block, rows, tokens, tokens, block)
        + attention * 2
        + (rows, matrix, matrix, matrix, rows, matrix),
        out_specs=(block, tokens, block, block)
        + attention * 2
        + (rows, matrix, matrix, matrix, rows, matrix),
        check_vma=False,
    )
```

```python
import functools

import jax
import jax.numpy as jnp
from jax import lax
from jax.experimental import pallas as pl
from jax.experimental.layout import Layout, with_layout_constraint
from jax.experimental.pallas import tpu as pltpu
from jax.sharding import Mesh
from jax.sharding import PartitionSpec as P

HD = 64
GAIN_LANES = 128
TOKEN_ROWS = 256
LANES = 128

norm_eps = 1e-06
masked_score = -1000000000.0
dp = ("group", "part")


def contract(first_op, second_op, first_dim, second_dim):
    return lax.dot_general(
        first_op,
        second_op,
        (((first_dim,), (second_dim,)), ((), ())),
        preferred_element_type=jnp.float32,
    )


def rows_first(array):
    return with_layout_constraint(array, Layout(major_to_minor=tuple(range(array.ndim))))


def norm_columns(inputs, scaling):
    return (
        inputs
        * lax.rsqrt(jnp.mean(inputs * inputs, axis=0, keepdims=True) + norm_eps)
        * scaling[:, None]
    )


def norm_back(inputs, scaling, upstream):
    unused, pullback = jax.vjp(norm_columns, inputs, scaling)
    return pullback(upstream)


def gated_unit(gate_in, upward):
    return jax.nn.gelu(gate_in, approximate=True) * upward


def swap(pieces, axis):
    return lax.all_to_all(pieces, axis, 0, 0, tiled=True)


def relocate(block):
    size = lax.axis_size("seq")
    pairs = [
        ((group * size + part) * size + at, (group * size + at) * size + part)
        for group in range(lax.axis_size("group"))
        for part in range(size)
        for at in range(size)
    ]
    return lax.ppermute(block, ("group", "part", "seq"), pairs)


def move_kernel(*refs, moves, count):
    for source, taken, target, put in moves:
        refs[count + target][put] = refs[source][taken]


def move(arrays, shapes, moves):
    return pl.pallas_call(
        functools.partial(move_kernel, moves=moves, count=len(arrays)),
        out_shape=[jax.ShapeDtypeStruct(shape, jnp.bfloat16) for shape in shapes],
    )(*arrays)


def sum_kernel(terms_ref, *refs, pieces):
    for ref, low, high in zip(refs, pieces[:-1], pieces[1:]):
        total = terms_ref[0, :, low:high].astype(jnp.float32)
        for block in range(1, terms_ref.shape[0]):
            total += terms_ref[block, :, low:high].astype(jnp.float32)
        ref[...] = total


def edges(sizes):
    return [sum(sizes[:at]) for at in range(len(sizes) + 1)]


every = slice(None)


def exchange(shards, after):
    n_seq = lax.axis_size("seq")
    rows = shards[0].shape[0]
    sizes = [shard.shape[1] for shard in shards]
    starts = edges(sizes)
    moves = [
        (at, (every, every), 0, (block, every, slice(starts[at], starts[at + 1])))
        for at in range(len(shards))
        for block in range(n_seq)
    ]
    (copies,) = move(shards, [(n_seq, rows, starts[-1])], moves)
    copies, after = lax.optimization_barrier((copies, after))
    return swap(copies, "seq"), after


def fetch(parts, sizes, extra):
    n_seq, rows, unused = parts.shape
    starts = edges(sizes)
    moves = [
        (
            0,
            (block, every, slice(starts[at], starts[at + 1])),
            0,
            (every, slice(low, low + sizes[at])),
        )
        for at in range(len(sizes))
        for block in range(n_seq)
        for low in [n_seq * starts[at] + block * sizes[at]]
    ]
    width = n_seq * starts[-1]
    if extra is not None:
        moves.append((1, (every, every), 0, (every, slice(width, width + extra.shape[1]))))
        width += extra.shape[1]
    (full,) = move([parts] if extra is None else [parts, extra], [(rows, width)], moves)
    return lax.all_gather(full, dp, axis=0, tiled=True)


def deliver(terms, sizes, extra, out_sizes):
    n_seq = lax.axis_size("seq")
    rows = terms.shape[0]
    starts = edges(sizes)
    moves = [
        (
            0,
            (every, slice(low, low + sizes[at])),
            0,
            (block, every, slice(starts[at], starts[at + 1])),
        )
        for at in range(len(sizes))
        for block in range(n_seq)
        for low in [n_seq * starts[at] + block * sizes[at]]
    ]
    width = starts[-1]
    if extra:
        low = n_seq * width
        moves += [
            (0, (every, slice(low, low + extra)), 0, (block, every, slice(width, width + extra)))
            for block in range(n_seq)
        ]
    (parts,) = move([terms], [(n_seq, rows, width + extra)], moves)
    return pl.pallas_call(
        functools.partial(sum_kernel, pieces=edges(out_sizes)),
        out_shape=[jax.ShapeDtypeStruct((rows, size), jnp.float32) for size in out_sizes],
    )(swap(parts, "seq"))


def cut(array, sizes):
    return jnp.split(array, edges(sizes)[1:-1], axis=1)


def head_rows(row, head):
    return slice(row + head * HD, row + (head + 1) * HD)


def score_columns(key_ref, key_row, queries, head, allowed):
    scores = jnp.concatenate(
        [
            contract(key_ref[block, head_rows(key_row, head), :], queries, 0, 0)
            for block in range(key_ref.shape[0])
        ],
        axis=0,
    )
    if allowed is not None:
        scores = jnp.where(allowed, scores, masked_score)
    exponent = jnp.exp(scores - jnp.max(scores, axis=0, keepdims=True))
    return exponent * (1.0 / jnp.sum(exponent, axis=0, keepdims=True))


def allowed_columns(prefix_ref, step, blocks, rows):
    key_pos = lax.broadcasted_iota(jnp.int32, (blocks * rows, rows), 0)
    query_pos = step * rows + lax.broadcasted_iota(jnp.int32, (blocks * rows, rows), 1)
    return (key_pos <= query_pos) | (key_pos < prefix_ref[0])


def attend_kernel(prefix_ref, *refs, places, causal):
    out_ref = refs[-1]
    step = pl.program_id(0)
    (q_at, q_row), (k_at, k_row), (v_at, v_row) = places
    blocks, unused, rows = refs[k_at].shape
    allowed = allowed_columns(prefix_ref, step, blocks, rows) if causal else None
    for head in range(out_ref.shape[1] // HD):
        queries = refs[q_at][step, head_rows(q_row, head), :]
        queries = queries * jnp.asarray(HD**-0.5, queries.dtype)
        shares = score_columns(refs[k_at], k_row, queries, head, allowed).astype(queries.dtype)
        total = jnp.zeros(queries.shape, jnp.float32)
        for block in range(blocks):
            values = refs[v_at][block, head_rows(v_row, head), :]
            total += contract(values, shares[block * rows : (block + 1) * rows], 1, 0)
        out_ref[0, head_rows(0, head), :] = total.astype(out_ref.dtype)


def attend_back_kernel(prefix_ref, *refs, places, spots, count, causal):
    upstream_ref = refs[count]
    out_ref, key_sum, value_sum = refs[count + 1 :]
    step = pl.program_id(0)
    (q_at, q_row), (k_at, k_row), (v_at, v_row) = places
    blocks, unused, rows = refs[k_at].shape
    allowed = allowed_columns(prefix_ref, step, blocks, rows) if causal else None

    @pl.when(step == 0)
    def _():
        key_sum[...] = jnp.zeros_like(key_sum)
        value_sum[...] = jnp.zeros_like(value_sum)

    for head in range(upstream_ref.shape[1] // HD):
        mine = head_rows(0, head)
        queries = refs[q_at][step, head_rows(q_row, head), :]
        queries = queries * jnp.asarray(HD**-0.5, queries.dtype)
        upstream = upstream_ref[0, mine, :]
        shares = score_columns(refs[k_at], k_row, queries, head, allowed)
        share_grads = jnp.concatenate(
            [
                contract(refs[v_at][block, head_rows(v_row, head), :], upstream, 0, 0)
                for block in range(blocks)
            ],
            axis=0,
        )
        centre = jnp.sum(shares * share_grads, axis=0, keepdims=True)
        score_grads = (shares * (share_grads - centre)).astype(queries.dtype)
        shares = shares.astype(queries.dtype)
        total = jnp.zeros(queries.shape, jnp.float32)
        for block in range(blocks):
            part = slice(block * rows, (block + 1) * rows)
            key_rows = refs[k_at][block, head_rows(k_row, head), :]
            total += contract(key_rows, score_grads[part], 1, 0)
            key_sum[block, mine, :] += contract(queries, score_grads[part], 1, 1)
            value_sum[block, mine, :] += contract(upstream, shares[part], 1, 1)
        out_ref[step, head_rows(spots[0], head), :] = (total * HD**-0.5).astype(out_ref.dtype)

    @pl.when(step == pl.num_programs(0) - 1)
    def _():
        width = key_sum.shape[1]
        out_ref[:, spots[1] : spots[1] + width, :] = key_sum[...].astype(out_ref.dtype)
        out_ref[:, spots[2] : spots[2] + width, :] = value_sum[...].astype(out_ref.dtype)


def exit_kernel(token_ref, table_ref, shifted_ref, product_ref, part_ref, logit_ref, *, rows):
    lanes = table_ref.shape[1]
    chunk = next(size for size in (1024, 512, 256, 128) if lanes % size == 0)
    tokens = token_ref[...]
    row_max = jnp.full((tokens.shape[0], 1), -jnp.inf, jnp.float32)
    for low in range(0, lanes, chunk):
        logits = contract(tokens, table_ref[:, low : low + chunk], 1, 0)
        if low + chunk > rows:
            lane = low + lax.broadcasted_iota(jnp.int32, (1, chunk), 1)
            logits = jnp.where(lane < rows, logits, -jnp.inf)
        logit_ref[:, low : low + chunk] = logits
        row_max = jnp.maximum(row_max, jnp.max(logits, axis=1, keepdims=True))
    row_sum = jnp.zeros_like(row_max)
    product = jnp.zeros(product_ref.shape, jnp.float32)
    for low in range(0, lanes, chunk):
        shifted = jnp.exp(logit_ref[:, low : low + chunk] - row_max)
        row_sum += jnp.sum(shifted, axis=1, keepdims=True)
        shifted = shifted.astype(shifted_ref.dtype)
        shifted_ref[:, low : low + chunk] = shifted
        product += contract(shifted, table_ref[:, low : low + chunk], 1, 1)
    product_ref[...] = product
    lane = lax.broadcasted_iota(jnp.int32, part_ref.shape, 1)
    part_ref[...] = jnp.where(lane == 0, row_max, row_sum)


def exit_rows(tokens, table, rows):
    count, width = tokens.shape
    lanes = table.shape[1]
    step_rows = min(TOKEN_ROWS, count)
    return pl.pallas_call(
        functools.partial(exit_kernel, rows=rows),
        grid=(count // step_rows,),
        in_specs=[pl.BlockSpec((step_rows, width), lambda step: (step, 0)), whole(table)],
        out_specs=[
            pl.BlockSpec((step_rows, lanes), lambda step: (step, 0)),
            pl.BlockSpec((step_rows, width), lambda step: (step, 0)),
            pl.BlockSpec((step_rows, LANES), lambda step: (step, 0)),
        ],
        out_shape=[
            jax.ShapeDtypeStruct((count, lanes), jnp.bfloat16),
            jax.ShapeDtypeStruct((count, width), jnp.float32),
            jax.ShapeDtypeStruct((count, LANES), jnp.float32),
        ],
        scratch_shapes=[pltpu.VMEM((step_rows, lanes), jnp.float32)],
    )(tokens, table)


def whole(array):
    return pl.BlockSpec(array.shape, lambda step: (0,) * len(array.shape))


def attend(prefix, arrays, places, width, causal):
    blocks, unused, rows = arrays[0].shape
    return pl.pallas_call(
        functools.partial(attend_kernel, places=places, causal=causal),
        grid=(blocks,),
        in_specs=[pl.BlockSpec(memory_space=pltpu.SMEM)] + [whole(array) for array in arrays],
        out_specs=pl.BlockSpec((1, width, rows), lambda step: (step, 0, 0)),
        out_shape=jax.ShapeDtypeStruct((blocks, width, rows), jnp.bfloat16),
    )(prefix, *arrays)


def attend_back(prefix, arrays, upstream, places, causal):
    blocks, width, rows = upstream.shape
    shape = jax.ShapeDtypeStruct((blocks, 3 * width, rows), jnp.bfloat16)
    return pl.pallas_call(
        functools.partial(
            attend_back_kernel,
            places=places,
            spots=(0, width, 2 * width),
            count=len(arrays),
            causal=causal,
        ),
        grid=(blocks,),
        in_specs=[pl.BlockSpec(memory_space=pltpu.SMEM)]
        + [whole(array) for array in arrays]
        + [pl.BlockSpec((1, width, rows), lambda step: (step, 0, 0))],
        out_specs=whole(shape),
        out_shape=shape,
        scratch_shapes=[pltpu.VMEM((blocks, width, rows), jnp.float32)] * 2,
    )(prefix, *arrays, upstream)


def per_device(
    hidden_in,
    encoder_in,
    prefix_len,
    exit_flags,
    target_ids,
    out_cotangent,
    self_gain,
    self_query,
    self_key,
    self_value,
    self_output,
    cross_gain,
    cross_query,
    cross_key,
    cross_value,
    cross_output,
    feed_gain,
    feed_gate,
    feed_up,
    feed_down,
    exit_gain,
    embedding,
):
    width = hidden_in.shape[2]
    n_seq = lax.axis_size("seq")
    n_dp = lax.axis_size(dp)
    own_rows, own = self_query.shape
    own_feed = feed_gate.shape[1]
    fold_rows = feed_down.shape[0]
    folds = -(-fold_rows // own_rows)
    vocab_rows = embedding.shape[0]
    vocab_lanes = -(-vocab_rows // LANES) * LANES
    low = jnp.bfloat16

    gains = jnp.stack([self_gain, cross_gain, feed_gain, exit_gain], axis=1)
    gains = jnp.pad(gains, ((0, 0), (0, GAIN_LANES - gains.shape[1])))
    near_parts, moved = exchange(
        [
            jnp.concatenate([self_query, self_key, self_value], axis=1),
            self_output,
            cross_query,
            jnp.concatenate([cross_key, cross_value], axis=1),
            cross_output,
        ],
        (),
    )
    near_sizes = (3 * own, own, own, 2 * own, own)

    marks = jnp.concatenate(
        [exit_flags, target_ids, jnp.broadcast_to(prefix_len[:, None], exit_flags.shape)], axis=0
    )
    near_parts, marks, hidden_in, encoder_in = lax.optimization_barrier(
        (near_parts, marks, hidden_in, encoder_in)
    )
    near = fetch(near_parts, near_sizes, gains)
    self_qkv, self_out, cross_q, cross_kv, cross_out, gain_columns = cut(
        near, tuple(n_seq * size for size in near_sizes) + (GAIN_LANES,)
    )
    moved = (
        relocate(marks),
        relocate(hidden_in.reshape(-1, width)),
        relocate(encoder_in.reshape(-1, width)),
    )
    folded = jnp.pad(feed_down, ((0, folds * own_rows - fold_rows), (0, 0)))
    feed_parts, (marks, hidden, states) = exchange(
        [feed_gate, feed_up]
        + [folded[fold * own_rows : (fold + 1) * own_rows] for fold in range(folds)],
        moved,
    )
    feed_sizes = (own_feed, own_feed) + (own,) * folds
    prefix_len = marks[2, :1]
    marks = lax.all_gather(marks[:2], dp, axis=0)
    shard = jnp.pad(embedding.T, ((0, 0), (0, vocab_lanes - vocab_rows)))
    feed_parts, shard, marks = lax.optimization_barrier((feed_parts, shard, marks))
    feed = fetch(feed_parts, feed_sizes, None)
    gate_full, up_full, *downs = cut(feed, tuple(n_seq * size for size in feed_sizes))
    table = lax.all_gather(shard, "seq", axis=0, tiled=True)
    cotangent = relocate(out_cotangent.reshape(-1, width))
    gain_one, gain_two, gain_three, gain_exit = gain_columns[:, :4].astype(jnp.float32).T

    def blocks(rows):
        return rows.astype(low).reshape(n_seq, -1, rows.shape[1])

    def fold_up(rows):
        rows = rows.reshape(n_dp, fold_rows, -1)
        rows = jnp.pad(rows, ((0, 0), (0, folds * own_rows - fold_rows), (0, 0)))
        return [
            rows[:, fold * own_rows : (fold + 1) * own_rows].reshape(width, -1)
            for fold in range(folds)
        ]

    def unfold(parts):
        parts = [part.reshape(n_dp, own_rows, -1) for part in parts]
        rows = jnp.concatenate(parts, axis=1)[:, :fold_rows]
        return rows.reshape(n_dp * fold_rows, -1)

    residual_in = hidden.T.astype(jnp.float32)
    token_count = residual_in.shape[1]
    residual_in, states, marks = lax.optimization_barrier((residual_in, states.T, marks))
    residual_in, states = rows_first(residual_in), rows_first(states)
    cotangent = rows_first(cotangent.T)
    normed_one = norm_columns(residual_in, gain_one).astype(low)
    attended = swap(
        jnp.concatenate(
            [
                blocks(contract(self_qkv, normed_one, 0, 0)),
                blocks(contract(cross_kv, states, 0, 0)),
            ],
            axis=1,
        ),
        "part",
    )
    self_places = ((0, 0), (0, own), (0, 2 * own))
    mixture_one = swap(attend(prefix_len, [attended], self_places, own, True), "part")
    mixture_one = mixture_one.reshape(width, token_count)
    after_self = residual_in + contract(self_out, mixture_one, 0, 0)
    normed_two = norm_columns(after_self, gain_two).astype(low)
    q_two = swap(blocks(contract(cross_q, normed_two, 0, 0)), "part")
    cross_places = ((0, 0), (1, 3 * own), (1, 4 * own))
    mixture_two = swap(attend(prefix_len, [q_two, attended], cross_places, own, False), "part")
    mixture_two = mixture_two.reshape(width, token_count)
    after_cross = after_self + contract(cross_out, mixture_two, 0, 0)
    normed_three = norm_columns(after_cross, gain_three).astype(low)
    gate_pre = contract(gate_full, normed_three, 0, 0)
    up_pre = contract(up_full, normed_three, 0, 0)
    hidden_mid = gated_unit(gate_pre, up_pre).astype(low)
    hidden_folds = fold_up(hidden_mid)
    after_feed = after_cross
    for down, hidden in zip(downs, hidden_folds):
        after_feed = after_feed + contract(down, hidden, 0, 0)
    block_output = relocate(after_feed.T.astype(low)).reshape(hidden_in.shape)
    normed_exit = rows_first(norm_columns(after_feed, gain_exit).astype(low).T)
    normed_exit, table, cotangent = lax.optimization_barrier((normed_exit, table, cotangent))

    tokens = lax.all_gather(normed_exit, dp, axis=0, tiled=True)
    flag_rows = marks[:, 0].reshape(-1, 1).astype(jnp.float32)
    target_rows = marks[:, 1].reshape(-1, 1) - lax.axis_index(dp) * vocab_rows
    hits = jnp.arange(vocab_lanes)[None, :] == target_rows
    hits = hits & (target_rows < vocab_rows)
    target_terms = contract(hits.astype(low), table, 1, 1).astype(low)
    tokens, target_terms = lax.optimization_barrier((tokens, target_terms))
    shifted, products, parts = exit_rows(tokens, table, vocab_rows)
    picked = jnp.sum(tokens.astype(jnp.float32) * target_terms.astype(jnp.float32), axis=1)
    row_max = parts[:, 0]
    parts = lax.all_gather(jnp.stack([row_max, parts[:, 1], picked]), dp, axis=0)
    top = jnp.max(parts[:, 0], axis=0)
    log_total = top + jnp.log(jnp.sum(parts[:, 1] * jnp.exp(parts[:, 0] - top), axis=0))
    all_losses = flag_rows[:, 0] * (log_total - jnp.sum(parts[:, 2], axis=0))
    token_losses = lax.dynamic_slice(
        all_losses, (lax.axis_index(dp) * token_count,), (token_count,)
    )
    token_losses = relocate(token_losses.reshape(exit_flags.shape))
    factor = flag_rows * jnp.exp(row_max - log_total)[:, None]
    exit_in_grad = lax.psum_scatter(
        rows_first((factor * products - flag_rows * target_terms.astype(jnp.float32)).astype(low)),
        dp,
        scatter_dimension=0,
        tiled=True,
    )
    logit_grads = jnp.where(hits, factor * shifted - flag_rows, factor * shifted).astype(low)
    table_terms = contract(tokens, logit_grads, 0, 0).astype(low)
    exit_in_grad, table_terms, block_output, token_losses = lax.optimization_barrier(
        (rows_first(exit_in_grad), table_terms, block_output, token_losses)
    )
    exit_in_grad = rows_first(exit_in_grad.T).astype(jnp.float32)
    table_sums = lax.psum_scatter(table_terms, "seq", scatter_dimension=0, tiled=True)

    feed_grad, full_exit_gain = norm_back(after_feed, gain_exit, exit_in_grad)
    feed_grad = feed_grad + cotangent
    branch_three = feed_grad.astype(low)
    hidden_mid_grad = unfold([contract(down, branch_three, 1, 0) for down in downs])
    unused, gated_pull = jax.vjp(gated_unit, gate_pre, up_pre)
    gate_grad, up_grad = gated_pull(hidden_mid_grad)
    gate_grad, up_grad = gate_grad.astype(low), up_grad.astype(low)
    normed_three_grad = contract(gate_full, gate_grad, 1, 0) + contract(up_full, up_grad, 1, 0)
    cross_grad, full_feed_gain = norm_back(after_cross, gain_three, normed_three_grad)
    cross_grad = cross_grad + feed_grad
    branch_two = cross_grad.astype(low)
    mixture_two_grad = blocks(contract(cross_out, branch_two, 1, 0))
    cross_grads = attend_back(
        prefix_len, [q_two, attended], swap(mixture_two_grad, "part"), cross_places, False
    )
    cross_grads = swap(cross_grads, "part")
    q_grad = cross_grads[:, :own].reshape(-1, token_count)
    kv_grad = cross_grads[:, own:].reshape(-1, token_count)
    encoder_grad = relocate(contract(kv_grad, cross_kv, 0, 1)).reshape(encoder_in.shape)
    rest_terms = jnp.concatenate(
        [
            contract(normed_two, q_grad, 1, 1).astype(low),
            contract(states, kv_grad, 1, 1).astype(low),
            contract(mixture_two, branch_two, 1, 1).astype(low),
            contract(normed_three, gate_grad, 1, 1).astype(low),
            contract(normed_three, up_grad, 1, 1).astype(low),
        ]
        + [contract(hidden, branch_three, 1, 1).astype(low) for hidden in hidden_folds],
        axis=1,
    )
    self_grad, full_cross_gain = norm_back(after_self, gain_two, contract(cross_q, q_grad, 1, 0))
    self_grad = self_grad + cross_grad
    branch_one = self_grad.astype(low)
    mixture_one_grad = blocks(contract(self_out, branch_one, 1, 0))
    mixture_one_grad, rest_terms = lax.optimization_barrier((mixture_one_grad, rest_terms))
    rest_terms, table_sums = lax.optimization_barrier((rest_terms, table_sums))
    rest_terms = lax.psum_scatter(rest_terms, dp, scatter_dimension=0, tiled=True)
    qkv_grad = attend_back(
        prefix_len, [attended], swap(mixture_one_grad, "part"), self_places, True
    )
    qkv_grad, encoder_grad = lax.optimization_barrier((qkv_grad, encoder_grad))
    qkv_grad = swap(qkv_grad, "part").reshape(-1, token_count)
    normed_one_grad = contract(self_qkv, qkv_grad, 1, 0)
    input_grad, full_self_gain = norm_back(residual_in, gain_one, normed_one_grad)
    hidden_grad = relocate((input_grad + self_grad).T).reshape(hidden_in.shape)
    gain_terms = jnp.stack(
        [full_self_gain, full_cross_gain, full_feed_gain, full_exit_gain], axis=1
    ).astype(low)
    gain_terms = jnp.pad(gain_terms, ((0, 0), (0, GAIN_LANES - gain_terms.shape[1])))
    self_terms = jnp.concatenate(
        [
            contract(normed_one, qkv_grad, 1, 1).astype(low),
            contract(mixture_one, branch_one, 1, 1).astype(low),
            gain_terms,
        ],
        axis=1,
    )
    self_terms, rest_terms = lax.optimization_barrier((self_terms, rest_terms))
    self_terms = lax.psum_scatter(self_terms, dp, scatter_dimension=0, tiled=True)
    embedding_grad = table_sums[:, :vocab_rows].astype(jnp.float32).T
    (
        cross_query_grad,
        cross_key_grad,
        cross_value_grad,
        cross_output_grad,
        feed_gate_grad,
        feed_up_grad,
        *down_sums,
    ) = deliver(rest_terms, near_sizes[2:] + feed_sizes, 0, (own,) * 4 + feed_sizes)
    down_grad = jnp.concatenate(down_sums, axis=0)[:fold_rows]
    self_query_grad, self_key_grad, self_value_grad, self_output_grad, gain_sums = deliver(
        self_terms, near_sizes[:2], GAIN_LANES, (own,) * 4 + (GAIN_LANES,)
    )
    gain_sums = gain_sums[:, :4].T
    return (
        block_output,
        token_losses,
        hidden_grad,
        encoder_grad,
        gain_sums[0],
        self_query_grad,
        self_key_grad,
        self_value_grad,
        self_output_grad,
        gain_sums[1],
        cross_query_grad,
        cross_key_grad,
        cross_value_grad,
        cross_output_grad,
        gain_sums[2],
        feed_gate_grad,
        feed_up_grad,
        down_grad,
        gain_sums[3],
        embedding_grad,
    )


def solution(mesh):
    size = mesh.shape["seq"]
    planes = Mesh(mesh.devices.reshape(-1, size, size), dp + ("seq",))
    tokens = P(dp, "seq")
    rows = P(dp)
    matrix = P(dp, "seq")
    block = P(dp, "seq", None)
    attention = (rows,) + (matrix,) * 4
    return jax.shard_map(
        per_device,
        mesh=planes,
        in_specs=(block, block, rows, tokens, tokens, block)
        + attention * 2
        + (rows, matrix, matrix, matrix, rows, matrix),
        out_specs=(block, tokens, block, block)
        + attention * 2
        + (rows, matrix, matrix, matrix, rows, matrix),
        check_vma=False,
    )
```

```python
import functools

import jax
import jax.numpy as jnp
from jax import lax
from jax.experimental import pallas as pl
from jax.experimental.layout import Layout, with_layout_constraint
from jax.experimental.pallas import tpu as pltpu
from jax.sharding import Mesh
from jax.sharding import PartitionSpec as P

HD = 64
GAIN_LANES = 128
TOKEN_ROWS = 256
LANES = 128

norm_eps = 1e-06
masked_score = -1000000000.0
dp = ("group", "part")


def contract(first_op, second_op, first_dim, second_dim):
    return lax.dot_general(
        first_op,
        second_op,
        (((first_dim,), (second_dim,)), ((), ())),
        preferred_element_type=jnp.float32,
    )


def rows_first(array):
    return with_layout_constraint(array, Layout(major_to_minor=tuple(range(array.ndim))))


def norm_columns(inputs, scaling):
    return (
        inputs
        * lax.rsqrt(jnp.mean(inputs * inputs, axis=0, keepdims=True) + norm_eps)
        * scaling[:, None]
    )


def norm_back(inputs, scaling, upstream):
    unused, pullback = jax.vjp(norm_columns, inputs, scaling)
    return pullback(upstream)


def gated_unit(gate_in, upward):
    return jax.nn.gelu(gate_in, approximate=True) * upward


def swap(pieces, axis):
    return lax.all_to_all(pieces, axis, 0, 0, tiled=True)


def relocate(block):
    size = lax.axis_size("seq")
    pairs = [
        ((group * size + part) * size + at, (group * size + at) * size + part)
        for group in range(lax.axis_size("group"))
        for part in range(size)
        for at in range(size)
    ]
    return lax.ppermute(block, ("group", "part", "seq"), pairs)


def move_kernel(*refs, moves, count):
    for source, taken, target, put in moves:
        refs[count + target][put] = refs[source][taken]


def move(arrays, shapes, moves):
    return pl.pallas_call(
        functools.partial(move_kernel, moves=moves, count=len(arrays)),
        out_shape=[jax.ShapeDtypeStruct(shape, jnp.bfloat16) for shape in shapes],
    )(*arrays)


def sum_kernel(terms_ref, *refs, pieces):
    for ref, low, high in zip(refs, pieces[:-1], pieces[1:]):
        total = terms_ref[0, :, low:high].astype(jnp.float32)
        for block in range(1, terms_ref.shape[0]):
            total += terms_ref[block, :, low:high].astype(jnp.float32)
        ref[...] = total


def edges(sizes):
    return [sum(sizes[:at]) for at in range(len(sizes) + 1)]


every = slice(None)


def exchange(shards):
    n_seq = lax.axis_size("seq")
    rows = shards[0].shape[0]
    sizes = [shard.shape[1] for shard in shards]
    starts = edges(sizes)
    moves = [
        (at, (every, every), 0, (block, every, slice(starts[at], starts[at + 1])))
        for at in range(len(shards))
        for block in range(n_seq)
    ]
    (copies,) = move(shards, [(n_seq, rows, starts[-1])], moves)
    return swap(copies, "seq")


def fetch(parts, sizes, extra):
    n_seq, rows, unused = parts.shape
    starts = edges(sizes)
    moves = [
        (
            0,
            (block, every, slice(starts[at], starts[at + 1])),
            0,
            (every, slice(low, low + sizes[at])),
        )
        for at in range(len(sizes))
        for block in range(n_seq)
        for low in [n_seq * starts[at] + block * sizes[at]]
    ]
    width = n_seq * starts[-1]
    if extra is not None:
        moves.append((1, (every, every), 0, (every, slice(width, width + extra.shape[1]))))
        width += extra.shape[1]
    (full,) = move([parts] if extra is None else [parts, extra], [(rows, width)], moves)
    return lax.all_gather(full, dp, axis=0, tiled=True)


def deliver(terms, sizes, extra, out_sizes):
    n_seq = lax.axis_size("seq")
    rows = terms.shape[0]
    starts = edges(sizes)
    moves = [
        (
            0,
            (every, slice(low, low + sizes[at])),
            0,
            (block, every, slice(starts[at], starts[at + 1])),
        )
        for at in range(len(sizes))
        for block in range(n_seq)
        for low in [n_seq * starts[at] + block * sizes[at]]
    ]
    width = starts[-1]
    if extra:
        low = n_seq * width
        moves += [
            (0, (every, slice(low, low + extra)), 0, (block, every, slice(width, width + extra)))
            for block in range(n_seq)
        ]
    (parts,) = move([terms], [(n_seq, rows, width + extra)], moves)
    return pl.pallas_call(
        functools.partial(sum_kernel, pieces=edges(out_sizes)),
        out_shape=[jax.ShapeDtypeStruct((rows, size), jnp.float32) for size in out_sizes],
    )(swap(parts, "seq"))


def cut(array, sizes):
    return jnp.split(array, edges(sizes)[1:-1], axis=1)


def head_rows(row, head):
    return slice(row + head * HD, row + (head + 1) * HD)


def score_columns(key_ref, key_row, queries, head, allowed):
    scores = jnp.concatenate(
        [
            contract(key_ref[block, head_rows(key_row, head), :], queries, 0, 0)
            for block in range(key_ref.shape[0])
        ],
        axis=0,
    )
    if allowed is not None:
        scores = jnp.where(allowed, scores, masked_score)
    exponent = jnp.exp(scores - jnp.max(scores, axis=0, keepdims=True))
    return exponent * (1.0 / jnp.sum(exponent, axis=0, keepdims=True))


def allowed_columns(prefix_ref, step, blocks, rows):
    key_pos = lax.broadcasted_iota(jnp.int32, (blocks * rows, rows), 0)
    query_pos = step * rows + lax.broadcasted_iota(jnp.int32, (blocks * rows, rows), 1)
    return (key_pos <= query_pos) | (key_pos < prefix_ref[0])


def attend_kernel(prefix_ref, *refs, places, causal):
    out_ref = refs[-1]
    step = pl.program_id(0)
    (q_at, q_row), (k_at, k_row), (v_at, v_row) = places
    blocks, unused, rows = refs[k_at].shape
    allowed = allowed_columns(prefix_ref, step, blocks, rows) if causal else None
    for head in range(out_ref.shape[1] // HD):
        queries = refs[q_at][step, head_rows(q_row, head), :]
        queries = queries * jnp.asarray(HD**-0.5, queries.dtype)
        shares = score_columns(refs[k_at], k_row, queries, head, allowed).astype(queries.dtype)
        total = jnp.zeros(queries.shape, jnp.float32)
        for block in range(blocks):
            values = refs[v_at][block, head_rows(v_row, head), :]
            total += contract(values, shares[block * rows : (block + 1) * rows], 1, 0)
        out_ref[0, head_rows(0, head), :] = total.astype(out_ref.dtype)


def attend_back_kernel(prefix_ref, *refs, places, spots, count, causal):
    upstream_ref = refs[count]
    out_ref, key_sum, value_sum = refs[count + 1 :]
    step = pl.program_id(0)
    (q_at, q_row), (k_at, k_row), (v_at, v_row) = places
    blocks, unused, rows = refs[k_at].shape
    allowed = allowed_columns(prefix_ref, step, blocks, rows) if causal else None

    @pl.when(step == 0)
    def _():
        key_sum[...] = jnp.zeros_like(key_sum)
        value_sum[...] = jnp.zeros_like(value_sum)

    for head in range(upstream_ref.shape[1] // HD):
        mine = head_rows(0, head)
        queries = refs[q_at][step, head_rows(q_row, head), :]
        queries = queries * jnp.asarray(HD**-0.5, queries.dtype)
        upstream = upstream_ref[0, mine, :]
        shares = score_columns(refs[k_at], k_row, queries, head, allowed)
        share_grads = jnp.concatenate(
            [
                contract(refs[v_at][block, head_rows(v_row, head), :], upstream, 0, 0)
                for block in range(blocks)
            ],
            axis=0,
        )
        centre = jnp.sum(shares * share_grads, axis=0, keepdims=True)
        score_grads = (shares * (share_grads - centre)).astype(queries.dtype)
        shares = shares.astype(queries.dtype)
        total = jnp.zeros(queries.shape, jnp.float32)
        for block in range(blocks):
            part = slice(block * rows, (block + 1) * rows)
            key_rows = refs[k_at][block, head_rows(k_row, head), :]
            total += contract(key_rows, score_grads[part], 1, 0)
            key_sum[block, mine, :] += contract(queries, score_grads[part], 1, 1)
            value_sum[block, mine, :] += contract(upstream, shares[part], 1, 1)
        out_ref[step, head_rows(spots[0], head), :] = (total * HD**-0.5).astype(out_ref.dtype)

    @pl.when(step == pl.num_programs(0) - 1)
    def _():
        width = key_sum.shape[1]
        out_ref[:, spots[1] : spots[1] + width, :] = key_sum[...].astype(out_ref.dtype)
        out_ref[:, spots[2] : spots[2] + width, :] = value_sum[...].astype(out_ref.dtype)


def exit_kernel(token_ref, table_ref, shifted_ref, product_ref, part_ref, logit_ref, *, rows):
    lanes = table_ref.shape[1]
    chunk = next(size for size in (1024, 512, 256, 128) if lanes % size == 0)
    tokens = token_ref[...]
    row_max = jnp.full((tokens.shape[0], 1), -jnp.inf, jnp.float32)
    for low in range(0, lanes, chunk):
        logits = contract(tokens, table_ref[:, low : low + chunk], 1, 0)
        if low + chunk > rows:
            lane = low + lax.broadcasted_iota(jnp.int32, (1, chunk), 1)
            logits = jnp.where(lane < rows, logits, -jnp.inf)
        logit_ref[:, low : low + chunk] = logits
        row_max = jnp.maximum(row_max, jnp.max(logits, axis=1, keepdims=True))
    row_sum = jnp.zeros_like(row_max)
    product = jnp.zeros(product_ref.shape, jnp.float32)
    for low in range(0, lanes, chunk):
        shifted = jnp.exp(logit_ref[:, low : low + chunk] - row_max)
        row_sum += jnp.sum(shifted, axis=1, keepdims=True)
        shifted = shifted.astype(shifted_ref.dtype)
        shifted_ref[:, low : low + chunk] = shifted
        product += contract(shifted, table_ref[:, low : low + chunk], 1, 1)
    product_ref[...] = product
    lane = lax.broadcasted_iota(jnp.int32, part_ref.shape, 1)
    part_ref[...] = jnp.where(lane == 0, row_max, row_sum)


def exit_rows(tokens, table, rows):
    count, width = tokens.shape
    lanes = table.shape[1]
    step_rows = min(TOKEN_ROWS, count)
    return pl.pallas_call(
        functools.partial(exit_kernel, rows=rows),
        grid=(count // step_rows,),
        in_specs=[pl.BlockSpec((step_rows, width), lambda step: (step, 0)), whole(table)],
        out_specs=[
            pl.BlockSpec((step_rows, lanes), lambda step: (step, 0)),
            pl.BlockSpec((step_rows, width), lambda step: (step, 0)),
            pl.BlockSpec((step_rows, LANES), lambda step: (step, 0)),
        ],
        out_shape=[
            jax.ShapeDtypeStruct((count, lanes), jnp.bfloat16),
            jax.ShapeDtypeStruct((count, width), jnp.float32),
            jax.ShapeDtypeStruct((count, LANES), jnp.float32),
        ],
        scratch_shapes=[pltpu.VMEM((step_rows, lanes), jnp.float32)],
    )(tokens, table)


def whole(array):
    return pl.BlockSpec(array.shape, lambda step: (0,) * len(array.shape))


def attend(prefix, arrays, places, width, causal):
    blocks, unused, rows = arrays[0].shape
    return pl.pallas_call(
        functools.partial(attend_kernel, places=places, causal=causal),
        grid=(blocks,),
        in_specs=[pl.BlockSpec(memory_space=pltpu.SMEM)] + [whole(array) for array in arrays],
        out_specs=pl.BlockSpec((1, width, rows), lambda step: (step, 0, 0)),
        out_shape=jax.ShapeDtypeStruct((blocks, width, rows), jnp.bfloat16),
    )(prefix, *arrays)


def attend_back(prefix, arrays, upstream, places, causal):
    blocks, width, rows = upstream.shape
    shape = jax.ShapeDtypeStruct((blocks, 3 * width, rows), jnp.bfloat16)
    return pl.pallas_call(
        functools.partial(
            attend_back_kernel,
            places=places,
            spots=(0, width, 2 * width),
            count=len(arrays),
            causal=causal,
        ),
        grid=(blocks,),
        in_specs=[pl.BlockSpec(memory_space=pltpu.SMEM)]
        + [whole(array) for array in arrays]
        + [pl.BlockSpec((1, width, rows), lambda step: (step, 0, 0))],
        out_specs=whole(shape),
        out_shape=shape,
        scratch_shapes=[pltpu.VMEM((blocks, width, rows), jnp.float32)] * 2,
    )(prefix, *arrays, upstream)


def per_device(
    hidden_in,
    encoder_in,
    prefix_len,
    exit_flags,
    target_ids,
    out_cotangent,
    self_gain,
    self_query,
    self_key,
    self_value,
    self_output,
    cross_gain,
    cross_query,
    cross_key,
    cross_value,
    cross_output,
    feed_gain,
    feed_gate,
    feed_up,
    feed_down,
    exit_gain,
    embedding,
):
    width = hidden_in.shape[2]
    n_seq = lax.axis_size("seq")
    n_dp = lax.axis_size(dp)
    own_rows, own = self_query.shape
    own_feed = feed_gate.shape[1]
    fold_rows = feed_down.shape[0]
    folds = -(-fold_rows // own_rows)
    vocab_rows = embedding.shape[0]
    vocab_lanes = -(-vocab_rows // LANES) * LANES
    low = jnp.bfloat16

    gains = jnp.stack([self_gain, cross_gain, feed_gain, exit_gain], axis=1)
    gains = jnp.pad(gains, ((0, 0), (0, GAIN_LANES - gains.shape[1])))
    folded = jnp.pad(feed_down, ((0, folds * own_rows - fold_rows), (0, 0)))
    parts = exchange(
        [
            jnp.concatenate([self_query, self_key, self_value], axis=1),
            self_output,
            cross_query,
            jnp.concatenate([cross_key, cross_value], axis=1),
            cross_output,
            feed_gate,
            feed_up,
        ]
        + [folded[fold * own_rows : (fold + 1) * own_rows] for fold in range(folds)]
    )
    self_sizes = (3 * own, own)
    rest_sizes = (own, 2 * own, own, own_feed, own_feed) + (own,) * folds

    marks = jnp.concatenate(
        [exit_flags, target_ids, jnp.broadcast_to(prefix_len[:, None], exit_flags.shape)], axis=0
    )
    parts, marks, hidden, states, cotangent = lax.optimization_barrier(
        (parts, marks, hidden_in, encoder_in, out_cotangent.astype(low))
    )
    weights = fetch(parts, self_sizes + rest_sizes, gains)
    self_qkv, self_out, cross_q, cross_kv, cross_out, gate_full, up_full, *downs = cut(
        weights, tuple(n_seq * size for size in self_sizes + rest_sizes) + (GAIN_LANES,)
    )
    gain_columns = downs.pop()
    hidden = relocate(hidden.reshape(-1, width))
    states = relocate(states.reshape(-1, width))
    marks = relocate(marks)
    prefix_len = marks[2, :1]
    marks = lax.all_gather(marks[:2], dp, axis=0)
    shard = jnp.pad(embedding.T, ((0, 0), (0, vocab_lanes - vocab_rows)))
    shard, marks, hidden, states = lax.optimization_barrier((shard, marks, hidden, states))
    table = lax.all_gather(shard, "seq", axis=0, tiled=True)
    cotangent = relocate(cotangent.reshape(-1, width))
    gain_one, gain_two, gain_three, gain_exit = gain_columns[:, :4].astype(jnp.float32).T

    def blocks(rows):
        return rows.astype(low).reshape(n_seq, -1, rows.shape[1])

    def fold_up(rows):
        rows = rows.reshape(n_dp, fold_rows, -1)
        rows = jnp.pad(rows, ((0, 0), (0, folds * own_rows - fold_rows), (0, 0)))
        return [
            rows[:, fold * own_rows : (fold + 1) * own_rows].reshape(width, -1)
            for fold in range(folds)
        ]

    def unfold(parts):
        parts = [part.reshape(n_dp, own_rows, -1) for part in parts]
        rows = jnp.concatenate(parts, axis=1)[:, :fold_rows]
        return rows.reshape(n_dp * fold_rows, -1)

    residual_in = hidden.T.astype(jnp.float32)
    token_count = residual_in.shape[1]
    residual_in, states, cotangent = lax.optimization_barrier((residual_in, states.T, cotangent.T))
    residual_in, states = rows_first(residual_in), rows_first(states)
    cotangent = rows_first(cotangent)
    normed_one = norm_columns(residual_in, gain_one).astype(low)
    attended = swap(
        jnp.concatenate(
            [
                blocks(contract(self_qkv, normed_one, 0, 0)),
                blocks(contract(cross_kv, states, 0, 0)),
            ],
            axis=1,
        ),
        "part",
    )
    self_places = ((0, 0), (0, own), (0, 2 * own))
    mixture_one = swap(attend(prefix_len, [attended], self_places, own, True), "part")
    mixture_one = mixture_one.reshape(width, token_count)
    after_self = residual_in + contract(self_out, mixture_one, 0, 0)
    normed_two = norm_columns(after_self, gain_two).astype(low)
    q_two = swap(blocks(contract(cross_q, normed_two, 0, 0)), "part")
    cross_places = ((0, 0), (1, 3 * own), (1, 4 * own))
    mixture_two = swap(attend(prefix_len, [q_two, attended], cross_places, own, False), "part")
    mixture_two = mixture_two.reshape(width, token_count)
    after_cross = after_self + contract(cross_out, mixture_two, 0, 0)
    normed_three = norm_columns(after_cross, gain_three).astype(low)
    gate_pre = contract(gate_full, normed_three, 0, 0)
    up_pre = contract(up_full, normed_three, 0, 0)
    hidden_mid = gated_unit(gate_pre, up_pre).astype(low)
    hidden_folds = fold_up(hidden_mid)
    after_feed = after_cross
    for down, hidden in zip(downs, hidden_folds):
        after_feed = after_feed + contract(down, hidden, 0, 0)
    block_output = relocate(after_feed.T.astype(low)).reshape(hidden_in.shape)
    normed_exit = rows_first(norm_columns(after_feed, gain_exit).astype(low).T)
    normed_exit, table = lax.optimization_barrier((normed_exit, table))

    tokens = lax.all_gather(normed_exit, dp, axis=0, tiled=True)
    flag_rows = marks[:, 0].reshape(-1, 1).astype(jnp.float32)
    target_rows = marks[:, 1].reshape(-1, 1) - lax.axis_index(dp) * vocab_rows
    hits = jnp.arange(vocab_lanes)[None, :] == target_rows
    hits = hits & (target_rows < vocab_rows)
    target_terms = contract(hits.astype(low), table, 1, 1).astype(low)
    tokens, target_terms = lax.optimization_barrier((tokens, target_terms))
    shifted, products, parts = exit_rows(tokens, table, vocab_rows)
    picked = jnp.sum(tokens.astype(jnp.float32) * target_terms.astype(jnp.float32), axis=1)
    row_max = parts[:, 0]
    parts = lax.all_gather(jnp.stack([row_max, parts[:, 1], picked]), dp, axis=0)
    top = jnp.max(parts[:, 0], axis=0)
    log_total = top + jnp.log(jnp.sum(parts[:, 1] * jnp.exp(parts[:, 0] - top), axis=0))
    all_losses = flag_rows[:, 0] * (log_total - jnp.sum(parts[:, 2], axis=0))
    token_losses = lax.dynamic_slice(
        all_losses, (lax.axis_index(dp) * token_count,), (token_count,)
    )
    token_losses = relocate(token_losses.reshape(exit_flags.shape))
    factor = flag_rows * jnp.exp(row_max - log_total)[:, None]
    exit_in_grad = lax.psum_scatter(
        rows_first((factor * products - flag_rows * target_terms.astype(jnp.float32)).astype(low)),
        dp,
        scatter_dimension=0,
        tiled=True,
    )
    logit_grads = jnp.where(hits, factor * shifted - flag_rows, factor * shifted).astype(low)
    table_terms = contract(tokens, logit_grads, 0, 0).astype(low)
    exit_in_grad, table_terms, block_output, token_losses = lax.optimization_barrier(
        (rows_first(exit_in_grad), table_terms, block_output, token_losses)
    )
    exit_in_grad = rows_first(exit_in_grad.T).astype(jnp.float32)
    table_sums = lax.psum_scatter(table_terms, "seq", scatter_dimension=0, tiled=True)

    feed_grad, full_exit_gain = norm_back(after_feed, gain_exit, exit_in_grad)
    feed_grad = feed_grad + cotangent
    branch_three = feed_grad.astype(low)
    hidden_mid_grad = unfold([contract(down, branch_three, 1, 0) for down in downs])
    unused, gated_pull = jax.vjp(gated_unit, gate_pre, up_pre)
    gate_grad, up_grad = gated_pull(hidden_mid_grad)
    gate_grad, up_grad = gate_grad.astype(low), up_grad.astype(low)
    normed_three_grad = contract(gate_full, gate_grad, 1, 0) + contract(up_full, up_grad, 1, 0)
    cross_grad, full_feed_gain = norm_back(after_cross, gain_three, normed_three_grad)
    cross_grad = cross_grad + feed_grad
    branch_two = cross_grad.astype(low)
    mixture_two_grad = blocks(contract(cross_out, branch_two, 1, 0))
    cross_grads = attend_back(
        prefix_len, [q_two, attended], swap(mixture_two_grad, "part"), cross_places, False
    )
    cross_grads = swap(cross_grads, "part")
    q_grad = cross_grads[:, :own].reshape(-1, token_count)
    kv_grad = cross_grads[:, own:].reshape(-1, token_count)
    encoder_grad = relocate(contract(kv_grad, cross_kv, 0, 1).astype(low)).astype(jnp.float32)
    rest_terms = jnp.concatenate(
        [
            contract(normed_two, q_grad, 1, 1).astype(low),
            contract(states, kv_grad, 1, 1).astype(low),
            contract(mixture_two, branch_two, 1, 1).astype(low),
            contract(normed_three, gate_grad, 1, 1).astype(low),
            contract(normed_three, up_grad, 1, 1).astype(low),
        ]
        + [contract(hidden, branch_three, 1, 1).astype(low) for hidden in hidden_folds],
        axis=1,
    )
    self_grad, full_cross_gain = norm_back(after_self, gain_two, contract(cross_q, q_grad, 1, 0))
    self_grad = self_grad + cross_grad
    branch_one = self_grad.astype(low)
    mixture_one_grad = blocks(contract(self_out, branch_one, 1, 0))
    mixture_one_grad, rest_terms = lax.optimization_barrier((mixture_one_grad, rest_terms))
    rest_terms, table_sums = lax.optimization_barrier((rest_terms, table_sums))
    rest_terms = lax.psum_scatter(rest_terms, dp, scatter_dimension=0, tiled=True)
    qkv_grad = attend_back(
        prefix_len, [attended], swap(mixture_one_grad, "part"), self_places, True
    )
    qkv_grad, encoder_grad = lax.optimization_barrier((qkv_grad, encoder_grad))
    qkv_grad = swap(qkv_grad, "part").reshape(-1, token_count)
    normed_one_grad = contract(self_qkv, qkv_grad, 1, 0)
    input_grad, full_self_gain = norm_back(residual_in, gain_one, normed_one_grad)
    hidden_grad = relocate((input_grad + self_grad).T.astype(low)).astype(jnp.float32)
    gain_terms = jnp.stack(
        [full_self_gain, full_cross_gain, full_feed_gain, full_exit_gain], axis=1
    ).astype(low)
    gain_terms = jnp.pad(gain_terms, ((0, 0), (0, GAIN_LANES - gain_terms.shape[1])))
    self_terms = jnp.concatenate(
        [
            contract(normed_one, qkv_grad, 1, 1).astype(low),
            contract(mixture_one, branch_one, 1, 1).astype(low),
            gain_terms,
        ],
        axis=1,
    )
    self_terms, rest_terms = lax.optimization_barrier((self_terms, rest_terms))
    self_terms = lax.psum_scatter(self_terms, dp, scatter_dimension=0, tiled=True)
    embedding_grad = table_sums[:, :vocab_rows].astype(jnp.float32).T
    (
        cross_query_grad,
        cross_key_grad,
        cross_value_grad,
        cross_output_grad,
        feed_gate_grad,
        feed_up_grad,
        *down_sums,
    ) = deliver(rest_terms, rest_sizes, 0, (own,) * 4 + rest_sizes[3:])
    down_grad = jnp.concatenate(down_sums, axis=0)[:fold_rows]
    self_query_grad, self_key_grad, self_value_grad, self_output_grad, gain_sums = deliver(
        self_terms, self_sizes, GAIN_LANES, (own,) * 4 + (GAIN_LANES,)
    )
    gain_sums = gain_sums[:, :4].T
    return (
        block_output,
        token_losses,
        hidden_grad.reshape(hidden_in.shape),
        encoder_grad.reshape(encoder_in.shape),
        gain_sums[0],
        self_query_grad,
        self_key_grad,
        self_value_grad,
        self_output_grad,
        gain_sums[1],
        cross_query_grad,
        cross_key_grad,
        cross_value_grad,
        cross_output_grad,
        gain_sums[2],
        feed_gate_grad,
        feed_up_grad,
        down_grad,
        gain_sums[3],
        embedding_grad,
    )


def solution(mesh):
    size = mesh.shape["seq"]
    planes = Mesh(mesh.devices.reshape(-1, size, size), dp + ("seq",))
    tokens = P(dp, "seq")
    rows = P(dp)
    matrix = P(dp, "seq")
    block = P(dp, "seq", None)
    attention = (rows,) + (matrix,) * 4
    return jax.shard_map(
        per_device,
        mesh=planes,
        in_specs=(block, block, rows, tokens, tokens, block)
        + attention * 2
        + (rows, matrix, matrix, matrix, rows, matrix),
        out_specs=(block, tokens, block, block)
        + attention * 2
        + (rows, matrix, matrix, matrix, rows, matrix),
        check_vma=False,
    )
```

```python
import functools

import jax
import jax.numpy as jnp
from jax import lax
from jax.experimental import pallas as pl
from jax.experimental.layout import Layout, with_layout_constraint
from jax.experimental.pallas import tpu as pltpu
from jax.sharding import Mesh
from jax.sharding import PartitionSpec as P

HD = 64
GAIN_LANES = 128
TOKEN_ROWS = 256
LANES = 128

norm_eps = 1e-06
masked_score = -1000000000.0
dp = ("group", "part")


def contract(first_op, second_op, first_dim, second_dim):
    return lax.dot_general(
        first_op,
        second_op,
        (((first_dim,), (second_dim,)), ((), ())),
        preferred_element_type=jnp.float32,
    )


def rows_first(array):
    return with_layout_constraint(array, Layout(major_to_minor=tuple(range(array.ndim))))


def norm_columns(inputs, scaling):
    return (
        inputs
        * lax.rsqrt(jnp.mean(inputs * inputs, axis=0, keepdims=True) + norm_eps)
        * scaling[:, None]
    )


def norm_back(inputs, scaling, upstream):
    unused, pullback = jax.vjp(norm_columns, inputs, scaling)
    return pullback(upstream)


def gated_unit(gate_in, upward):
    return jax.nn.gelu(gate_in, approximate=True) * upward


def swap(pieces, axis):
    return lax.all_to_all(pieces, axis, 0, 0, tiled=True)


def relocate(block):
    size = lax.axis_size("seq")
    pairs = [
        ((group * size + part) * size + at, (group * size + at) * size + part)
        for group in range(lax.axis_size("group"))
        for part in range(size)
        for at in range(size)
    ]
    return lax.ppermute(block, ("group", "part", "seq"), pairs)


def move_kernel(*refs, moves, count):
    for source, taken, target, put in moves:
        refs[count + target][put] = refs[source][taken]


def move(arrays, shapes, moves):
    return pl.pallas_call(
        functools.partial(move_kernel, moves=moves, count=len(arrays)),
        out_shape=[jax.ShapeDtypeStruct(shape, jnp.bfloat16) for shape in shapes],
    )(*arrays)


def sum_kernel(terms_ref, *refs, pieces):
    for ref, low, high in zip(refs, pieces[:-1], pieces[1:]):
        total = terms_ref[0, :, low:high].astype(jnp.float32)
        for block in range(1, terms_ref.shape[0]):
            total += terms_ref[block, :, low:high].astype(jnp.float32)
        ref[...] = total


def edges(sizes):
    return [sum(sizes[:at]) for at in range(len(sizes) + 1)]


every = slice(None)


def gather_kernel(full_ref, *refs, pieces):
    for ref, (start, size, copies) in zip(refs, pieces):
        for block in range(copies):
            ref[:, block * size : (block + 1) * size] = full_ref[block, :, start : start + size]


def matrices(full, lanes, pieces):
    n_seq, rows, unused = full.shape
    return pl.pallas_call(
        functools.partial(gather_kernel, pieces=pieces),
        grid=(rows // LANES,),
        in_specs=[pl.BlockSpec((n_seq, LANES, lanes), lambda step: (0, step, 0))],
        out_specs=[
            pl.BlockSpec((LANES, size * copies), lambda step: (step, 0))
            for start, size, copies in pieces
        ],
        out_shape=[
            jax.ShapeDtypeStruct((rows, size * copies), jnp.bfloat16)
            for start, size, copies in pieces
        ],
    )(full)


def deliver(terms, sizes, extra, out_sizes):
    n_seq = lax.axis_size("seq")
    rows = terms.shape[0]
    starts = edges(sizes)
    moves = [
        (
            0,
            (every, slice(low, low + sizes[at])),
            0,
            (block, every, slice(starts[at], starts[at + 1])),
        )
        for at in range(len(sizes))
        for block in range(n_seq)
        for low in [n_seq * starts[at] + block * sizes[at]]
    ]
    width = starts[-1]
    if extra:
        low = n_seq * width
        moves += [
            (0, (every, slice(low, low + extra)), 0, (block, every, slice(width, width + extra)))
            for block in range(n_seq)
        ]
    (parts,) = move([terms], [(n_seq, rows, width + extra)], moves)
    return pl.pallas_call(
        functools.partial(sum_kernel, pieces=edges(out_sizes)),
        out_shape=[jax.ShapeDtypeStruct((rows, size), jnp.float32) for size in out_sizes],
    )(swap(parts, "seq"))


def cut(array, sizes):
    return jnp.split(array, edges(sizes)[1:-1], axis=1)


def head_rows(row, head):
    return slice(row + head * HD, row + (head + 1) * HD)


def score_columns(key_ref, key_row, queries, head, allowed):
    scores = jnp.concatenate(
        [
            contract(key_ref[block, head_rows(key_row, head), :], queries, 0, 0)
            for block in range(key_ref.shape[0])
        ],
        axis=0,
    )
    if allowed is not None:
        scores = jnp.where(allowed, scores, masked_score)
    exponent = jnp.exp(scores - jnp.max(scores, axis=0, keepdims=True))
    return exponent * (1.0 / jnp.sum(exponent, axis=0, keepdims=True))


def allowed_columns(prefix_ref, step, blocks, rows):
    key_pos = lax.broadcasted_iota(jnp.int32, (blocks * rows, rows), 0)
    query_pos = step * rows + lax.broadcasted_iota(jnp.int32, (blocks * rows, rows), 1)
    return (key_pos <= query_pos) | (key_pos < prefix_ref[0])


def attend_kernel(prefix_ref, *refs, places, causal):
    out_ref = refs[-1]
    step = pl.program_id(0)
    (q_at, q_row), (k_at, k_row), (v_at, v_row) = places
    blocks, unused, rows = refs[k_at].shape
    allowed = allowed_columns(prefix_ref, step, blocks, rows) if causal else None
    for head in range(out_ref.shape[1] // HD):
        queries = refs[q_at][step, head_rows(q_row, head), :]
        queries = queries * jnp.asarray(HD**-0.5, queries.dtype)
        shares = score_columns(refs[k_at], k_row, queries, head, allowed).astype(queries.dtype)
        total = jnp.zeros(queries.shape, jnp.float32)
        for block in range(blocks):
            values = refs[v_at][block, head_rows(v_row, head), :]
            total += contract(values, shares[block * rows : (block + 1) * rows], 1, 0)
        out_ref[0, head_rows(0, head), :] = total.astype(out_ref.dtype)


def attend_back_kernel(prefix_ref, *refs, places, spots, count, causal):
    upstream_ref = refs[count]
    out_ref, key_sum, value_sum = refs[count + 1 :]
    step = pl.program_id(0)
    (q_at, q_row), (k_at, k_row), (v_at, v_row) = places
    blocks, unused, rows = refs[k_at].shape
    allowed = allowed_columns(prefix_ref, step, blocks, rows) if causal else None

    @pl.when(step == 0)
    def _():
        key_sum[...] = jnp.zeros_like(key_sum)
        value_sum[...] = jnp.zeros_like(value_sum)

    for head in range(upstream_ref.shape[1] // HD):
        mine = head_rows(0, head)
        queries = refs[q_at][step, head_rows(q_row, head), :]
        queries = queries * jnp.asarray(HD**-0.5, queries.dtype)
        upstream = upstream_ref[0, mine, :]
        shares = score_columns(refs[k_at], k_row, queries, head, allowed)
        share_grads = jnp.concatenate(
            [
                contract(refs[v_at][block, head_rows(v_row, head), :], upstream, 0, 0)
                for block in range(blocks)
            ],
            axis=0,
        )
        centre = jnp.sum(shares * share_grads, axis=0, keepdims=True)
        score_grads = (shares * (share_grads - centre)).astype(queries.dtype)
        shares = shares.astype(queries.dtype)
        total = jnp.zeros(queries.shape, jnp.float32)
        for block in range(blocks):
            part = slice(block * rows, (block + 1) * rows)
            key_rows = refs[k_at][block, head_rows(k_row, head), :]
            total += contract(key_rows, score_grads[part], 1, 0)
            key_sum[block, mine, :] += contract(queries, score_grads[part], 1, 1)
            value_sum[block, mine, :] += contract(upstream, shares[part], 1, 1)
        out_ref[step, head_rows(spots[0], head), :] = (total * HD**-0.5).astype(out_ref.dtype)

    @pl.when(step == pl.num_programs(0) - 1)
    def _():
        width = key_sum.shape[1]
        out_ref[:, spots[1] : spots[1] + width, :] = key_sum[...].astype(out_ref.dtype)
        out_ref[:, spots[2] : spots[2] + width, :] = value_sum[...].astype(out_ref.dtype)


def exit_kernel(token_ref, table_ref, shifted_ref, product_ref, part_ref, logit_ref, *, rows):
    lanes = table_ref.shape[1]
    chunk = next(size for size in (1024, 512, 256, 128) if lanes % size == 0)
    tokens = token_ref[...]
    row_max = jnp.full((tokens.shape[0], 1), -jnp.inf, jnp.float32)
    for low in range(0, lanes, chunk):
        logits = contract(tokens, table_ref[:, low : low + chunk], 1, 0)
        if low + chunk > rows:
            lane = low + lax.broadcasted_iota(jnp.int32, (1, chunk), 1)
            logits = jnp.where(lane < rows, logits, -jnp.inf)
        logit_ref[:, low : low + chunk] = logits
        row_max = jnp.maximum(row_max, jnp.max(logits, axis=1, keepdims=True))
    row_sum = jnp.zeros_like(row_max)
    product = jnp.zeros(product_ref.shape, jnp.float32)
    for low in range(0, lanes, chunk):
        shifted = jnp.exp(logit_ref[:, low : low + chunk] - row_max)
        row_sum += jnp.sum(shifted, axis=1, keepdims=True)
        shifted = shifted.astype(shifted_ref.dtype)
        shifted_ref[:, low : low + chunk] = shifted
        product += contract(shifted, table_ref[:, low : low + chunk], 1, 1)
    product_ref[...] = product
    lane = lax.broadcasted_iota(jnp.int32, part_ref.shape, 1)
    part_ref[...] = jnp.where(lane == 0, row_max, row_sum)


def exit_rows(tokens, table, rows):
    count, width = tokens.shape
    lanes = table.shape[1]
    step_rows = min(TOKEN_ROWS, count)
    return pl.pallas_call(
        functools.partial(exit_kernel, rows=rows),
        grid=(count // step_rows,),
        in_specs=[pl.BlockSpec((step_rows, width), lambda step: (step, 0)), whole(table)],
        out_specs=[
            pl.BlockSpec((step_rows, lanes), lambda step: (step, 0)),
            pl.BlockSpec((step_rows, width), lambda step: (step, 0)),
            pl.BlockSpec((step_rows, LANES), lambda step: (step, 0)),
        ],
        out_shape=[
            jax.ShapeDtypeStruct((count, lanes), jnp.bfloat16),
            jax.ShapeDtypeStruct((count, width), jnp.float32),
            jax.ShapeDtypeStruct((count, LANES), jnp.float32),
        ],
        scratch_shapes=[pltpu.VMEM((step_rows, lanes), jnp.float32)],
    )(tokens, table)


def whole(array):
    return pl.BlockSpec(array.shape, lambda step: (0,) * len(array.shape))


def attend(prefix, arrays, places, width, causal):
    blocks, unused, rows = arrays[0].shape
    return pl.pallas_call(
        functools.partial(attend_kernel, places=places, causal=causal),
        grid=(blocks,),
        in_specs=[pl.BlockSpec(memory_space=pltpu.SMEM)] + [whole(array) for array in arrays],
        out_specs=pl.BlockSpec((1, width, rows), lambda step: (step, 0, 0)),
        out_shape=jax.ShapeDtypeStruct((blocks, width, rows), jnp.bfloat16),
    )(prefix, *arrays)


def attend_back(prefix, arrays, upstream, places, causal):
    blocks, width, rows = upstream.shape
    shape = jax.ShapeDtypeStruct((blocks, 3 * width, rows), jnp.bfloat16)
    return pl.pallas_call(
        functools.partial(
            attend_back_kernel,
            places=places,
            spots=(0, width, 2 * width),
            count=len(arrays),
            causal=causal,
        ),
        grid=(blocks,),
        in_specs=[pl.BlockSpec(memory_space=pltpu.SMEM)]
        + [whole(array) for array in arrays]
        + [pl.BlockSpec((1, width, rows), lambda step: (step, 0, 0))],
        out_specs=whole(shape),
        out_shape=shape,
        scratch_shapes=[pltpu.VMEM((blocks, width, rows), jnp.float32)] * 2,
    )(prefix, *arrays, upstream)


def per_device(
    hidden_in,
    encoder_in,
    prefix_len,
    exit_flags,
    target_ids,
    out_cotangent,
    self_gain,
    self_query,
    self_key,
    self_value,
    self_output,
    cross_gain,
    cross_query,
    cross_key,
    cross_value,
    cross_output,
    feed_gain,
    feed_gate,
    feed_up,
    feed_down,
    exit_gain,
    embedding,
):
    width = hidden_in.shape[2]
    n_seq = lax.axis_size("seq")
    n_dp = lax.axis_size(dp)
    own_rows, own = self_query.shape
    own_feed = feed_gate.shape[1]
    fold_rows = feed_down.shape[0]
    folds = -(-fold_rows // own_rows)
    vocab_rows = embedding.shape[0]
    vocab_lanes = -(-vocab_rows // LANES) * LANES
    low = jnp.bfloat16

    gains = jnp.stack([self_gain, cross_gain, feed_gain, exit_gain], axis=1)
    early = -(-(5 * own + 4) // LANES) * LANES
    gains = jnp.pad(gains, ((0, 0), (0, early - 5 * own - 4)))
    folded = jnp.pad(feed_down, ((0, folds * own_rows - fold_rows), (0, 0)))
    shards = [
        self_query,
        self_key,
        self_value,
        cross_key,
        cross_value,
        gains,
        self_output,
        cross_query,
        cross_output,
        feed_gate,
        feed_up,
    ] + [folded[fold * own_rows : (fold + 1) * own_rows] for fold in range(folds)]
    starts = edges([shard.shape[1] for shard in shards])
    (flat,) = move(
        shards,
        [(own_rows, starts[-1])],
        [
            (at, (every, every), 0, (every, slice(starts[at], starts[at + 1])))
            for at in range(len(shards))
        ],
    )
    full = lax.all_gather(flat, ("seq",) + dp, axis=0, tiled=True).reshape(n_seq, width, -1)
    self_qkv, cross_kv, gain_columns = matrices(
        full,
        early,
        ((0, 3 * own, n_seq), (3 * own, 2 * own, n_seq), (5 * own, early - 5 * own, 1)),
    )
    rest_sizes = (own, 2 * own, own, own, own_feed, own_feed) + (own,) * folds

    marks = jnp.concatenate(
        [exit_flags, target_ids, jnp.broadcast_to(prefix_len[:, None], exit_flags.shape)], axis=0
    )
    hidden = relocate(hidden_in.reshape(-1, width))
    states = relocate(encoder_in.reshape(-1, width))
    marks = relocate(marks)
    prefix_len = marks[2, :1]
    marks = lax.all_gather(marks[:2], dp, axis=0)
    shard = jnp.pad(embedding.T, ((0, 0), (0, vocab_lanes - vocab_rows)))
    shard, marks, hidden, states = lax.optimization_barrier((shard, marks, hidden, states))
    table = lax.all_gather(shard, "seq", axis=0, tiled=True)
    cotangent = relocate(out_cotangent.reshape(-1, width).astype(low))
    gain_one, gain_two, gain_three, gain_exit = gain_columns[:, :4].astype(jnp.float32).T

    def blocks(rows):
        return rows.astype(low).reshape(n_seq, -1, rows.shape[1])

    def fold_up(rows):
        rows = rows.reshape(n_dp, fold_rows, -1)
        rows = jnp.pad(rows, ((0, 0), (0, folds * own_rows - fold_rows), (0, 0)))
        return [
            rows[:, fold * own_rows : (fold + 1) * own_rows].reshape(width, -1)
            for fold in range(folds)
        ]

    def unfold(parts):
        parts = [part.reshape(n_dp, own_rows, -1) for part in parts]
        rows = jnp.concatenate(parts, axis=1)[:, :fold_rows]
        return rows.reshape(n_dp * fold_rows, -1)

    residual_in = hidden.T.astype(jnp.float32)
    token_count = residual_in.shape[1]
    residual_in, states, cotangent = lax.optimization_barrier((residual_in, states.T, cotangent.T))
    residual_in, states = rows_first(residual_in), rows_first(states)
    cotangent = rows_first(cotangent)
    normed_one = norm_columns(residual_in, gain_one).astype(low)
    attended = jnp.concatenate(
        [blocks(contract(self_qkv, normed_one, 0, 0)), blocks(contract(cross_kv, states, 0, 0))],
        axis=1,
    )
    attended, full = lax.optimization_barrier((attended, full))
    attended = swap(attended, "part")
    self_out, cross_q, cross_out, gate_full, up_full, *downs = matrices(
        full,
        starts[-1],
        tuple(
            (starts[at], starts[at + 1] - starts[at], n_seq) for at in range(6, len(shards))
        ),
    )
    attended, self_out = lax.optimization_barrier((attended, self_out))
    self_places = ((0, 0), (0, own), (0, 2 * own))
    mixture_one = swap(attend(prefix_len, [attended], self_places, own, True), "part")
    mixture_one = mixture_one.reshape(width, token_count)
    after_self = residual_in + contract(self_out, mixture_one, 0, 0)
    normed_two = norm_columns(after_self, gain_two).astype(low)
    q_two = swap(blocks(contract(cross_q, normed_two, 0, 0)), "part")
    cross_places = ((0, 0), (1, 3 * own), (1, 4 * own))
    mixture_two = swap(attend(prefix_len, [q_two, attended], cross_places, own, False), "part")
    mixture_two = mixture_two.reshape(width, token_count)
    after_cross = after_self + contract(cross_out, mixture_two, 0, 0)
    normed_three = norm_columns(after_cross, gain_three).astype(low)
    gate_pre = contract(gate_full, normed_three, 0, 0)
    up_pre = contract(up_full, normed_three, 0, 0)
    hidden_mid = gated_unit(gate_pre, up_pre).astype(low)
    hidden_folds = fold_up(hidden_mid)
    after_feed = after_cross
    for down, hidden in zip(downs, hidden_folds):
        after_feed = after_feed + contract(down, hidden, 0, 0)
    block_output = relocate(after_feed.T.astype(low)).reshape(hidden_in.shape)
    normed_exit = rows_first(norm_columns(after_feed, gain_exit).astype(low).T)
    normed_exit, table = lax.optimization_barrier((normed_exit, table))

    tokens = lax.all_gather(normed_exit, dp, axis=0, tiled=True)
    flag_rows = marks[:, 0].reshape(-1, 1).astype(jnp.float32)
    target_rows = marks[:, 1].reshape(-1, 1) - lax.axis_index(dp) * vocab_rows
    hits = jnp.arange(vocab_lanes)[None, :] == target_rows
    hits = hits & (target_rows < vocab_rows)
    target_terms = contract(hits.astype(low), table, 1, 1).astype(low)
    tokens, target_terms = lax.optimization_barrier((tokens, target_terms))
    shifted, products, parts = exit_rows(tokens, table, vocab_rows)
    picked = jnp.sum(tokens.astype(jnp.float32) * target_terms.astype(jnp.float32), axis=1)
    row_max = parts[:, 0]
    parts = lax.all_gather(jnp.stack([row_max, parts[:, 1], picked]), dp, axis=0)
    top = jnp.max(parts[:, 0], axis=0)
    log_total = top + jnp.log(jnp.sum(parts[:, 1] * jnp.exp(parts[:, 0] - top), axis=0))
    all_losses = flag_rows[:, 0] * (log_total - jnp.sum(parts[:, 2], axis=0))
    token_losses = lax.dynamic_slice(
        all_losses, (lax.axis_index(dp) * token_count,), (token_count,)
    )
    token_losses = relocate(token_losses.reshape(exit_flags.shape))
    factor = flag_rows * jnp.exp(row_max - log_total)[:, None]
    exit_in_grad = lax.psum_scatter(
        rows_first((factor * products - flag_rows * target_terms.astype(jnp.float32)).astype(low)),
        dp,
        scatter_dimension=0,
        tiled=True,
    )
    logit_grads = jnp.where(hits, factor * shifted - flag_rows, factor * shifted).astype(low)
    table_terms = contract(tokens, logit_grads, 0, 0).astype(low)
    exit_in_grad, table_terms, block_output, token_losses = lax.optimization_barrier(
        (rows_first(exit_in_grad), table_terms, block_output, token_losses)
    )
    exit_in_grad = rows_first(exit_in_grad.T).astype(jnp.float32)
    table_sums = lax.psum_scatter(table_terms, "seq", scatter_dimension=0, tiled=True)

    feed_grad, full_exit_gain = norm_back(after_feed, gain_exit, exit_in_grad)
    feed_grad = feed_grad + cotangent
    branch_three = feed_grad.astype(low)
    hidden_mid_grad = unfold([contract(down, branch_three, 1, 0) for down in downs])
    unused, gated_pull = jax.vjp(gated_unit, gate_pre, up_pre)
    gate_grad, up_grad = gated_pull(hidden_mid_grad)
    gate_grad, up_grad = gate_grad.astype(low), up_grad.astype(low)
    normed_three_grad = contract(gate_full, gate_grad, 1, 0) + contract(up_full, up_grad, 1, 0)
    cross_grad, full_feed_gain = norm_back(after_cross, gain_three, normed_three_grad)
    cross_grad = cross_grad + feed_grad
    branch_two = cross_grad.astype(low)
    mixture_two_grad = blocks(contract(cross_out, branch_two, 1, 0))
    cross_grads = attend_back(
        prefix_len, [q_two, attended], swap(mixture_two_grad, "part"), cross_places, False
    )
    cross_grads = swap(cross_grads, "part")
    q_grad = cross_grads[:, :own].reshape(-1, token_count)
    kv_grad = cross_grads[:, own:].reshape(-1, token_count)
    encoder_grad = relocate(contract(kv_grad, cross_kv, 0, 1).astype(low)).astype(jnp.float32)
    self_grad, full_cross_gain = norm_back(after_self, gain_two, contract(cross_q, q_grad, 1, 0))
    self_grad = self_grad + cross_grad
    branch_one = self_grad.astype(low)
    rest_terms = jnp.concatenate(
        [
            contract(normed_two, q_grad, 1, 1).astype(low),
            contract(states, kv_grad, 1, 1).astype(low),
            contract(mixture_two, branch_two, 1, 1).astype(low),
            contract(mixture_one, branch_one, 1, 1).astype(low),
            contract(normed_three, gate_grad, 1, 1).astype(low),
            contract(normed_three, up_grad, 1, 1).astype(low),
        ]
        + [contract(hidden, branch_three, 1, 1).astype(low) for hidden in hidden_folds],
        axis=1,
    )
    mixture_one_grad = blocks(contract(self_out, branch_one, 1, 0))
    mixture_one_grad, rest_terms = lax.optimization_barrier((mixture_one_grad, rest_terms))
    rest_terms, table_sums = lax.optimization_barrier((rest_terms, table_sums))
    rest_terms = lax.psum_scatter(rest_terms, dp, scatter_dimension=0, tiled=True)
    qkv_grad = attend_back(
        prefix_len, [attended], swap(mixture_one_grad, "part"), self_places, True
    )
    qkv_grad, encoder_grad = lax.optimization_barrier((qkv_grad, encoder_grad))
    qkv_grad = swap(qkv_grad, "part").reshape(-1, token_count)
    normed_one_grad = contract(self_qkv, qkv_grad, 1, 0)
    input_grad, full_self_gain = norm_back(residual_in, gain_one, normed_one_grad)
    hidden_grad = relocate((input_grad + self_grad).T.astype(low)).astype(jnp.float32)
    gain_terms = jnp.stack(
        [full_self_gain, full_cross_gain, full_feed_gain, full_exit_gain], axis=1
    ).astype(low)
    gain_terms = jnp.pad(gain_terms, ((0, 0), (0, GAIN_LANES - gain_terms.shape[1])))
    self_terms = jnp.concatenate(
        [
            contract(normed_one, qkv_grad, 1, 1).astype(low),
            gain_terms,
        ],
        axis=1,
    )
    self_terms, rest_terms = lax.optimization_barrier((self_terms, rest_terms))
    self_terms = lax.psum_scatter(self_terms, dp, scatter_dimension=0, tiled=True)
    embedding_grad = table_sums[:, :vocab_rows].astype(jnp.float32).T
    (
        cross_query_grad,
        cross_key_grad,
        cross_value_grad,
        cross_output_grad,
        self_output_grad,
        feed_gate_grad,
        feed_up_grad,
        *down_sums,
    ) = deliver(rest_terms, rest_sizes, 0, (own,) * 5 + rest_sizes[4:])
    down_grad = jnp.concatenate(down_sums, axis=0)[:fold_rows]
    self_query_grad, self_key_grad, self_value_grad, gain_sums = deliver(
        self_terms, (3 * own,), GAIN_LANES, (own,) * 3 + (GAIN_LANES,)
    )
    gain_sums = gain_sums[:, :4].T
    return (
        block_output,
        token_losses,
        hidden_grad.reshape(hidden_in.shape),
        encoder_grad.reshape(encoder_in.shape),
        gain_sums[0],
        self_query_grad,
        self_key_grad,
        self_value_grad,
        self_output_grad,
        gain_sums[1],
        cross_query_grad,
        cross_key_grad,
        cross_value_grad,
        cross_output_grad,
        gain_sums[2],
        feed_gate_grad,
        feed_up_grad,
        down_grad,
        gain_sums[3],
        embedding_grad,
    )


def solution(mesh):
    size = mesh.shape["seq"]
    planes = Mesh(mesh.devices.reshape(-1, size, size), dp + ("seq",))
    tokens = P(dp, "seq")
    rows = P(dp)
    matrix = P(dp, "seq")
    block = P(dp, "seq", None)
    attention = (rows,) + (matrix,) * 4
    return jax.shard_map(
        per_device,
        mesh=planes,
        in_specs=(block, block, rows, tokens, tokens, block)
        + attention * 2
        + (rows, matrix, matrix, matrix, rows, matrix),
        out_specs=(block, tokens, block, block)
        + attention * 2
        + (rows, matrix, matrix, matrix, rows, matrix),
        check_vma=False,
    )
```

```python
import functools

import jax
import jax.numpy as jnp
from jax import lax
from jax.experimental import pallas as pl
from jax.experimental.layout import Layout, with_layout_constraint
from jax.experimental.pallas import tpu as pltpu
from jax.sharding import Mesh
from jax.sharding import PartitionSpec as P

HD = 64
GAIN_LANES = 128
LANES = 128

norm_eps = 1e-06
masked_score = -1000000000.0
dp = ("group", "part")


def contract(first_op, second_op, first_dim, second_dim):
    return lax.dot_general(
        first_op,
        second_op,
        (((first_dim,), (second_dim,)), ((), ())),
        preferred_element_type=jnp.float32,
    )


def rows_first(array):
    return with_layout_constraint(array, Layout(major_to_minor=tuple(range(array.ndim))))


def norm_columns(inputs, scaling):
    return (
        inputs
        * lax.rsqrt(jnp.mean(inputs * inputs, axis=0, keepdims=True) + norm_eps)
        * scaling[:, None]
    )


def norm_back(inputs, scaling, upstream):
    unused, pullback = jax.vjp(norm_columns, inputs, scaling)
    return pullback(upstream)


def gated_unit(gate_in, upward):
    return jax.nn.gelu(gate_in, approximate=True) * upward


def swap(pieces, axis):
    return lax.all_to_all(pieces, axis, 0, 0, tiled=True)


def relocate(block):
    size = lax.axis_size("seq")
    pairs = [
        ((group * size + part) * size + at, (group * size + at) * size + part)
        for group in range(lax.axis_size("group"))
        for part in range(size)
        for at in range(size)
    ]
    return lax.ppermute(block, ("group", "part", "seq"), pairs)


def move_kernel(*refs, moves, count):
    for source, taken, target, put in moves:
        refs[count + target][put] = refs[source][taken]


def move(arrays, shapes, moves):
    return pl.pallas_call(
        functools.partial(move_kernel, moves=moves, count=len(arrays)),
        out_shape=[jax.ShapeDtypeStruct(shape, jnp.bfloat16) for shape in shapes],
    )(*arrays)


def sum_kernel(terms_ref, *refs, pieces):
    for ref, low, high in zip(refs, pieces[:-1], pieces[1:]):
        total = terms_ref[0, :, low:high].astype(jnp.float32)
        for block in range(1, terms_ref.shape[0]):
            total += terms_ref[block, :, low:high].astype(jnp.float32)
        ref[...] = total


def edges(sizes):
    return [sum(sizes[:at]) for at in range(len(sizes) + 1)]


every = slice(None)


def gather_kernel(full_ref, *refs, pieces):
    for ref, (start, size, copies) in zip(refs, pieces):
        for block in range(copies):
            ref[:, block * size : (block + 1) * size] = full_ref[block, :, start : start + size]


def matrices(full, lanes, pieces):
    n_seq, rows, unused = full.shape
    return pl.pallas_call(
        functools.partial(gather_kernel, pieces=pieces),
        grid=(rows // LANES,),
        in_specs=[pl.BlockSpec((n_seq, LANES, lanes), lambda step: (0, step, 0))],
        out_specs=[
            pl.BlockSpec((LANES, size * copies), lambda step: (step, 0))
            for start, size, copies in pieces
        ],
        out_shape=[
            jax.ShapeDtypeStruct((rows, size * copies), jnp.bfloat16)
            for start, size, copies in pieces
        ],
    )(full)


def deliver(terms, sizes, extra, out_sizes):
    n_seq = lax.axis_size("seq")
    rows = terms.shape[0]
    starts = edges(sizes)
    moves = [
        (
            0,
            (every, slice(low, low + sizes[at])),
            0,
            (block, every, slice(starts[at], starts[at + 1])),
        )
        for at in range(len(sizes))
        for block in range(n_seq)
        for low in [n_seq * starts[at] + block * sizes[at]]
    ]
    width = starts[-1]
    if extra:
        low = n_seq * width
        moves += [
            (0, (every, slice(low, low + extra)), 0, (block, every, slice(width, width + extra)))
            for block in range(n_seq)
        ]
    (parts,) = move([terms], [(n_seq, rows, width + extra)], moves)
    return pl.pallas_call(
        functools.partial(sum_kernel, pieces=edges(out_sizes)),
        out_shape=[jax.ShapeDtypeStruct((rows, size), jnp.float32) for size in out_sizes],
    )(swap(parts, "seq"))


def cut(array, sizes):
    return jnp.split(array, edges(sizes)[1:-1], axis=1)


def head_rows(row, head):
    return slice(row + head * HD, row + (head + 1) * HD)


def score_columns(key_ref, key_row, queries, head, allowed):
    scores = jnp.concatenate(
        [
            contract(key_ref[block, head_rows(key_row, head), :], queries, 0, 0)
            for block in range(key_ref.shape[0])
        ],
        axis=0,
    )
    if allowed is not None:
        scores = jnp.where(allowed, scores, masked_score)
    exponent = jnp.exp(scores - jnp.max(scores, axis=0, keepdims=True))
    return exponent * (1.0 / jnp.sum(exponent, axis=0, keepdims=True))


def allowed_columns(prefix_ref, step, blocks, rows):
    key_pos = lax.broadcasted_iota(jnp.int32, (blocks * rows, rows), 0)
    query_pos = step * rows + lax.broadcasted_iota(jnp.int32, (blocks * rows, rows), 1)
    return (key_pos <= query_pos) | (key_pos < prefix_ref[0])


def attend_kernel(prefix_ref, *refs, places, causal):
    out_ref = refs[-1]
    step = pl.program_id(0)
    (q_at, q_row), (k_at, k_row), (v_at, v_row) = places
    blocks, unused, rows = refs[k_at].shape
    allowed = allowed_columns(prefix_ref, step, blocks, rows) if causal else None
    for head in range(out_ref.shape[1] // HD):
        queries = refs[q_at][step, head_rows(q_row, head), :]
        queries = queries * jnp.asarray(HD**-0.5, queries.dtype)
        shares = score_columns(refs[k_at], k_row, queries, head, allowed).astype(queries.dtype)
        total = jnp.zeros(queries.shape, jnp.float32)
        for block in range(blocks):
            values = refs[v_at][block, head_rows(v_row, head), :]
            total += contract(values, shares[block * rows : (block + 1) * rows], 1, 0)
        out_ref[0, head_rows(0, head), :] = total.astype(out_ref.dtype)


def attend_back_kernel(prefix_ref, *refs, places, spots, count, causal):
    upstream_ref = refs[count]
    out_ref, key_sum, value_sum = refs[count + 1 :]
    step = pl.program_id(0)
    (q_at, q_row), (k_at, k_row), (v_at, v_row) = places
    blocks, unused, rows = refs[k_at].shape
    allowed = allowed_columns(prefix_ref, step, blocks, rows) if causal else None

    @pl.when(step == 0)
    def _():
        key_sum[...] = jnp.zeros_like(key_sum)
        value_sum[...] = jnp.zeros_like(value_sum)

    for head in range(upstream_ref.shape[1] // HD):
        mine = head_rows(0, head)
        queries = refs[q_at][step, head_rows(q_row, head), :]
        queries = queries * jnp.asarray(HD**-0.5, queries.dtype)
        upstream = upstream_ref[0, mine, :]
        shares = score_columns(refs[k_at], k_row, queries, head, allowed)
        share_grads = jnp.concatenate(
            [
                contract(refs[v_at][block, head_rows(v_row, head), :], upstream, 0, 0)
                for block in range(blocks)
            ],
            axis=0,
        )
        centre = jnp.sum(shares * share_grads, axis=0, keepdims=True)
        score_grads = (shares * (share_grads - centre)).astype(queries.dtype)
        shares = shares.astype(queries.dtype)
        total = jnp.zeros(queries.shape, jnp.float32)
        for block in range(blocks):
            part = slice(block * rows, (block + 1) * rows)
            key_rows = refs[k_at][block, head_rows(k_row, head), :]
            total += contract(key_rows, score_grads[part], 1, 0)
            key_sum[block, mine, :] += contract(queries, score_grads[part], 1, 1)
            value_sum[block, mine, :] += contract(upstream, shares[part], 1, 1)
        out_ref[step, head_rows(spots[0], head), :] = (total * HD**-0.5).astype(out_ref.dtype)

    @pl.when(step == pl.num_programs(0) - 1)
    def _():
        width = key_sum.shape[1]
        out_ref[:, spots[1] : spots[1] + width, :] = key_sum[...].astype(out_ref.dtype)
        out_ref[:, spots[2] : spots[2] + width, :] = value_sum[...].astype(out_ref.dtype)


def exit_kernel(
    count_ref,
    token_ref,
    target_ref,
    table_ref,
    shifted_ref,
    product_ref,
    part_ref,
    logit_ref,
    *,
    rows,
):
    lanes = table_ref.shape[1]
    chunk = next(size for size in (1024, 512, 256, 128) if lanes % size == 0)
    step_rows = token_ref.shape[0]
    flagged = count_ref[pl.program_id(0)]

    def part_rows(first, last):
        here = slice(first, last)
        tokens = token_ref[here]
        row_max = jnp.full((last - first, 1), -jnp.inf, jnp.float32)
        for low in range(0, lanes, chunk):
            logits = contract(tokens, table_ref[:, low : low + chunk], 1, 0)
            if low + chunk > rows:
                lane = low + lax.broadcasted_iota(jnp.int32, (1, chunk), 1)
                logits = jnp.where(lane < rows, logits, -jnp.inf)
            logit_ref[here, low : low + chunk] = logits
            row_max = jnp.maximum(row_max, jnp.max(logits, axis=1, keepdims=True))
        row_sum = jnp.zeros_like(row_max)
        product = jnp.zeros((last - first, product_ref.shape[1]), jnp.float32)
        for low in range(0, lanes, chunk):
            shifted = jnp.exp(logit_ref[here, low : low + chunk] - row_max)
            row_sum += jnp.sum(shifted, axis=1, keepdims=True)
            shifted = shifted.astype(shifted_ref.dtype)
            shifted_ref[here, low : low + chunk] = shifted
            product += contract(shifted, table_ref[:, low : low + chunk], 1, 1)
        product_ref[here] = product
        picked = tokens.astype(jnp.float32) * target_ref[here].astype(jnp.float32)
        picked = jnp.sum(picked, axis=1, keepdims=True)
        lane = lax.broadcasted_iota(jnp.int32, (last - first, part_ref.shape[1]), 1)
        part_ref[here] = jnp.where(lane == 0, row_max, jnp.where(lane == 1, row_sum, picked))

    split = step_rows * 9 // 16
    part_rows(0, split)

    @pl.when(flagged > split)
    def _():
        part_rows(split, step_rows)

    @pl.when(flagged <= split)
    def _():
        here = slice(split, step_rows)
        shifted_ref[here] = jnp.zeros((step_rows - split, lanes), shifted_ref.dtype)
        product_ref[here] = jnp.zeros((step_rows - split, product_ref.shape[1]), jnp.float32)
        lane = lax.broadcasted_iota(jnp.int32, (step_rows - split, part_ref.shape[1]), 1)
        part_ref[here] = jnp.where(lane == 1, 1.0, 0.0)


def exit_rows(counts, tokens, targets, table, rows):
    count, width = tokens.shape
    lanes = table.shape[1]
    step_rows = count // counts.shape[0]
    block = pl.BlockSpec((step_rows, width), lambda step: (step, 0))
    return pl.pallas_call(
        functools.partial(exit_kernel, rows=rows),
        grid=(count // step_rows,),
        in_specs=[pl.BlockSpec(memory_space=pltpu.SMEM), block, block, whole(table)],
        out_specs=[
            pl.BlockSpec((step_rows, lanes), lambda step: (step, 0)),
            pl.BlockSpec((step_rows, width), lambda step: (step, 0)),
            pl.BlockSpec((step_rows, LANES), lambda step: (step, 0)),
        ],
        out_shape=[
            jax.ShapeDtypeStruct((count, lanes), jnp.bfloat16),
            jax.ShapeDtypeStruct((count, width), jnp.float32),
            jax.ShapeDtypeStruct((count, LANES), jnp.float32),
        ],
        scratch_shapes=[pltpu.VMEM((step_rows, lanes), jnp.float32)],
    )(counts, tokens, targets, table)


def whole(array):
    return pl.BlockSpec(array.shape, lambda step: (0,) * len(array.shape))


def attend(prefix, arrays, places, width, causal):
    blocks, unused, rows = arrays[0].shape
    return pl.pallas_call(
        functools.partial(attend_kernel, places=places, causal=causal),
        grid=(blocks,),
        in_specs=[pl.BlockSpec(memory_space=pltpu.SMEM)] + [whole(array) for array in arrays],
        out_specs=pl.BlockSpec((1, width, rows), lambda step: (step, 0, 0)),
        out_shape=jax.ShapeDtypeStruct((blocks, width, rows), jnp.bfloat16),
    )(prefix, *arrays)


def attend_back(prefix, arrays, upstream, places, causal):
    blocks, width, rows = upstream.shape
    shape = jax.ShapeDtypeStruct((blocks, 3 * width, rows), jnp.bfloat16)
    return pl.pallas_call(
        functools.partial(
            attend_back_kernel,
            places=places,
            spots=(0, width, 2 * width),
            count=len(arrays),
            causal=causal,
        ),
        grid=(blocks,),
        in_specs=[pl.BlockSpec(memory_space=pltpu.SMEM)]
        + [whole(array) for array in arrays]
        + [pl.BlockSpec((1, width, rows), lambda step: (step, 0, 0))],
        out_specs=whole(shape),
        out_shape=shape,
        scratch_shapes=[pltpu.VMEM((blocks, width, rows), jnp.float32)] * 2,
    )(prefix, *arrays, upstream)


def per_device(
    hidden_in,
    encoder_in,
    prefix_len,
    exit_flags,
    target_ids,
    out_cotangent,
    self_gain,
    self_query,
    self_key,
    self_value,
    self_output,
    cross_gain,
    cross_query,
    cross_key,
    cross_value,
    cross_output,
    feed_gain,
    feed_gate,
    feed_up,
    feed_down,
    exit_gain,
    embedding,
):
    width = hidden_in.shape[2]
    n_seq = lax.axis_size("seq")
    n_dp = lax.axis_size(dp)
    own_rows, own = self_query.shape
    own_feed = feed_gate.shape[1]
    fold_rows = feed_down.shape[0]
    folds = -(-fold_rows // own_rows)
    vocab_rows = embedding.shape[0]
    vocab_lanes = -(-vocab_rows // LANES) * LANES
    low = jnp.bfloat16

    gains = jnp.stack([self_gain, cross_gain, feed_gain, exit_gain], axis=1)
    early = -(-(5 * own + 4) // LANES) * LANES
    gains = jnp.pad(gains, ((0, 0), (0, early - 5 * own - 4)))
    folded = jnp.pad(feed_down, ((0, folds * own_rows - fold_rows), (0, 0)))
    shards = [
        self_query,
        self_key,
        self_value,
        cross_key,
        cross_value,
        gains,
        self_output,
        cross_query,
        cross_output,
        feed_gate,
        feed_up,
    ] + [folded[fold * own_rows : (fold + 1) * own_rows] for fold in range(folds)]
    starts = edges([shard.shape[1] for shard in shards])
    (flat,) = move(
        shards,
        [(own_rows, starts[-1])],
        [
            (at, (every, every), 0, (every, slice(starts[at], starts[at + 1])))
            for at in range(len(shards))
        ],
    )
    full = lax.all_gather(flat, ("seq",) + dp, axis=0, tiled=True).reshape(n_seq, width, -1)
    self_qkv, cross_kv, gain_columns = matrices(
        full,
        early,
        ((0, 3 * own, n_seq), (3 * own, 2 * own, n_seq), (5 * own, early - 5 * own, 1)),
    )
    rest_sizes = (own, 2 * own, own, own, own_feed, own_feed) + (own,) * folds

    marks = jnp.concatenate(
        [exit_flags, target_ids, jnp.broadcast_to(prefix_len[:, None], exit_flags.shape)], axis=0
    )
    hidden = relocate(hidden_in.reshape(-1, width))
    states = relocate(encoder_in.reshape(-1, width))
    marks = relocate(marks)
    prefix_len = marks[2, :1]
    place = jnp.arange(marks.shape[1])
    key = (1 - marks[0]) * marks.shape[1] + place
    rank = jnp.sum((key[None, :] < key[:, None]).astype(jnp.int32), axis=1)
    order = place[:, None] == rank[None, :]
    marks = jnp.sum(jnp.where(order[None], marks[:2, None, :], 0), axis=2)
    marks = lax.all_gather(marks, dp, axis=0)
    order_low = order.astype(low)
    shard = jnp.pad(embedding.T, ((0, 0), (0, vocab_lanes - vocab_rows)))
    shard, marks, hidden, states = lax.optimization_barrier((shard, marks, hidden, states))
    table = lax.all_gather(shard, "seq", axis=0, tiled=True)
    gain_one, gain_two, gain_three, gain_exit = gain_columns[:, :4].astype(jnp.float32).T

    def blocks(rows):
        return rows.astype(low).reshape(n_seq, -1, rows.shape[1])

    def fold_up(rows):
        rows = rows.reshape(n_dp, fold_rows, -1)
        rows = jnp.pad(rows, ((0, 0), (0, folds * own_rows - fold_rows), (0, 0)))
        return [
            rows[:, fold * own_rows : (fold + 1) * own_rows].reshape(width, -1)
            for fold in range(folds)
        ]

    def unfold(parts):
        parts = [part.reshape(n_dp, own_rows, -1) for part in parts]
        rows = jnp.concatenate(parts, axis=1)[:, :fold_rows]
        return rows.reshape(n_dp * fold_rows, -1)

    residual_in = hidden.T.astype(jnp.float32)
    token_count = residual_in.shape[1]
    residual_in, states = lax.optimization_barrier((residual_in, states.T))
    residual_in, states = rows_first(residual_in), rows_first(states)
    normed_one = norm_columns(residual_in, gain_one).astype(low)
    attended = jnp.concatenate(
        [blocks(contract(self_qkv, normed_one, 0, 0)), blocks(contract(cross_kv, states, 0, 0))],
        axis=1,
    )
    attended, full = lax.optimization_barrier((attended, full))
    attended = swap(attended, "part")
    self_out, cross_q, cross_out, gate_full, up_full, *downs = matrices(
        full,
        starts[-1],
        tuple(
            (starts[at], starts[at + 1] - starts[at], n_seq) for at in range(6, len(shards))
        ),
    )
    attended, self_out = lax.optimization_barrier((attended, self_out))
    self_places = ((0, 0), (0, own), (0, 2 * own))
    mixture_one = swap(attend(prefix_len, [attended], self_places, own, True), "part")
    mixture_one = mixture_one.reshape(width, token_count)
    after_self = residual_in + contract(self_out, mixture_one, 0, 0)
    normed_two = norm_columns(after_self, gain_two).astype(low)
    q_two = swap(blocks(contract(cross_q, normed_two, 0, 0)), "part")
    cross_places = ((0, 0), (1, 3 * own), (1, 4 * own))
    mixture_two = swap(attend(prefix_len, [q_two, attended], cross_places, own, False), "part")
    mixture_two = mixture_two.reshape(width, token_count)
    after_cross = after_self + contract(cross_out, mixture_two, 0, 0)
    normed_three = norm_columns(after_cross, gain_three).astype(low)
    gate_pre = contract(gate_full, normed_three, 0, 0)
    up_pre = contract(up_full, normed_three, 0, 0)
    hidden_mid = gated_unit(gate_pre, up_pre).astype(low)
    hidden_folds = fold_up(hidden_mid)
    after_feed = after_cross
    for down, hidden in zip(downs, hidden_folds):
        after_feed = after_feed + contract(down, hidden, 0, 0)
    block_output = relocate(after_feed.T.astype(low)).reshape(hidden_in.shape)
    normed_exit = contract(order_low, norm_columns(after_feed, gain_exit).astype(low), 1, 1)
    normed_exit = rows_first(normed_exit.astype(low))
    normed_exit, table = lax.optimization_barrier((normed_exit, table))

    tokens = lax.all_gather(normed_exit, dp, axis=0, tiled=True)
    flag_rows = marks[:, 0].reshape(-1, 1).astype(jnp.float32)
    target_rows = marks[:, 1].reshape(-1, 1) - lax.axis_index(dp) * vocab_rows
    hits = jnp.arange(vocab_lanes)[None, :] == target_rows
    hits = hits & (target_rows < vocab_rows)
    target_terms = contract(hits.astype(low), table, 1, 1).astype(low)
    tokens, target_terms = lax.optimization_barrier((tokens, target_terms))
    tokens, cotangent = lax.optimization_barrier((tokens, out_cotangent))
    cotangent = relocate(cotangent.reshape(-1, width).astype(low))
    counts = jnp.sum(marks[:, 0], axis=1)
    shifted, products, parts = exit_rows(counts, tokens, target_terms, table, vocab_rows)
    row_max = parts[:, 0]
    parts = lax.all_gather(parts[:, :3].T, dp, axis=0)
    top = jnp.max(parts[:, 0], axis=0)
    log_total = top + jnp.log(jnp.sum(parts[:, 1] * jnp.exp(parts[:, 0] - top), axis=0))
    all_losses = flag_rows[:, 0] * (log_total - jnp.sum(parts[:, 2], axis=0))
    token_losses = lax.dynamic_slice(
        all_losses, (lax.axis_index(dp) * token_count,), (token_count,)
    )
    token_losses = jnp.sum(jnp.where(order, token_losses[:, None], 0.0), axis=0)
    token_losses = relocate(token_losses.reshape(exit_flags.shape))
    factor = flag_rows * jnp.exp(row_max - log_total)[:, None]
    exit_in_grad = lax.psum_scatter(
        rows_first((factor * products - flag_rows * target_terms.astype(jnp.float32)).astype(low)),
        dp,
        scatter_dimension=0,
        tiled=True,
    )
    logit_grads = jnp.where(hits, factor * shifted - flag_rows, factor * shifted).astype(low)
    table_terms = contract(tokens, logit_grads, 0, 0).astype(low)
    exit_in_grad, table_terms, block_output, token_losses, cotangent = lax.optimization_barrier(
        (rows_first(exit_in_grad), table_terms, block_output, token_losses, cotangent)
    )
    cotangent = rows_first(cotangent.T)
    exit_in_grad = rows_first(contract(exit_in_grad, order_low, 0, 0))
    table_sums = lax.psum_scatter(table_terms, "seq", scatter_dimension=0, tiled=True)

    feed_grad, full_exit_gain = norm_back(after_feed, gain_exit, exit_in_grad)
    feed_grad = feed_grad + cotangent
    branch_three = feed_grad.astype(low)
    hidden_mid_grad = unfold([contract(down, branch_three, 1, 0) for down in downs])
    unused, gated_pull = jax.vjp(gated_unit, gate_pre, up_pre)
    gate_grad, up_grad = gated_pull(hidden_mid_grad)
    gate_grad, up_grad = gate_grad.astype(low), up_grad.astype(low)
    normed_three_grad = contract(gate_full, gate_grad, 1, 0) + contract(up_full, up_grad, 1, 0)
    cross_grad, full_feed_gain = norm_back(after_cross, gain_three, normed_three_grad)
    cross_grad = cross_grad + feed_grad
    branch_two = cross_grad.astype(low)
    mixture_two_grad = blocks(contract(cross_out, branch_two, 1, 0))
    cross_grads = attend_back(
        prefix_len, [q_two, attended], swap(mixture_two_grad, "part"), cross_places, False
    )
    cross_grads = swap(cross_grads, "part")
    q_grad = cross_grads[:, :own].reshape(-1, token_count)
    kv_grad = cross_grads[:, own:].reshape(-1, token_count)
    encoder_grad = relocate(contract(kv_grad, cross_kv, 0, 1).astype(low)).astype(jnp.float32)
    self_grad, full_cross_gain = norm_back(after_self, gain_two, contract(cross_q, q_grad, 1, 0))
    self_grad = self_grad + cross_grad
    branch_one = self_grad.astype(low)
    rest_terms = jnp.concatenate(
        [
            contract(normed_two, q_grad, 1, 1).astype(low),
            contract(states, kv_grad, 1, 1).astype(low),
            contract(mixture_two, branch_two, 1, 1).astype(low),
            contract(mixture_one, branch_one, 1, 1).astype(low),
            contract(normed_three, gate_grad, 1, 1).astype(low),
            contract(normed_three, up_grad, 1, 1).astype(low),
        ]
        + [contract(hidden, branch_three, 1, 1).astype(low) for hidden in hidden_folds],
        axis=1,
    )
    mixture_one_grad = blocks(contract(self_out, branch_one, 1, 0))
    mixture_one_grad, rest_terms = lax.optimization_barrier((mixture_one_grad, rest_terms))
    rest_terms, table_sums = lax.optimization_barrier((rest_terms, table_sums))
    rest_terms = lax.psum_scatter(rest_terms, dp, scatter_dimension=0, tiled=True)
    qkv_grad = attend_back(
        prefix_len, [attended], swap(mixture_one_grad, "part"), self_places, True
    )
    qkv_grad, encoder_grad = lax.optimization_barrier((qkv_grad, encoder_grad))
    qkv_grad = swap(qkv_grad, "part").reshape(-1, token_count)
    normed_one_grad = contract(self_qkv, qkv_grad, 1, 0)
    input_grad, full_self_gain = norm_back(residual_in, gain_one, normed_one_grad)
    hidden_grad = relocate((input_grad + self_grad).T.astype(low)).astype(jnp.float32)
    gain_terms = jnp.stack(
        [full_self_gain, full_cross_gain, full_feed_gain, full_exit_gain], axis=1
    ).astype(low)
    gain_terms = jnp.pad(gain_terms, ((0, 0), (0, GAIN_LANES - gain_terms.shape[1])))
    self_terms = jnp.concatenate(
        [
            contract(normed_one, qkv_grad, 1, 1).astype(low),
            gain_terms,
        ],
        axis=1,
    )
    self_terms, rest_terms = lax.optimization_barrier((self_terms, rest_terms))
    self_terms = lax.psum_scatter(self_terms, dp, scatter_dimension=0, tiled=True)
    embedding_grad = table_sums[:, :vocab_rows].astype(jnp.float32).T
    (
        cross_query_grad,
        cross_key_grad,
        cross_value_grad,
        cross_output_grad,
        self_output_grad,
        feed_gate_grad,
        feed_up_grad,
        *down_sums,
    ) = deliver(rest_terms, rest_sizes, 0, (own,) * 5 + rest_sizes[4:])
    down_grad = jnp.concatenate(down_sums, axis=0)[:fold_rows]
    self_query_grad, self_key_grad, self_value_grad, gain_sums = deliver(
        self_terms, (3 * own,), GAIN_LANES, (own,) * 3 + (GAIN_LANES,)
    )
    gain_sums = gain_sums[:, :4].T
    return (
        block_output,
        token_losses,
        hidden_grad.reshape(hidden_in.shape),
        encoder_grad.reshape(encoder_in.shape),
        gain_sums[0],
        self_query_grad,
        self_key_grad,
        self_value_grad,
        self_output_grad,
        gain_sums[1],
        cross_query_grad,
        cross_key_grad,
        cross_value_grad,
        cross_output_grad,
        gain_sums[2],
        feed_gate_grad,
        feed_up_grad,
        down_grad,
        gain_sums[3],
        embedding_grad,
    )


def solution(mesh):
    size = mesh.shape["seq"]
    planes = Mesh(mesh.devices.reshape(-1, size, size), dp + ("seq",))
    tokens = P(dp, "seq")
    rows = P(dp)
    matrix = P(dp, "seq")
    block = P(dp, "seq", None)
    attention = (rows,) + (matrix,) * 4
    return jax.shard_map(
        per_device,
        mesh=planes,
        in_specs=(block, block, rows, tokens, tokens, block)
        + attention * 2
        + (rows, matrix, matrix, matrix, rows, matrix),
        out_specs=(block, tokens, block, block)
        + attention * 2
        + (rows, matrix, matrix, matrix, rows, matrix),
        check_vma=False,
    )
```

```python
import functools

import jax
import jax.numpy as jnp
from jax import lax
from jax.experimental import pallas as pl
from jax.experimental.layout import Layout, with_layout_constraint
from jax.experimental.pallas import tpu as pltpu
from jax.sharding import Mesh
from jax.sharding import PartitionSpec as P

HD = 64
GAIN_LANES = 128
LANES = 128

norm_eps = 1e-06
masked_score = -1000000000.0
dp = ("group", "part")


def contract(first_op, second_op, first_dim, second_dim):
    return lax.dot_general(
        first_op,
        second_op,
        (((first_dim,), (second_dim,)), ((), ())),
        preferred_element_type=jnp.float32,
    )


def rows_first(array):
    return with_layout_constraint(array, Layout(major_to_minor=tuple(range(array.ndim))))


def norm_columns(inputs, scaling):
    return (
        inputs
        * lax.rsqrt(jnp.mean(inputs * inputs, axis=0, keepdims=True) + norm_eps)
        * scaling[:, None]
    )


def norm_back(inputs, scaling, upstream):
    unused, pullback = jax.vjp(norm_columns, inputs, scaling)
    return pullback(upstream)


def gated_unit(gate_in, upward):
    return jax.nn.gelu(gate_in, approximate=True) * upward


def swap(pieces, axis):
    return lax.all_to_all(pieces, axis, 0, 0, tiled=True)


def relocate(block):
    size = lax.axis_size("seq")
    pairs = [
        ((group * size + part) * size + at, (group * size + at) * size + part)
        for group in range(lax.axis_size("group"))
        for part in range(size)
        for at in range(size)
    ]
    return lax.ppermute(block, ("group", "part", "seq"), pairs)


def move_kernel(*refs, moves, count):
    for source, taken, target, put in moves:
        refs[count + target][put] = refs[source][taken]


def move(arrays, shapes, moves):
    return pl.pallas_call(
        functools.partial(move_kernel, moves=moves, count=len(arrays)),
        out_shape=[jax.ShapeDtypeStruct(shape, jnp.bfloat16) for shape in shapes],
    )(*arrays)


def sum_kernel(terms_ref, *refs, pieces):
    for ref, low, high in zip(refs, pieces[:-1], pieces[1:]):
        total = terms_ref[0, :, low:high].astype(jnp.float32)
        for block in range(1, terms_ref.shape[0]):
            total += terms_ref[block, :, low:high].astype(jnp.float32)
        ref[...] = total


def edges(sizes):
    return [sum(sizes[:at]) for at in range(len(sizes) + 1)]


every = slice(None)


def gather_kernel(full_ref, *refs, pieces):
    for ref, (start, size, copies) in zip(refs, pieces):
        for block in range(copies):
            ref[:, block * size : (block + 1) * size] = full_ref[block, :, start : start + size]


def matrices(full, lanes, pieces):
    n_seq, rows, unused = full.shape
    return pl.pallas_call(
        functools.partial(gather_kernel, pieces=pieces),
        grid=(rows // LANES,),
        in_specs=[pl.BlockSpec((n_seq, LANES, lanes), lambda step: (0, step, 0))],
        out_specs=[
            pl.BlockSpec((LANES, size * copies), lambda step: (step, 0))
            for start, size, copies in pieces
        ],
        out_shape=[
            jax.ShapeDtypeStruct((rows, size * copies), jnp.bfloat16)
            for start, size, copies in pieces
        ],
    )(full)


def deliver(terms, sizes, extra, out_sizes):
    n_seq = lax.axis_size("seq")
    rows = terms.shape[0]
    starts = edges(sizes)
    moves = [
        (
            0,
            (every, slice(low, low + sizes[at])),
            0,
            (block, every, slice(starts[at], starts[at + 1])),
        )
        for at in range(len(sizes))
        for block in range(n_seq)
        for low in [n_seq * starts[at] + block * sizes[at]]
    ]
    width = starts[-1]
    if extra:
        low = n_seq * width
        moves += [
            (0, (every, slice(low, low + extra)), 0, (block, every, slice(width, width + extra)))
            for block in range(n_seq)
        ]
    (parts,) = move([terms], [(n_seq, rows, width + extra)], moves)
    return pl.pallas_call(
        functools.partial(sum_kernel, pieces=edges(out_sizes)),
        out_shape=[jax.ShapeDtypeStruct((rows, size), jnp.float32) for size in out_sizes],
    )(swap(parts, "seq"))


def cut(array, sizes):
    return jnp.split(array, edges(sizes)[1:-1], axis=1)


def head_rows(row, head):
    return slice(row + head * HD, row + (head + 1) * HD)


def score_columns(key_ref, key_row, queries, head, allowed):
    scores = jnp.concatenate(
        [
            contract(key_ref[block, head_rows(key_row, head), :], queries, 0, 0)
            for block in range(key_ref.shape[0])
        ],
        axis=0,
    )
    if allowed is not None:
        scores = jnp.where(allowed, scores, masked_score)
    exponent = jnp.exp(scores - jnp.max(scores, axis=0, keepdims=True))
    return exponent * (1.0 / jnp.sum(exponent, axis=0, keepdims=True))


def allowed_columns(prefix_ref, step, blocks, rows):
    key_pos = lax.broadcasted_iota(jnp.int32, (blocks * rows, rows), 0)
    query_pos = step * rows + lax.broadcasted_iota(jnp.int32, (blocks * rows, rows), 1)
    return (key_pos <= query_pos) | (key_pos < prefix_ref[0])


def attend_kernel(prefix_ref, *refs, places, causal):
    out_ref = refs[-1]
    step = pl.program_id(0)
    (q_at, q_row), (k_at, k_row), (v_at, v_row) = places
    blocks, unused, rows = refs[k_at].shape
    allowed = allowed_columns(prefix_ref, step, blocks, rows) if causal else None
    for head in range(out_ref.shape[1] // HD):
        queries = refs[q_at][step, head_rows(q_row, head), :]
        queries = queries * jnp.asarray(HD**-0.5, queries.dtype)
        shares = score_columns(refs[k_at], k_row, queries, head, allowed).astype(queries.dtype)
        total = jnp.zeros(queries.shape, jnp.float32)
        for block in range(blocks):
            values = refs[v_at][block, head_rows(v_row, head), :]
            total += contract(values, shares[block * rows : (block + 1) * rows], 1, 0)
        out_ref[0, head_rows(0, head), :] = total.astype(out_ref.dtype)


def attend_back_kernel(prefix_ref, *refs, places, spots, count, causal):
    upstream_ref = refs[count]
    out_ref, key_sum, value_sum = refs[count + 1 :]
    step = pl.program_id(0)
    (q_at, q_row), (k_at, k_row), (v_at, v_row) = places
    blocks, unused, rows = refs[k_at].shape
    allowed = allowed_columns(prefix_ref, step, blocks, rows) if causal else None

    @pl.when(step == 0)
    def _():
        key_sum[...] = jnp.zeros_like(key_sum)
        value_sum[...] = jnp.zeros_like(value_sum)

    for head in range(upstream_ref.shape[1] // HD):
        mine = head_rows(0, head)
        queries = refs[q_at][step, head_rows(q_row, head), :]
        queries = queries * jnp.asarray(HD**-0.5, queries.dtype)
        upstream = upstream_ref[0, mine, :]
        shares = score_columns(refs[k_at], k_row, queries, head, allowed)
        share_grads = jnp.concatenate(
            [
                contract(refs[v_at][block, head_rows(v_row, head), :], upstream, 0, 0)
                for block in range(blocks)
            ],
            axis=0,
        )
        centre = jnp.sum(shares * share_grads, axis=0, keepdims=True)
        score_grads = (shares * (share_grads - centre)).astype(queries.dtype)
        shares = shares.astype(queries.dtype)
        total = jnp.zeros(queries.shape, jnp.float32)
        for block in range(blocks):
            part = slice(block * rows, (block + 1) * rows)
            key_rows = refs[k_at][block, head_rows(k_row, head), :]
            total += contract(key_rows, score_grads[part], 1, 0)
            key_sum[block, mine, :] += contract(queries, score_grads[part], 1, 1)
            value_sum[block, mine, :] += contract(upstream, shares[part], 1, 1)
        out_ref[step, head_rows(spots[0], head), :] = (total * HD**-0.5).astype(out_ref.dtype)

    @pl.when(step == pl.num_programs(0) - 1)
    def _():
        width = key_sum.shape[1]
        out_ref[:, spots[1] : spots[1] + width, :] = key_sum[...].astype(out_ref.dtype)
        out_ref[:, spots[2] : spots[2] + width, :] = value_sum[...].astype(out_ref.dtype)


def exit_kernel(
    count_ref,
    token_ref,
    target_ref,
    table_ref,
    shifted_ref,
    product_ref,
    part_ref,
    logit_ref,
    *,
    rows,
):
    lanes = table_ref.shape[1]
    chunk = next(size for size in (1024, 512, 256, 128) if lanes % size == 0)
    step_rows = token_ref.shape[0]
    flagged = count_ref[pl.program_id(0)]

    def part_rows(first, last):
        here = slice(first, last)
        tokens = token_ref[here]
        row_max = jnp.full((last - first, 1), -jnp.inf, jnp.float32)
        for low in range(0, lanes, chunk):
            logits = contract(tokens, table_ref[:, low : low + chunk], 1, 0)
            if low + chunk > rows:
                lane = low + lax.broadcasted_iota(jnp.int32, (1, chunk), 1)
                logits = jnp.where(lane < rows, logits, -jnp.inf)
            logit_ref[here, low : low + chunk] = logits
            row_max = jnp.maximum(row_max, jnp.max(logits, axis=1, keepdims=True))
        row_sum = jnp.zeros_like(row_max)
        product = jnp.zeros((last - first, product_ref.shape[1]), jnp.float32)
        for low in range(0, lanes, chunk):
            shifted = jnp.exp(logit_ref[here, low : low + chunk] - row_max)
            row_sum += jnp.sum(shifted, axis=1, keepdims=True)
            shifted = shifted.astype(shifted_ref.dtype)
            shifted_ref[here, low : low + chunk] = shifted
            product += contract(shifted, table_ref[:, low : low + chunk], 1, 1)
        product_ref[here] = product
        picked = tokens.astype(jnp.float32) * target_ref[here].astype(jnp.float32)
        picked = jnp.sum(picked, axis=1, keepdims=True)
        lane = lax.broadcasted_iota(jnp.int32, (last - first, part_ref.shape[1]), 1)
        part_ref[here] = jnp.where(lane == 0, row_max, jnp.where(lane == 1, row_sum, picked))

    split = step_rows * 9 // 16
    part_rows(0, split)

    @pl.when(flagged > split)
    def _():
        part_rows(split, step_rows)

    @pl.when(flagged <= split)
    def _():
        here = slice(split, step_rows)
        shifted_ref[here] = jnp.zeros((step_rows - split, lanes), shifted_ref.dtype)
        product_ref[here] = jnp.zeros((step_rows - split, product_ref.shape[1]), jnp.float32)
        lane = lax.broadcasted_iota(jnp.int32, (step_rows - split, part_ref.shape[1]), 1)
        part_ref[here] = jnp.where(lane == 1, 1.0, 0.0)


def exit_rows(counts, tokens, targets, table, rows):
    count, width = tokens.shape
    lanes = table.shape[1]
    step_rows = count // counts.shape[0]
    block = pl.BlockSpec((step_rows, width), lambda step: (step, 0))
    return pl.pallas_call(
        functools.partial(exit_kernel, rows=rows),
        grid=(count // step_rows,),
        in_specs=[pl.BlockSpec(memory_space=pltpu.SMEM), block, block, whole(table)],
        out_specs=[
            pl.BlockSpec((step_rows, lanes), lambda step: (step, 0)),
            pl.BlockSpec((step_rows, width), lambda step: (step, 0)),
            pl.BlockSpec((step_rows, LANES), lambda step: (step, 0)),
        ],
        out_shape=[
            jax.ShapeDtypeStruct((count, lanes), jnp.bfloat16),
            jax.ShapeDtypeStruct((count, width), jnp.float32),
            jax.ShapeDtypeStruct((count, LANES), jnp.float32),
        ],
        scratch_shapes=[pltpu.VMEM((step_rows, lanes), jnp.float32)],
    )(counts, tokens, targets, table)


def whole(array):
    return pl.BlockSpec(array.shape, lambda step: (0,) * len(array.shape))


def attend(prefix, arrays, places, width, causal):
    blocks, unused, rows = arrays[0].shape
    return pl.pallas_call(
        functools.partial(attend_kernel, places=places, causal=causal),
        grid=(blocks,),
        in_specs=[pl.BlockSpec(memory_space=pltpu.SMEM)] + [whole(array) for array in arrays],
        out_specs=pl.BlockSpec((1, width, rows), lambda step: (step, 0, 0)),
        out_shape=jax.ShapeDtypeStruct((blocks, width, rows), jnp.bfloat16),
    )(prefix, *arrays)


def attend_back(prefix, arrays, upstream, places, causal):
    blocks, width, rows = upstream.shape
    shape = jax.ShapeDtypeStruct((blocks, 3 * width, rows), jnp.bfloat16)
    return pl.pallas_call(
        functools.partial(
            attend_back_kernel,
            places=places,
            spots=(0, width, 2 * width),
            count=len(arrays),
            causal=causal,
        ),
        grid=(blocks,),
        in_specs=[pl.BlockSpec(memory_space=pltpu.SMEM)]
        + [whole(array) for array in arrays]
        + [pl.BlockSpec((1, width, rows), lambda step: (step, 0, 0))],
        out_specs=whole(shape),
        out_shape=shape,
        scratch_shapes=[pltpu.VMEM((blocks, width, rows), jnp.float32)] * 2,
    )(prefix, *arrays, upstream)


def per_device(
    hidden_in,
    encoder_in,
    prefix_len,
    exit_flags,
    target_ids,
    out_cotangent,
    self_gain,
    self_query,
    self_key,
    self_value,
    self_output,
    cross_gain,
    cross_query,
    cross_key,
    cross_value,
    cross_output,
    feed_gain,
    feed_gate,
    feed_up,
    feed_down,
    exit_gain,
    embedding,
):
    width = hidden_in.shape[2]
    n_seq = lax.axis_size("seq")
    n_dp = lax.axis_size(dp)
    own_rows, own = self_query.shape
    own_feed = feed_gate.shape[1]
    fold_rows = feed_down.shape[0]
    folds = -(-fold_rows // own_rows)
    vocab_rows = embedding.shape[0]
    vocab_lanes = -(-vocab_rows // LANES) * LANES
    low = jnp.bfloat16

    gains = jnp.stack([self_gain, cross_gain, feed_gain, exit_gain], axis=1)
    early = -(-(5 * own + 4) // LANES) * LANES
    gains = jnp.pad(gains, ((0, 0), (0, early - 5 * own - 4)))
    folded = jnp.pad(feed_down, ((0, folds * own_rows - fold_rows), (0, 0)))
    shards = [
        self_query,
        self_key,
        self_value,
        cross_key,
        cross_value,
        gains,
        self_output,
        cross_query,
        cross_output,
        feed_gate,
        feed_up,
    ] + [folded[fold * own_rows : (fold + 1) * own_rows] for fold in range(folds)]
    starts = edges([shard.shape[1] for shard in shards])
    (flat,) = move(
        shards,
        [(own_rows, starts[-1])],
        [
            (at, (every, every), 0, (every, slice(starts[at], starts[at + 1])))
            for at in range(len(shards))
        ],
    )
    full = lax.all_gather(flat, ("seq",) + dp, axis=0, tiled=True).reshape(n_seq, width, -1)
    self_qkv, cross_kv, gain_columns = matrices(
        full,
        early,
        ((0, 3 * own, n_seq), (3 * own, 2 * own, n_seq), (5 * own, early - 5 * own, 1)),
    )
    rest_sizes = (own, 2 * own, own, own, own_feed, own_feed) + (own,) * folds

    marks = jnp.concatenate(
        [exit_flags, target_ids, jnp.broadcast_to(prefix_len[:, None], exit_flags.shape)], axis=0
    )
    hidden = relocate(hidden_in.reshape(-1, width))
    states = relocate(encoder_in.reshape(-1, width))
    marks = relocate(marks)
    prefix_len = marks[2, :1]
    place = jnp.arange(marks.shape[1])
    key = (1 - marks[0]) * marks.shape[1] + place
    rank = jnp.sum((key[None, :] < key[:, None]).astype(jnp.int32), axis=1)
    order = place[:, None] == rank[None, :]
    marks = jnp.sum(jnp.where(order[None], marks[:2, None, :], 0), axis=2)
    marks = lax.all_gather(marks, dp, axis=0)
    order_low = order.astype(low)
    shard = jnp.pad(embedding.T, ((0, 0), (0, vocab_lanes - vocab_rows)))
    shard, marks, hidden, states = lax.optimization_barrier((shard, marks, hidden, states))
    table = lax.all_gather(shard, "seq", axis=0, tiled=True)
    gain_one, gain_two, gain_three, gain_exit = gain_columns[:, :4].astype(jnp.float32).T

    def blocks(rows):
        return rows.astype(low).reshape(n_seq, -1, rows.shape[1])

    def fold_up(rows):
        rows = rows.reshape(n_dp, fold_rows, -1)
        rows = jnp.pad(rows, ((0, 0), (0, folds * own_rows - fold_rows), (0, 0)))
        return [
            rows[:, fold * own_rows : (fold + 1) * own_rows].reshape(width, -1)
            for fold in range(folds)
        ]

    def unfold(parts):
        parts = [part.reshape(n_dp, own_rows, -1) for part in parts]
        rows = jnp.concatenate(parts, axis=1)[:, :fold_rows]
        return rows.reshape(n_dp * fold_rows, -1)

    residual_in = hidden.T.astype(jnp.float32)
    token_count = residual_in.shape[1]
    residual_in, states = lax.optimization_barrier((residual_in, states.T))
    residual_in, states = rows_first(residual_in), rows_first(states)
    normed_one = norm_columns(residual_in, gain_one).astype(low)
    attended = jnp.concatenate(
        [blocks(contract(self_qkv, normed_one, 0, 0)), blocks(contract(cross_kv, states, 0, 0))],
        axis=1,
    )
    attended, full = lax.optimization_barrier((attended, full))
    attended = swap(attended, "part")
    self_out, cross_q, cross_out, gate_full, up_full, *downs = matrices(
        full,
        starts[-1],
        tuple(
            (starts[at], starts[at + 1] - starts[at], n_seq) for at in range(6, len(shards))
        ),
    )
    attended, self_out = lax.optimization_barrier((attended, self_out))
    self_places = ((0, 0), (0, own), (0, 2 * own))
    mixture_one = swap(attend(prefix_len, [attended], self_places, own, True), "part")
    mixture_one = mixture_one.reshape(width, token_count)
    after_self = residual_in + contract(self_out, mixture_one, 0, 0)
    normed_two = norm_columns(after_self, gain_two).astype(low)
    q_two = swap(blocks(contract(cross_q, normed_two, 0, 0)), "part")
    cross_places = ((0, 0), (1, 3 * own), (1, 4 * own))
    mixture_two = swap(attend(prefix_len, [q_two, attended], cross_places, own, False), "part")
    mixture_two = mixture_two.reshape(width, token_count)
    after_cross = after_self + contract(cross_out, mixture_two, 0, 0)
    normed_three = norm_columns(after_cross, gain_three).astype(low)
    gate_pre = contract(gate_full, normed_three, 0, 0)
    up_pre = contract(up_full, normed_three, 0, 0)
    hidden_mid = gated_unit(gate_pre, up_pre).astype(low)
    hidden_folds = fold_up(hidden_mid)
    after_feed = after_cross
    for down, hidden in zip(downs, hidden_folds):
        after_feed = after_feed + contract(down, hidden, 0, 0)
    block_output = after_feed.T.astype(low)
    normed_exit = contract(order_low, norm_columns(after_feed, gain_exit).astype(low), 1, 1)
    normed_exit = rows_first(normed_exit.astype(low))
    normed_exit, table = lax.optimization_barrier((normed_exit, table))

    tokens = lax.all_gather(normed_exit, dp, axis=0, tiled=True)
    flag_rows = marks[:, 0].reshape(-1, 1).astype(jnp.float32)
    target_rows = marks[:, 1].reshape(-1, 1) - lax.axis_index(dp) * vocab_rows
    hits = jnp.arange(vocab_lanes)[None, :] == target_rows
    hits = hits & (target_rows < vocab_rows)
    target_terms = contract(hits.astype(low), table, 1, 1).astype(low)
    tokens, target_terms = lax.optimization_barrier((tokens, target_terms))
    tokens, cotangent, block_output = lax.optimization_barrier(
        (tokens, out_cotangent, block_output)
    )
    cotangent = relocate(cotangent.reshape(-1, width).astype(low))
    block_output = relocate(block_output)
    counts = jnp.sum(marks[:, 0], axis=1)
    shifted, products, parts = exit_rows(counts, tokens, target_terms, table, vocab_rows)
    parts, cotangent, block_output = lax.optimization_barrier((parts, cotangent, block_output))
    block_output = block_output.reshape(hidden_in.shape)
    row_max = parts[:, 0]
    parts = lax.all_gather(parts[:, :3].T, dp, axis=0)
    top = jnp.max(parts[:, 0], axis=0)
    log_total = top + jnp.log(jnp.sum(parts[:, 1] * jnp.exp(parts[:, 0] - top), axis=0))
    all_losses = flag_rows[:, 0] * (log_total - jnp.sum(parts[:, 2], axis=0))
    token_losses = lax.dynamic_slice(
        all_losses, (lax.axis_index(dp) * token_count,), (token_count,)
    )
    token_losses = jnp.sum(jnp.where(order, token_losses[:, None], 0.0), axis=0)
    token_losses = relocate(token_losses.reshape(exit_flags.shape))
    factor = flag_rows * jnp.exp(row_max - log_total)[:, None]
    exit_in_grad = lax.psum_scatter(
        rows_first((factor * products - flag_rows * target_terms.astype(jnp.float32)).astype(low)),
        dp,
        scatter_dimension=0,
        tiled=True,
    )
    logit_grads = jnp.where(hits, factor * shifted - flag_rows, factor * shifted).astype(low)
    table_terms = contract(tokens, logit_grads, 0, 0).astype(low)
    exit_in_grad, table_terms, token_losses = lax.optimization_barrier(
        (rows_first(exit_in_grad), table_terms, token_losses)
    )
    cotangent = rows_first(cotangent.T)
    exit_in_grad = rows_first(contract(exit_in_grad, order_low, 0, 0))
    table_sums = lax.psum_scatter(table_terms, "seq", scatter_dimension=0, tiled=True)

    feed_grad, full_exit_gain = norm_back(after_feed, gain_exit, exit_in_grad)
    feed_grad = feed_grad + cotangent
    branch_three = feed_grad.astype(low)
    hidden_mid_grad = unfold([contract(down, branch_three, 1, 0) for down in downs])
    unused, gated_pull = jax.vjp(gated_unit, gate_pre, up_pre)
    gate_grad, up_grad = gated_pull(hidden_mid_grad)
    gate_grad, up_grad = gate_grad.astype(low), up_grad.astype(low)
    normed_three_grad = contract(gate_full, gate_grad, 1, 0) + contract(up_full, up_grad, 1, 0)
    cross_grad, full_feed_gain = norm_back(after_cross, gain_three, normed_three_grad)
    cross_grad = cross_grad + feed_grad
    branch_two = cross_grad.astype(low)
    mixture_two_grad = blocks(contract(cross_out, branch_two, 1, 0))
    cross_grads = attend_back(
        prefix_len, [q_two, attended], swap(mixture_two_grad, "part"), cross_places, False
    )
    cross_grads = swap(cross_grads, "part")
    q_grad = cross_grads[:, :own].reshape(-1, token_count)
    kv_grad = cross_grads[:, own:].reshape(-1, token_count)
    encoder_grad = relocate(contract(kv_grad, cross_kv, 0, 1).astype(low)).astype(jnp.float32)
    self_grad, full_cross_gain = norm_back(after_self, gain_two, contract(cross_q, q_grad, 1, 0))
    self_grad = self_grad + cross_grad
    branch_one = self_grad.astype(low)
    rest_terms = jnp.concatenate(
        [
            contract(normed_two, q_grad, 1, 1).astype(low),
            contract(states, kv_grad, 1, 1).astype(low),
            contract(mixture_two, branch_two, 1, 1).astype(low),
            contract(mixture_one, branch_one, 1, 1).astype(low),
            contract(normed_three, gate_grad, 1, 1).astype(low),
            contract(normed_three, up_grad, 1, 1).astype(low),
        ]
        + [contract(hidden, branch_three, 1, 1).astype(low) for hidden in hidden_folds],
        axis=1,
    )
    mixture_one_grad = blocks(contract(self_out, branch_one, 1, 0))
    mixture_one_grad, rest_terms = lax.optimization_barrier((mixture_one_grad, rest_terms))
    rest_terms, table_sums = lax.optimization_barrier((rest_terms, table_sums))
    rest_terms = lax.psum_scatter(rest_terms, dp, scatter_dimension=0, tiled=True)
    qkv_grad = attend_back(
        prefix_len, [attended], swap(mixture_one_grad, "part"), self_places, True
    )
    qkv_grad, encoder_grad = lax.optimization_barrier((qkv_grad, encoder_grad))
    qkv_grad = swap(qkv_grad, "part").reshape(-1, token_count)
    normed_one_grad = contract(self_qkv, qkv_grad, 1, 0)
    input_grad, full_self_gain = norm_back(residual_in, gain_one, normed_one_grad)
    hidden_grad = relocate((input_grad + self_grad).T.astype(low)).astype(jnp.float32)
    gain_terms = jnp.stack(
        [full_self_gain, full_cross_gain, full_feed_gain, full_exit_gain], axis=1
    ).astype(low)
    gain_terms = jnp.pad(gain_terms, ((0, 0), (0, GAIN_LANES - gain_terms.shape[1])))
    self_terms = jnp.concatenate(
        [
            contract(normed_one, qkv_grad, 1, 1).astype(low),
            gain_terms,
        ],
        axis=1,
    )
    self_terms, rest_terms, hidden_grad = lax.optimization_barrier(
        (self_terms, rest_terms, hidden_grad)
    )
    self_terms = lax.psum_scatter(self_terms, dp, scatter_dimension=0, tiled=True)
    embedding_grad = table_sums[:, :vocab_rows].astype(jnp.float32).T
    (
        cross_query_grad,
        cross_key_grad,
        cross_value_grad,
        cross_output_grad,
        self_output_grad,
        feed_gate_grad,
        feed_up_grad,
        *down_sums,
    ) = deliver(rest_terms, rest_sizes, 0, (own,) * 5 + rest_sizes[4:])
    down_grad = jnp.concatenate(down_sums, axis=0)[:fold_rows]
    self_query_grad, self_key_grad, self_value_grad, gain_sums = deliver(
        self_terms, (3 * own,), GAIN_LANES, (own,) * 3 + (GAIN_LANES,)
    )
    gain_sums = gain_sums[:, :4].T
    return (
        block_output,
        token_losses,
        hidden_grad.reshape(hidden_in.shape),
        encoder_grad.reshape(encoder_in.shape),
        gain_sums[0],
        self_query_grad,
        self_key_grad,
        self_value_grad,
        self_output_grad,
        gain_sums[1],
        cross_query_grad,
        cross_key_grad,
        cross_value_grad,
        cross_output_grad,
        gain_sums[2],
        feed_gate_grad,
        feed_up_grad,
        down_grad,
        gain_sums[3],
        embedding_grad,
    )


def solution(mesh):
    size = mesh.shape["seq"]
    planes = Mesh(mesh.devices.reshape(-1, size, size), dp + ("seq",))
    tokens = P(dp, "seq")
    rows = P(dp)
    matrix = P(dp, "seq")
    block = P(dp, "seq", None)
    attention = (rows,) + (matrix,) * 4
    return jax.shard_map(
        per_device,
        mesh=planes,
        in_specs=(block, block, rows, tokens, tokens, block)
        + attention * 2
        + (rows, matrix, matrix, matrix, rows, matrix),
        out_specs=(block, tokens, block, block)
        + attention * 2
        + (rows, matrix, matrix, matrix, rows, matrix),
        check_vma=False,
    )
```

```python
import functools

import jax
import jax.numpy as jnp
from jax import lax
from jax.experimental import pallas as pl
from jax.experimental.layout import Layout, with_layout_constraint
from jax.experimental.pallas import tpu as pltpu
from jax.sharding import Mesh
from jax.sharding import PartitionSpec as P

HD = 64
GAIN_LANES = 128
LANES = 128

norm_eps = 1e-06
masked_score = -1000000000.0
dp = ("group", "part")


def contract(first_op, second_op, first_dim, second_dim):
    return lax.dot_general(
        first_op,
        second_op,
        (((first_dim,), (second_dim,)), ((), ())),
        preferred_element_type=jnp.float32,
    )


def rows_first(array):
    return with_layout_constraint(array, Layout(major_to_minor=tuple(range(array.ndim))))


def norm_columns(inputs, scaling):
    return (
        inputs
        * lax.rsqrt(jnp.mean(inputs * inputs, axis=0, keepdims=True) + norm_eps)
        * scaling[:, None]
    )


def norm_back(inputs, scaling, upstream):
    unused, pullback = jax.vjp(norm_columns, inputs, scaling)
    return pullback(upstream)


def gated_unit(gate_in, upward):
    return jax.nn.gelu(gate_in, approximate=True) * upward


def swap(pieces, axis):
    return lax.all_to_all(pieces, axis, 0, 0, tiled=True)


def relocate(block):
    size = lax.axis_size("seq")
    pairs = [
        ((group * size + part) * size + at, (group * size + at) * size + part)
        for group in range(lax.axis_size("group"))
        for part in range(size)
        for at in range(size)
    ]
    return lax.ppermute(block, ("group", "part", "seq"), pairs)


def move_kernel(*refs, moves, count):
    for source, taken, target, put in moves:
        refs[count + target][put] = refs[source][taken]


def move(arrays, shapes, moves):
    return pl.pallas_call(
        functools.partial(move_kernel, moves=moves, count=len(arrays)),
        out_shape=[jax.ShapeDtypeStruct(shape, jnp.bfloat16) for shape in shapes],
    )(*arrays)


def sum_kernel(terms_ref, *refs, pieces):
    for ref, low, high in zip(refs, pieces[:-1], pieces[1:]):
        total = terms_ref[0, :, low:high].astype(jnp.float32)
        for block in range(1, terms_ref.shape[0]):
            total += terms_ref[block, :, low:high].astype(jnp.float32)
        ref[...] = total


def edges(sizes):
    return [sum(sizes[:at]) for at in range(len(sizes) + 1)]


every = slice(None)


def gather_kernel(full_ref, *refs, pieces):
    for ref, (start, size, copies) in zip(refs, pieces):
        for block in range(copies):
            ref[:, block * size : (block + 1) * size] = full_ref[block, :, start : start + size]


def matrices(full, lanes, pieces):
    n_seq, rows, unused = full.shape
    return pl.pallas_call(
        functools.partial(gather_kernel, pieces=pieces),
        grid=(rows // LANES,),
        in_specs=[pl.BlockSpec((n_seq, LANES, lanes), lambda step: (0, step, 0))],
        out_specs=[
            pl.BlockSpec((LANES, size * copies), lambda step: (step, 0))
            for start, size, copies in pieces
        ],
        out_shape=[
            jax.ShapeDtypeStruct((rows, size * copies), jnp.bfloat16)
            for start, size, copies in pieces
        ],
    )(full)


def deliver(terms, sizes, extra, out_sizes):
    n_seq = lax.axis_size("seq")
    rows = terms.shape[0]
    starts = edges(sizes)
    moves = [
        (
            0,
            (every, slice(low, low + sizes[at])),
            0,
            (block, every, slice(starts[at], starts[at + 1])),
        )
        for at in range(len(sizes))
        for block in range(n_seq)
        for low in [n_seq * starts[at] + block * sizes[at]]
    ]
    width = starts[-1]
    if extra:
        low = n_seq * width
        moves += [
            (0, (every, slice(low, low + extra)), 0, (block, every, slice(width, width + extra)))
            for block in range(n_seq)
        ]
    (parts,) = move([terms], [(n_seq, rows, width + extra)], moves)
    return pl.pallas_call(
        functools.partial(sum_kernel, pieces=edges(out_sizes)),
        out_shape=[jax.ShapeDtypeStruct((rows, size), jnp.float32) for size in out_sizes],
    )(swap(parts, "seq"))


def cut(array, sizes):
    return jnp.split(array, edges(sizes)[1:-1], axis=1)


def head_rows(row, head):
    return slice(row + head * HD, row + (head + 1) * HD)


def score_columns(key_ref, key_row, queries, head, allowed):
    scores = jnp.concatenate(
        [
            contract(key_ref[block, head_rows(key_row, head), :], queries, 0, 0)
            for block in range(key_ref.shape[0])
        ],
        axis=0,
    )
    if allowed is not None:
        scores = jnp.where(allowed, scores, masked_score)
    exponent = jnp.exp(scores - jnp.max(scores, axis=0, keepdims=True))
    return exponent * (1.0 / jnp.sum(exponent, axis=0, keepdims=True))


def allowed_columns(prefix_ref, step, blocks, rows):
    key_pos = lax.broadcasted_iota(jnp.int32, (blocks * rows, rows), 0)
    query_pos = step * rows + lax.broadcasted_iota(jnp.int32, (blocks * rows, rows), 1)
    return (key_pos <= query_pos) | (key_pos < prefix_ref[0])


def attend_kernel(prefix_ref, *refs, places, causal):
    out_ref = refs[-1]
    step = pl.program_id(0)
    (q_at, q_row), (k_at, k_row), (v_at, v_row) = places
    blocks, unused, rows = refs[k_at].shape
    allowed = allowed_columns(prefix_ref, step, blocks, rows) if causal else None
    for head in range(out_ref.shape[1] // HD):
        queries = refs[q_at][step, head_rows(q_row, head), :]
        queries = queries * jnp.asarray(HD**-0.5, queries.dtype)
        shares = score_columns(refs[k_at], k_row, queries, head, allowed).astype(queries.dtype)
        total = jnp.zeros(queries.shape, jnp.float32)
        for block in range(blocks):
            values = refs[v_at][block, head_rows(v_row, head), :]
            total += contract(values, shares[block * rows : (block + 1) * rows], 1, 0)
        out_ref[0, head_rows(0, head), :] = total.astype(out_ref.dtype)


def attend_back_kernel(prefix_ref, *refs, places, spots, count, causal):
    upstream_ref = refs[count]
    out_ref, key_sum, value_sum = refs[count + 1 :]
    step = pl.program_id(0)
    (q_at, q_row), (k_at, k_row), (v_at, v_row) = places
    blocks, unused, rows = refs[k_at].shape
    allowed = allowed_columns(prefix_ref, step, blocks, rows) if causal else None

    @pl.when(step == 0)
    def _():
        key_sum[...] = jnp.zeros_like(key_sum)
        value_sum[...] = jnp.zeros_like(value_sum)

    for head in range(upstream_ref.shape[1] // HD):
        mine = head_rows(0, head)
        queries = refs[q_at][step, head_rows(q_row, head), :]
        queries = queries * jnp.asarray(HD**-0.5, queries.dtype)
        upstream = upstream_ref[0, mine, :]
        shares = score_columns(refs[k_at], k_row, queries, head, allowed)
        share_grads = jnp.concatenate(
            [
                contract(refs[v_at][block, head_rows(v_row, head), :], upstream, 0, 0)
                for block in range(blocks)
            ],
            axis=0,
        )
        centre = jnp.sum(shares * share_grads, axis=0, keepdims=True)
        score_grads = (shares * (share_grads - centre)).astype(queries.dtype)
        shares = shares.astype(queries.dtype)
        total = jnp.zeros(queries.shape, jnp.float32)
        for block in range(blocks):
            part = slice(block * rows, (block + 1) * rows)
            key_rows = refs[k_at][block, head_rows(k_row, head), :]
            total += contract(key_rows, score_grads[part], 1, 0)
            key_sum[block, mine, :] += contract(queries, score_grads[part], 1, 1)
            value_sum[block, mine, :] += contract(upstream, shares[part], 1, 1)
        out_ref[step, head_rows(spots[0], head), :] = (total * HD**-0.5).astype(out_ref.dtype)

    @pl.when(step == pl.num_programs(0) - 1)
    def _():
        width = key_sum.shape[1]
        out_ref[:, spots[1] : spots[1] + width, :] = key_sum[...].astype(out_ref.dtype)
        out_ref[:, spots[2] : spots[2] + width, :] = value_sum[...].astype(out_ref.dtype)


def exit_kernel(
    count_ref,
    token_ref,
    target_ref,
    table_ref,
    shifted_ref,
    product_ref,
    part_ref,
    logit_ref,
    *,
    rows,
):
    lanes = table_ref.shape[1]
    chunk = next(size for size in (1024, 512, 256, 128) if lanes % size == 0)
    step_rows = token_ref.shape[0]
    flagged = count_ref[pl.program_id(0)]

    def part_rows(first, last):
        here = slice(first, last)
        tokens = token_ref[here]
        row_max = jnp.full((last - first, 1), -jnp.inf, jnp.float32)
        for low in range(0, lanes, chunk):
            logits = contract(tokens, table_ref[:, low : low + chunk], 1, 0)
            if low + chunk > rows:
                lane = low + lax.broadcasted_iota(jnp.int32, (1, chunk), 1)
                logits = jnp.where(lane < rows, logits, -jnp.inf)
            logit_ref[here, low : low + chunk] = logits
            row_max = jnp.maximum(row_max, jnp.max(logits, axis=1, keepdims=True))
        row_sum = jnp.zeros_like(row_max)
        product = jnp.zeros((last - first, product_ref.shape[1]), jnp.float32)
        for low in range(0, lanes, chunk):
            shifted = jnp.exp(logit_ref[here, low : low + chunk] - row_max)
            row_sum += jnp.sum(shifted, axis=1, keepdims=True)
            shifted = shifted.astype(shifted_ref.dtype)
            shifted_ref[here, low : low + chunk] = shifted
            product += contract(shifted, table_ref[:, low : low + chunk], 1, 1)
        product_ref[here] = product
        picked = tokens.astype(jnp.float32) * target_ref[here].astype(jnp.float32)
        picked = jnp.sum(picked, axis=1, keepdims=True)
        lane = lax.broadcasted_iota(jnp.int32, (last - first, part_ref.shape[1]), 1)
        part_ref[here] = jnp.where(lane == 0, row_max, jnp.where(lane == 1, row_sum, picked))

    split = step_rows * 9 // 16
    part_rows(0, split)

    @pl.when(flagged > split)
    def _():
        part_rows(split, step_rows)

    @pl.when(flagged <= split)
    def _():
        here = slice(split, step_rows)
        shifted_ref[here] = jnp.zeros((step_rows - split, lanes), shifted_ref.dtype)
        product_ref[here] = jnp.zeros((step_rows - split, product_ref.shape[1]), jnp.float32)
        lane = lax.broadcasted_iota(jnp.int32, (step_rows - split, part_ref.shape[1]), 1)
        part_ref[here] = jnp.where(lane == 1, 1.0, 0.0)


def exit_rows(counts, tokens, targets, table, rows):
    count, width = tokens.shape
    lanes = table.shape[1]
    step_rows = count // counts.shape[0]
    block = pl.BlockSpec((step_rows, width), lambda step: (step, 0))
    return pl.pallas_call(
        functools.partial(exit_kernel, rows=rows),
        grid=(count // step_rows,),
        in_specs=[pl.BlockSpec(memory_space=pltpu.SMEM), block, block, whole(table)],
        out_specs=[
            pl.BlockSpec((step_rows, lanes), lambda step: (step, 0)),
            pl.BlockSpec((step_rows, width), lambda step: (step, 0)),
            pl.BlockSpec((step_rows, LANES), lambda step: (step, 0)),
        ],
        out_shape=[
            jax.ShapeDtypeStruct((count, lanes), jnp.bfloat16),
            jax.ShapeDtypeStruct((count, width), jnp.float32),
            jax.ShapeDtypeStruct((count, LANES), jnp.float32),
        ],
        scratch_shapes=[pltpu.VMEM((step_rows, lanes), jnp.float32)],
    )(counts, tokens, targets, table)


def whole(array):
    return pl.BlockSpec(array.shape, lambda step: (0,) * len(array.shape))


def attend(prefix, arrays, places, width, causal):
    blocks, unused, rows = arrays[0].shape
    return pl.pallas_call(
        functools.partial(attend_kernel, places=places, causal=causal),
        grid=(blocks,),
        in_specs=[pl.BlockSpec(memory_space=pltpu.SMEM)] + [whole(array) for array in arrays],
        out_specs=pl.BlockSpec((1, width, rows), lambda step: (step, 0, 0)),
        out_shape=jax.ShapeDtypeStruct((blocks, width, rows), jnp.bfloat16),
    )(prefix, *arrays)


def attend_back(prefix, arrays, upstream, places, causal):
    blocks, width, rows = upstream.shape
    shape = jax.ShapeDtypeStruct((blocks, 3 * width, rows), jnp.bfloat16)
    return pl.pallas_call(
        functools.partial(
            attend_back_kernel,
            places=places,
            spots=(0, width, 2 * width),
            count=len(arrays),
            causal=causal,
        ),
        grid=(blocks,),
        in_specs=[pl.BlockSpec(memory_space=pltpu.SMEM)]
        + [whole(array) for array in arrays]
        + [pl.BlockSpec((1, width, rows), lambda step: (step, 0, 0))],
        out_specs=whole(shape),
        out_shape=shape,
        scratch_shapes=[pltpu.VMEM((blocks, width, rows), jnp.float32)] * 2,
    )(prefix, *arrays, upstream)


def per_device(
    hidden_in,
    encoder_in,
    prefix_len,
    exit_flags,
    target_ids,
    out_cotangent,
    self_gain,
    self_query,
    self_key,
    self_value,
    self_output,
    cross_gain,
    cross_query,
    cross_key,
    cross_value,
    cross_output,
    feed_gain,
    feed_gate,
    feed_up,
    feed_down,
    exit_gain,
    embedding,
):
    width = hidden_in.shape[2]
    n_seq = lax.axis_size("seq")
    n_dp = lax.axis_size(dp)
    own_rows, own = self_query.shape
    own_feed = feed_gate.shape[1]
    fold_rows = feed_down.shape[0]
    folds = -(-fold_rows // own_rows)
    vocab_rows = embedding.shape[0]
    vocab_lanes = -(-vocab_rows // LANES) * LANES
    low = jnp.bfloat16

    gains = jnp.stack([self_gain, cross_gain, feed_gain, exit_gain], axis=1)
    early = -(-(5 * own + 4) // LANES) * LANES
    gains = jnp.pad(gains, ((0, 0), (0, early - 5 * own - 4)))
    folded = jnp.pad(feed_down, ((0, folds * own_rows - fold_rows), (0, 0)))
    shards = [
        self_query,
        self_key,
        self_value,
        cross_key,
        cross_value,
        gains,
        self_output,
        cross_query,
        cross_output,
        feed_gate,
        feed_up,
    ] + [folded[fold * own_rows : (fold + 1) * own_rows] for fold in range(folds)]
    starts = edges([shard.shape[1] for shard in shards])
    (flat,) = move(
        shards,
        [(own_rows, starts[-1])],
        [
            (at, (every, every), 0, (every, slice(starts[at], starts[at + 1])))
            for at in range(len(shards))
        ],
    )
    full = lax.all_gather(flat, ("seq",) + dp, axis=0, tiled=True).reshape(n_seq, width, -1)
    self_qkv, cross_kv, gain_columns = matrices(
        full,
        early,
        ((0, 3 * own, n_seq), (3 * own, 2 * own, n_seq), (5 * own, early - 5 * own, 1)),
    )
    rest_sizes = (own, 2 * own, own, own, own_feed, own_feed) + (own,) * folds

    marks = jnp.concatenate(
        [exit_flags, target_ids, jnp.broadcast_to(prefix_len[:, None], exit_flags.shape)], axis=0
    )
    hidden = relocate(hidden_in.reshape(-1, width))
    states = relocate(encoder_in.reshape(-1, width))
    marks = relocate(marks)
    prefix_len = marks[2, :1]
    place = jnp.arange(marks.shape[1])
    key = (1 - marks[0]) * marks.shape[1] + place
    rank = jnp.sum((key[None, :] < key[:, None]).astype(jnp.int32), axis=1)
    order = place[:, None] == rank[None, :]
    marks = jnp.sum(jnp.where(order[None], marks[:2, None, :], 0), axis=2)
    marks = lax.all_gather(marks, dp, axis=0)
    order_low = order.astype(low)
    shard = jnp.pad(embedding.T, ((0, 0), (0, vocab_lanes - vocab_rows)))
    shard, marks, hidden, states = lax.optimization_barrier((shard, marks, hidden, states))
    table = lax.all_gather(shard, "seq", axis=0, tiled=True)
    gain_one, gain_two, gain_three, gain_exit = gain_columns[:, :4].astype(jnp.float32).T

    def blocks(rows):
        return rows.astype(low).reshape(n_seq, -1, rows.shape[1])

    def fold_up(rows):
        rows = rows.reshape(n_dp, fold_rows, -1)
        rows = jnp.pad(rows, ((0, 0), (0, folds * own_rows - fold_rows), (0, 0)))
        return [
            rows[:, fold * own_rows : (fold + 1) * own_rows].reshape(width, -1)
            for fold in range(folds)
        ]

    def unfold(parts):
        parts = [part.reshape(n_dp, own_rows, -1) for part in parts]
        rows = jnp.concatenate(parts, axis=1)[:, :fold_rows]
        return rows.reshape(n_dp * fold_rows, -1)

    residual_in = hidden.T.astype(jnp.float32)
    token_count = residual_in.shape[1]
    residual_in, states = lax.optimization_barrier((residual_in, states.T))
    residual_in, states = rows_first(residual_in), rows_first(states)
    normed_one = norm_columns(residual_in, gain_one).astype(low)
    attended = jnp.concatenate(
        [blocks(contract(self_qkv, normed_one, 0, 0)), blocks(contract(cross_kv, states, 0, 0))],
        axis=1,
    )
    attended, full = lax.optimization_barrier((attended, full))
    attended = swap(attended, "part")
    self_out, cross_q, cross_out, gate_full, up_full, *downs = matrices(
        full,
        starts[-1],
        tuple(
            (starts[at], starts[at + 1] - starts[at], n_seq) for at in range(6, len(shards))
        ),
    )
    attended, self_out = lax.optimization_barrier((attended, self_out))
    self_places = ((0, 0), (0, own), (0, 2 * own))
    mixture_one = swap(attend(prefix_len, [attended], self_places, own, True), "part")
    mixture_one = mixture_one.reshape(width, token_count)
    after_self = residual_in + contract(self_out, mixture_one, 0, 0)
    normed_two = norm_columns(after_self, gain_two).astype(low)
    q_two = swap(blocks(contract(cross_q, normed_two, 0, 0)), "part")
    cross_places = ((0, 0), (1, 3 * own), (1, 4 * own))
    mixture_two = swap(attend(prefix_len, [q_two, attended], cross_places, own, False), "part")
    mixture_two = mixture_two.reshape(width, token_count)
    after_cross = after_self + contract(cross_out, mixture_two, 0, 0)
    normed_three = norm_columns(after_cross, gain_three).astype(low)
    gate_pre = contract(gate_full, normed_three, 0, 0)
    up_pre = contract(up_full, normed_three, 0, 0)
    hidden_mid = gated_unit(gate_pre, up_pre).astype(low)
    hidden_folds = fold_up(hidden_mid)
    after_feed = after_cross
    for down, hidden in zip(downs, hidden_folds):
        after_feed = after_feed + contract(down, hidden, 0, 0)
    block_output = after_feed.T.astype(low)
    normed_exit = contract(order_low, norm_columns(after_feed, gain_exit).astype(low), 1, 1)
    normed_exit = rows_first(normed_exit.astype(low))
    normed_exit, table, cotangent, block_output = lax.optimization_barrier(
        (normed_exit, table, out_cotangent, block_output)
    )

    tokens = lax.all_gather(normed_exit, dp, axis=0, tiled=True)
    flag_rows = marks[:, 0].reshape(-1, 1).astype(jnp.float32)
    target_rows = marks[:, 1].reshape(-1, 1) - lax.axis_index(dp) * vocab_rows
    hits = jnp.arange(vocab_lanes)[None, :] == target_rows
    hits = hits & (target_rows < vocab_rows)
    target_terms = contract(hits.astype(low), table, 1, 1).astype(low)
    tokens, target_terms = lax.optimization_barrier((tokens, target_terms))
    cotangent = relocate(cotangent.reshape(-1, width).astype(low))
    block_output = relocate(block_output)
    tokens, cotangent, block_output = lax.optimization_barrier((tokens, cotangent, block_output))
    counts = jnp.sum(marks[:, 0], axis=1)
    shifted, products, parts = exit_rows(counts, tokens, target_terms, table, vocab_rows)
    block_output = block_output.reshape(hidden_in.shape)
    row_max = parts[:, 0]
    parts = lax.all_gather(parts[:, :3].T, dp, axis=0)
    top = jnp.max(parts[:, 0], axis=0)
    log_total = top + jnp.log(jnp.sum(parts[:, 1] * jnp.exp(parts[:, 0] - top), axis=0))
    all_losses = flag_rows[:, 0] * (log_total - jnp.sum(parts[:, 2], axis=0))
    token_losses = lax.dynamic_slice(
        all_losses, (lax.axis_index(dp) * token_count,), (token_count,)
    )
    token_losses = jnp.sum(jnp.where(order, token_losses[:, None], 0.0), axis=0)
    token_losses = relocate(token_losses.reshape(exit_flags.shape))
    factor = flag_rows * jnp.exp(row_max - log_total)[:, None]
    exit_in_grad = lax.psum_scatter(
        rows_first((factor * products - flag_rows * target_terms.astype(jnp.float32)).astype(low)),
        dp,
        scatter_dimension=0,
        tiled=True,
    )
    logit_grads = jnp.where(hits, factor * shifted - flag_rows, factor * shifted).astype(low)
    table_terms = contract(tokens, logit_grads, 0, 0).astype(low)
    exit_in_grad, table_terms, token_losses = lax.optimization_barrier(
        (rows_first(exit_in_grad), table_terms, token_losses)
    )
    cotangent = rows_first(cotangent.T)
    exit_in_grad = rows_first(contract(exit_in_grad, order_low, 0, 0))
    table_sums = lax.psum_scatter(table_terms, "seq", scatter_dimension=0, tiled=True)

    feed_grad, full_exit_gain = norm_back(after_feed, gain_exit, exit_in_grad)
    feed_grad = feed_grad + cotangent
    branch_three = feed_grad.astype(low)
    hidden_mid_grad = unfold([contract(down, branch_three, 1, 0) for down in downs])
    unused, gated_pull = jax.vjp(gated_unit, gate_pre, up_pre)
    gate_grad, up_grad = gated_pull(hidden_mid_grad)
    gate_grad, up_grad = gate_grad.astype(low), up_grad.astype(low)
    normed_three_grad = contract(gate_full, gate_grad, 1, 0) + contract(up_full, up_grad, 1, 0)
    cross_grad, full_feed_gain = norm_back(after_cross, gain_three, normed_three_grad)
    cross_grad = cross_grad + feed_grad
    branch_two = cross_grad.astype(low)
    mixture_two_grad = blocks(contract(cross_out, branch_two, 1, 0))
    cross_grads = attend_back(
        prefix_len, [q_two, attended], swap(mixture_two_grad, "part"), cross_places, False
    )
    cross_grads = swap(cross_grads, "part")
    q_grad = cross_grads[:, :own].reshape(-1, token_count)
    kv_grad = cross_grads[:, own:].reshape(-1, token_count)
    encoder_grad = relocate(contract(kv_grad, cross_kv, 0, 1).astype(low)).astype(jnp.float32)
    self_grad, full_cross_gain = norm_back(after_self, gain_two, contract(cross_q, q_grad, 1, 0))
    self_grad = self_grad + cross_grad
    branch_one = self_grad.astype(low)
    rest_terms = jnp.concatenate(
        [
            contract(normed_two, q_grad, 1, 1).astype(low),
            contract(states, kv_grad, 1, 1).astype(low),
            contract(mixture_two, branch_two, 1, 1).astype(low),
            contract(mixture_one, branch_one, 1, 1).astype(low),
            contract(normed_three, gate_grad, 1, 1).astype(low),
            contract(normed_three, up_grad, 1, 1).astype(low),
        ]
        + [contract(hidden, branch_three, 1, 1).astype(low) for hidden in hidden_folds],
        axis=1,
    )
    mixture_one_grad = blocks(contract(self_out, branch_one, 1, 0))
    mixture_one_grad, rest_terms = lax.optimization_barrier((mixture_one_grad, rest_terms))
    rest_terms, table_sums = lax.optimization_barrier((rest_terms, table_sums))
    rest_terms = lax.psum_scatter(rest_terms, dp, scatter_dimension=0, tiled=True)
    qkv_grad = attend_back(
        prefix_len, [attended], swap(mixture_one_grad, "part"), self_places, True
    )
    qkv_grad, encoder_grad = lax.optimization_barrier((qkv_grad, encoder_grad))
    qkv_grad = swap(qkv_grad, "part").reshape(-1, token_count)
    normed_one_grad = contract(self_qkv, qkv_grad, 1, 0)
    input_grad, full_self_gain = norm_back(residual_in, gain_one, normed_one_grad)
    hidden_grad = relocate((input_grad + self_grad).T.astype(low)).astype(jnp.float32)
    gain_terms = jnp.stack(
        [full_self_gain, full_cross_gain, full_feed_gain, full_exit_gain], axis=1
    ).astype(low)
    gain_terms = jnp.pad(gain_terms, ((0, 0), (0, GAIN_LANES - gain_terms.shape[1])))
    self_terms = jnp.concatenate(
        [
            contract(normed_one, qkv_grad, 1, 1).astype(low),
            gain_terms,
        ],
        axis=1,
    )
    self_terms, rest_terms, hidden_grad = lax.optimization_barrier(
        (self_terms, rest_terms, hidden_grad)
    )
    self_terms = lax.psum_scatter(self_terms, dp, scatter_dimension=0, tiled=True)
    embedding_grad = table_sums[:, :vocab_rows].astype(jnp.float32).T
    (
        cross_query_grad,
        cross_key_grad,
        cross_value_grad,
        cross_output_grad,
        self_output_grad,
        feed_gate_grad,
        feed_up_grad,
        *down_sums,
    ) = deliver(rest_terms, rest_sizes, 0, (own,) * 5 + rest_sizes[4:])
    down_grad = jnp.concatenate(down_sums, axis=0)[:fold_rows]
    self_query_grad, self_key_grad, self_value_grad, gain_sums = deliver(
        self_terms, (3 * own,), GAIN_LANES, (own,) * 3 + (GAIN_LANES,)
    )
    gain_sums = gain_sums[:, :4].T
    return (
        block_output,
        token_losses,
        hidden_grad.reshape(hidden_in.shape),
        encoder_grad.reshape(encoder_in.shape),
        gain_sums[0],
        self_query_grad,
        self_key_grad,
        self_value_grad,
        self_output_grad,
        gain_sums[1],
        cross_query_grad,
        cross_key_grad,
        cross_value_grad,
        cross_output_grad,
        gain_sums[2],
        feed_gate_grad,
        feed_up_grad,
        down_grad,
        gain_sums[3],
        embedding_grad,
    )


def solution(mesh):
    size = mesh.shape["seq"]
    planes = Mesh(mesh.devices.reshape(-1, size, size), dp + ("seq",))
    tokens = P(dp, "seq")
    rows = P(dp)
    matrix = P(dp, "seq")
    block = P(dp, "seq", None)
    attention = (rows,) + (matrix,) * 4
    return jax.shard_map(
        per_device,
        mesh=planes,
        in_specs=(block, block, rows, tokens, tokens, block)
        + attention * 2
        + (rows, matrix, matrix, matrix, rows, matrix),
        out_specs=(block, tokens, block, block)
        + attention * 2
        + (rows, matrix, matrix, matrix, rows, matrix),
        check_vma=False,
    )
```
